256 devices in a mesh: facet: 16 (over x, y), chan: 16 (over z, core).
Axes of the slice: x: 4, y: 4, z: 8, core: 2. Of those that a mesh axis runs over, the one named last changes fastest.
Arguments:
- visibility: float32 [4096, 2, 512], P(('facet', 'chan')), may hold values from -6 to 6
- uv_coords: float32 [4096, 2, 512], P(('facet', 'chan')), may hold values from 0 to 63
- vis_count: int32 [4096], P(('facet', 'chan')), may hold values from 256 to 512, as said below
- subgrid_facet: int32 [4096, 1], P(('facet', 'chan')), may hold values from 0 to 15; in each aligned block of 16 rows (0 to 15, 16 to 31, ...) at most 2 rows name the same one
- row_offset: int32 [4096], P(('facet', 'chan')), may hold values from 0 to 64
- col_offset: int32 [4096], P(('facet', 'chan')), may hold values from 0 to 4032
- model_facet: bfloat16 [16, 128, 2, 4096], P('facet'), may hold values from -6 to 6
Outputs:
- facet_image: float32 [16, 128, 2, 4096], P('facet', 'chan')
- residual_vis: float32 [4096, 2, 512], P(('facet', 'chan'))
The draws below stay inside these ranges and needn't reach their ends.
Inputs may be any that keep to these rules, and one draw needn't show every extreme that they name: `subgrid_facet`: in every device's block of 16 subgrids at most 2 name the same facet, a bound that some block reaches. `vis_count`: in every device's block of 16 subgrids one subgrid has all 512 visibilities live.
All inputs are finite; a program needn't handle non-finite values.
Results may differ from the reference program's by a relative error of at most 0.012.
Values may be sent and summed in bfloat16 or wider, within the bound.
A program may use at most 64 MiB of HBM per device.

```python
import math
import jax
import jax.numpy as jnp
import numpy as np
from jax import lax

SUB = 64
FACET = 4096
F_ROWS = 128
NV = 512
S_DEV = 16
CAP = 2
FACETS = 16
S_TOTAL = 4096


def draw_vis_count(key, part):
    block_count = S_TOTAL // S_DEV
    first_key, second_key = jax.random.split(jax.random.fold_in(key, 7))
    base_counts = jax.random.randint(first_key, (block_count, S_DEV), NV // 2, NV + 1)
    peak_index = jax.random.randint(second_key, (block_count, 1), 0, S_DEV)
    filled = jnp.where(jnp.arange(S_DEV)[None, :] == peak_index, NV, base_counts)
    return filled.reshape(S_TOTAL).astype(jnp.int32)


def plant(entries, rng, low, largest):
    dims = entries.shape
    spot = [jax.random.randint(jax.random.fold_in(rng, axis), (), 0, dims[axis]) for axis in range(len(dims))]
    entries = entries.at[tuple(spot)].set(low)
    longest = dims.index(max(dims))
    spot[longest] = (spot[longest] + 1) % dims[longest]
    return entries.at[tuple(spot)].set(largest)


def block_scale(own_key, dims, shards, smallest, largest):
    def one(dim, shards_of):
        draws = jax.random.uniform(jax.random.fold_in(jax.random.fold_in(own_key, 6), dim), (shards_of,), jnp.float32, smallest / len(shards), largest / len(shards))
        return jnp.repeat(jnp.exp(draws), dims[dim] // shards_of).reshape((-1,) + (1,) * (len(dims) - dim - 1))

    loudness = one(*shards[0])
    for cut in shards[1:]:
        loudness = loudness * one(*cut)
    return loudness


def routed_block(key, own, number, rows, count, top, reach, skew):
    sequence = jax.random.permutation(key, count)
    heavy_load, common = load_shares(count, rows * top, reach, skew, True), load_shares(count, rows * top, reach, skew, False)
    places = jnp.arange(count)

    def named(lengths, rotation):
        used = int((lengths > 0).sum())
        fixed = max(1, used // 4)
        moved = fixed + (places - fixed + rotation * (used - fixed)) % max(1, count - fixed)
        return jnp.zeros((count,), jnp.int32).at[sequence[jnp.where(places < fixed, places, moved)]].set(jnp.asarray(lengths, jnp.int32))

    lengths = jnp.where(number % 4 == 0, named(heavy_load, number // 4), named(common, number - number // 4 - 1))
    mixed = jax.random.permutation(jax.random.fold_in(own, 3), count)
    giver, sink = mixed[0:count // 2 * 2:2], mixed[1:count // 2 * 2:2]
    room = jnp.minimum(lengths[giver] - 1, reach - lengths[sink]) // 2
    room = jnp.where((giver == sequence[0]) | (sink == sequence[0]) | (lengths[sink] == 0), 0, jnp.maximum(room, 0))
    moved = jax.random.randint(jax.random.fold_in(own, 4), (count // 2,), 0, 1 << 20) % (room + 1)
    lengths = lengths.at[giver].add(-moved).at[sink].add(moved)
    members = jnp.searchsorted(jnp.cumsum(lengths), jnp.arange(rows * top), side="right").astype(jnp.int32)
    listing = members.reshape(top, rows).T
    listing = listing[jax.random.permutation(jax.random.fold_in(own, 1), rows)]
    rotation = jax.random.randint(jax.random.fold_in(own, 2), (rows, 1), 0, top)
    return jnp.take_along_axis(listing, (jnp.arange(top)[None, :] + rotation) % top, axis=1)


def load_shares(count, total, limit, slope, full):
    portions = [(1 << 20) // math.isqrt(rank ** slope) + 1 for rank in range(1, count + 1)]
    largest = limit if full else min(limit, max(-(-total // count), total * portions[0] // sum(portions)))
    least = 1 if total - largest >= count - 1 else 0
    given, rest = [largest] + [least] * (count - 1), total - largest - least * (count - 1)
    while rest > 0:
        free = [i for i in range(1, count) if given[i] < largest] or [i for i in range(1, count) if given[i] < limit]
        whole, remaining = sum([portions[i] for i in free]), rest
        for i in free:
            addition = min(limit - given[i], max(1, remaining * portions[i] // whole), rest)
            given[i] = given[i] + addition
            rest = rest - addition
    return np.array(given)


def normal_values(key, extent, scale, limit, cuts=(), kind=jnp.bfloat16):
    array = jax.random.normal(key, extent, jnp.float32) * scale
    if len(cuts) > 0:
        array = block_scale(key, extent, cuts, -0.22, 0.18) * array
    return jnp.clip(array, min=-limit, max=limit).astype(kind)


def setup_inputs(seed: int = 0) -> dict:
    key_of = jax.random.split(jax.random.key(seed), 8)
    visibility = normal_values(key_of[0], (S_TOTAL, 2, NV), 1.0, 6.0, ((0, 256),), jnp.float32)
    uv_coords = jnp.clip(63.0 * jax.random.uniform(key_of[1], (S_TOTAL, 2, NV), jnp.float32) ** block_scale(key_of[1], (S_TOTAL, 2, NV), ((0, 256),), -0.2, 0.2), 0.0, 63.0)
    vis_count = draw_vis_count(jax.random.fold_in(key_of[7], 71), 0)
    subgrid_facet_keys = jax.random.split(jax.random.fold_in(key_of[3], 1), S_TOTAL // S_DEV)
    subgrid_facet_turns = jax.random.permutation(jax.random.fold_in(key_of[3], 3), S_TOTAL // S_DEV)
    subgrid_facet = jax.vmap(lambda own, number: routed_block(jax.random.fold_in(key_of[3], 2), own, number, S_DEV, FACETS, 1, CAP, 2))(subgrid_facet_keys, subgrid_facet_turns).reshape((S_TOTAL, 1))
    row_offset = plant(jax.random.randint(key_of[4], (S_TOTAL,), 0, F_ROWS - SUB + 1), jax.random.fold_in(key_of[4], 1), 0, F_ROWS - SUB).astype(jnp.int32)
    col_offset = plant(jax.random.randint(key_of[5], (S_TOTAL,), 0, FACET - SUB + 1), jax.random.fold_in(key_of[5], 1), 0, FACET - SUB).astype(jnp.int32)
    model_facet = normal_values(key_of[6], (FACETS, F_ROWS, 2, FACET), 1.0, 6.0, ((0, 16),))
    return dict(visibility=visibility, uv_coords=uv_coords, vis_count=vis_count, subgrid_facet=subgrid_facet, row_offset=row_offset, col_offset=col_offset, model_facet=model_facet)


KERNEL_COEF = 1.0

def dft_tables(length):
    index_line = jnp.arange(length, dtype=jnp.int32)
    phase = index_line[:, None] * index_line[None, :] % length
    angle = 2.0 * math.pi * phase.astype(jnp.float32) / length
    cos_table = (jnp.cos(angle) / math.sqrt(length)).astype(jnp.bfloat16)
    sin_table = (-jnp.sin(angle) / math.sqrt(length)).astype(jnp.bfloat16)
    right_forward = jnp.concatenate([jnp.concatenate([cos_table, sin_table], 1), jnp.concatenate([-sin_table, cos_table], 1)], 0)
    right_inverse = jnp.concatenate([jnp.concatenate([cos_table, -sin_table], 1), jnp.concatenate([sin_table, cos_table], 1)], 0)
    return (cos_table, sin_table, right_forward, right_inverse)

def swap_halves(values):
    half_width = values.shape[-1] // 2
    return jnp.concatenate([-values[..., half_width:], values[..., :half_width]], -1)

def left_product(table, values):
    return jnp.einsum('ja,sam->sjm', table.astype(jnp.float32), values.astype(jnp.float32))

def forward_transform(sub_grid, tables):
    cos_table, sin_table, right_forward, right_inverse = tables
    half = (left_product(cos_table, sub_grid) + left_product(sin_table, swap_halves(sub_grid))).astype(jnp.bfloat16)
    return jnp.einsum('sjb,bm->sjm', half.astype(jnp.float32), right_forward.astype(jnp.float32)).astype(jnp.bfloat16)

def inverse_transform(sub_grid, tables):
    cos_table, sin_table, right_forward, right_inverse = tables
    half = (left_product(cos_table, sub_grid) - left_product(sin_table, swap_halves(sub_grid))).astype(jnp.bfloat16)
    return jnp.einsum('sjb,bm->sjm', half.astype(jnp.float32), right_inverse.astype(jnp.float32)).astype(jnp.bfloat16)

def kernels(coords):
    pixel_grid = jnp.arange(SUB, dtype=jnp.int32).astype(jnp.float32)
    delta_u = pixel_grid[None, None, :] - coords[:, 0, :, None]
    delta_v = pixel_grid[None, None, :] - coords[:, 1, :, None]
    return (jnp.exp(-KERNEL_COEF * delta_u * delta_u), jnp.exp(-KERNEL_COEF * delta_v * delta_v))

def reference(visibility, uv_coords, vis_count, subgrid_facet, row_offset, col_offset, model_facet):
    tables = dft_tables(SUB)
    block_count = S_TOTAL // S_DEV

    def blocked(values):
        return values.reshape((block_count, S_DEV) + values.shape[1:])
    inputs = (blocked(visibility), blocked(uv_coords), blocked(vis_count), blocked(subgrid_facet[:, 0]), blocked(row_offset), blocked(col_offset))
    two_parts = jnp.arange(2, dtype=jnp.int32)
    pixel_line = jnp.arange(SUB, dtype=jnp.int32)

    def one_block(canvas, block):
        vis_block, coord_block, count_block, facet_ids, row_start, col_start = block
        kernel_u, kernel_v = kernels(coord_block)
        live_mask = (jnp.arange(NV, dtype=jnp.int32)[None, :] < count_block[:, None]).astype(jnp.float32)
        weighted = vis_block * live_mask[:, None, :]
        spread = (jnp.transpose(weighted, (0, 2, 1))[:, :, :, None] * kernel_v[:, :, None, :]).reshape(S_DEV, NV, 2 * SUB).astype(jnp.bfloat16)
        kernel_low = kernel_u.astype(jnp.bfloat16)
        gridded = jnp.einsum('ska,skm->sam', kernel_low.astype(jnp.float32), spread.astype(jnp.float32)).astype(jnp.bfloat16)
        patch = forward_transform(gridded, tables)
        row_index = (row_start[:, None] + pixel_line[None, :]).astype(jnp.int32)
        col_index = (col_start[:, None] + pixel_line[None, :]).astype(jnp.int32)
        where_facet = facet_ids[:, None, None, None]
        where_row = row_index[:, :, None, None]
        where_part = two_parts[None, None, :, None]
        where_col = col_index[:, None, None, :]
        values = patch.astype(jnp.float32).reshape(S_DEV, SUB, 2, SUB)
        canvas = canvas.at[where_facet, where_row, where_part, where_col].add(values)
        picked = model_facet[where_facet, where_row, where_part, where_col].reshape(S_DEV, SUB, 2 * SUB)
        image_grid = inverse_transform(picked, tables)
        degridded = jnp.einsum('ska,sam->skm', kernel_low.astype(jnp.float32), image_grid.astype(jnp.float32)).reshape(S_DEV, NV, 2, SUB)
        predicted = lax.optimization_barrier(jnp.sum(degridded * kernel_v[:, :, None, :], -1))
        residual = (vis_block - jnp.transpose(predicted, (0, 2, 1))) * live_mask[:, None, :]
        return (canvas, residual)
    start_canvas = jnp.zeros((FACETS, F_ROWS, 2, FACET), jnp.float32)
    canvas, residual = lax.scan(one_block, start_canvas, inputs)
    return (canvas, residual.reshape(S_TOTAL, 2, NV))
```

```python
import functools
import math

import jax
import jax.numpy as jnp
import numpy as np
from jax import lax
from jax.experimental import pallas as pl
from jax.experimental.pallas import tpu as pltpu
from jax.sharding import PartitionSpec as P

SUB = 64
FACET = 4096
F_ROWS = 128
NV = 512
LANES = 128
TILES = FACET // LANES
SLOTS = 2


def dft_tables():
    line = np.arange(SUB)
    angle = 2.0 * math.pi * (line[:, None] * line[None, :] % SUB) / SUB
    cos_table = (np.cos(angle) / math.sqrt(SUB)).astype(jnp.bfloat16)
    sin_table = (-np.sin(angle) / math.sqrt(SUB)).astype(jnp.bfloat16)
    left_forward = np.concatenate([cos_table, sin_table], 1)
    left_inverse = np.concatenate([cos_table, -sin_table], 1)
    right_forward = np.concatenate(
        [np.concatenate([cos_table, sin_table], 1), np.concatenate([-sin_table, cos_table], 1)], 0
    )
    right_inverse = np.concatenate(
        [np.concatenate([cos_table, -sin_table], 1), np.concatenate([sin_table, cos_table], 1)], 0
    )
    return left_forward, right_forward, left_inverse, right_inverse


def kernel_of(coords):
    pixels = lax.broadcasted_iota(jnp.int32, (SUB, NV), 0).astype(jnp.float32)
    delta = pixels - coords
    return jnp.exp(-(delta * delta))


def live_row(count):
    lane = lax.broadcasted_iota(jnp.int32, (1, NV), 1)
    return (lane < count).astype(jnp.float32)


def facet_peers(me, side):
    x, y = me // side, lax.rem(me, side)
    order = {0: 0, 2: 2}
    steps = [(dx, dy) for dx in range(side) for dy in range(side) if dx or dy]
    steps.sort(key=lambda step: -sum(min(d, side - d) for d in step))
    return [lax.rem(x + dx, side) * side + lax.rem(y + dy, side) for dx, dy in steps], [
        lax.rem(x + side - dx, side) * side + lax.rem(y + side - dy, side) for dx, dy in steps
    ]


def grid_kernel(
    facets, side, subgrids,
    cnt, fid, row, col, vis, uv,
    ku_out, kv_out, grid_in, meta_in,
    grids, grid_send, meta_send, first, last,
    send_sem, recv_sem, meta_send_sem, meta_recv_sem, own_sem,
):
    me = lax.axis_index("facet")
    targets, sources = facet_peers(me, side)
    barrier = pltpu.get_barrier_semaphore()
    for peer in targets:
        pl.semaphore_signal(barrier, inc=1, device_id={"facet": peer})

    ids = [fid[s] for s in range(subgrids)]

    def find(facet, carry):
        low = jnp.int32(subgrids)
        high = jnp.int32(-1)
        for s in range(subgrids):
            same = ids[s] == facet
            high = jnp.where(same, s, high)
            back = subgrids - 1 - s
            low = jnp.where(ids[back] == facet, back, low)
        first[facet] = low
        last[facet] = high
        return carry

    lax.fori_loop(0, facets, find, 0)

    def grid_one(s, carry):
        ku = kernel_of(uv[s, pl.ds(0, 1), :]).astype(jnp.bfloat16)
        kv = kernel_of(uv[s, pl.ds(1, 1), :])
        live = live_row(cnt[s])
        re = (vis[s, pl.ds(0, 1), :] * live) * kv
        im = (vis[s, pl.ds(1, 1), :] * live) * kv
        spread = jnp.concatenate([re.astype(jnp.bfloat16), im.astype(jnp.bfloat16)], 0)
        ku_out[s] = ku
        kv_out[s] = kv.astype(jnp.bfloat16)
        grids[s] = lax.dot_general(
            ku, spread, (((1,), (1,)), ((), ())), preferred_element_type=jnp.float32
        ).astype(jnp.bfloat16)
        return carry

    lax.fori_loop(0, subgrids, grid_one, 0, unroll=2)

    lane = lax.broadcasted_iota(jnp.int32, (1, LANES), 1)

    def pack(facet, carry):
        low, high = first[facet], last[facet]
        one = jnp.minimum(low, subgrids - 1)
        two = jnp.maximum(high, 0)
        grid_send[facet, 0] = grids[one]
        grid_send[facet, 1] = grids[two]
        values = (
            (high >= 0).astype(jnp.int32), row[one], col[one],
            (high > low).astype(jnp.int32), row[two], col[two],
        )
        line = jnp.zeros((1, LANES), jnp.int32)
        for place, value in enumerate(values):
            line = jnp.where(lane == place, value, line)
        meta_send[facet] = line
        return carry

    lax.fori_loop(0, facets, pack, 0)

    pl.semaphore_wait(barrier, facets - 1)
    started = []
    for i, peer in enumerate(targets):
        for src, dst, ssem, rsem in (
            (meta_send, meta_in, meta_send_sem, meta_recv_sem),
            (grid_send, grid_in, send_sem, recv_sem),
        ):
            copy = pltpu.make_async_remote_copy(
                src_ref=src.at[peer], dst_ref=dst.at[me], send_sem=ssem.at[i], recv_sem=rsem.at[i],
                device_id={"facet": peer},
            )
            copy.start()
            started.append(copy)
    own = pltpu.make_async_copy(grid_send.at[me], grid_in.at[me], own_sem.at[0])
    own_meta = pltpu.make_async_copy(meta_send.at[me], meta_in.at[me], own_sem.at[1])
    own.start()
    own_meta.start()
    for copy in started:
        copy.wait()
    own.wait()
    own_meta.wait()


def swapped(values):
    half = values.shape[-1] // 2
    return jnp.concatenate([-values[:, half:], values[:, :half]], 1)


def left_pair(table, one, two):
    upper = jnp.concatenate([one, two], 1)
    lower = jnp.concatenate([swapped(one), swapped(two)], 1)
    out = jnp.dot(table, jnp.concatenate([upper, lower], 0), preferred_element_type=jnp.float32)
    return out.astype(jnp.bfloat16)


def facet_kernel(
    facets, chans,
    meta, grid_in, model, left_f, right_f, left_i, right_i,
    canvas_out, back_out,
    canvas, halves, patches,
):
    rows = F_ROWS // chans
    lane = lax.broadcasted_iota(jnp.int32, (SUB, LANES), 1)
    zero = jnp.zeros((F_ROWS, LANES), jnp.float32)

    def clear(tile, carry):
        canvas[0, tile] = zero
        canvas[1, tile] = zero
        return carry

    lax.fori_loop(0, TILES + 1, clear, 0)

    def forward(facet, carry):
        out = left_pair(left_f[...], grid_in[facet, 0], grid_in[facet, 1])
        halves[pl.ds(pl.multiple_of(facet * 2 * SUB, 2 * SUB), SUB), :] = out[:, :LANES]
        halves[pl.ds(pl.multiple_of(facet * 2 * SUB + SUB, SUB), SUB), :] = out[:, LANES:]
        return carry

    lax.fori_loop(0, facets, forward, 0, unroll=4)

    def forward_right(block, carry):
        at = pl.ds(pl.multiple_of(block * 256, 256), 256)
        patches[at, :] = jnp.dot(halves[at, :], right_f[...], preferred_element_type=jnp.float32)
        return carry

    lax.fori_loop(0, facets * SLOTS * SUB // 256, forward_right, 0, unroll=2)

    def add(facet, carry):
        for slot in range(SLOTS):
            valid = meta[facet, 0, 3 * slot]

            @pl.when(valid > 0)
            def _():
                top = meta[facet, 0, 3 * slot + 1]
                col = meta[facet, 0, 3 * slot + 2]
                tile, shift = col // LANES, lax.rem(col, LANES)
                patch = patches[pl.ds(pl.multiple_of((facet * 2 + slot) * SUB, SUB), SUB), :]
                inside = (lane >= shift) & (lane < shift + SUB)
                at = pl.ds(top, SUB)
                turned = (
                    pltpu.roll(patch, shift, 1),
                    pltpu.roll(patch, lax.rem(shift + SUB, LANES), 1),
                )
                for part in range(2):
                    canvas[part, tile, at, :] += jnp.where(inside, turned[part], 0.0)

                @pl.when(shift > SUB)
                def _():
                    beyond = lane < shift - SUB
                    for part in range(2):
                        canvas[part, tile + 1, at, :] += jnp.where(beyond, turned[part], 0.0)

        return carry

    lax.fori_loop(0, facets, add, 0)

    def emit(pair, carry):
        for part in range(2):
            for chan in range(chans):
                both = jnp.concatenate(
                    [canvas[part, 2 * pair + i, pl.ds(chan * rows, rows), :] for i in range(2)], 0
                )
                at = pl.ds(pl.multiple_of(part * (TILES * rows) + pair * 2 * rows, 2 * rows), 2 * rows)
                canvas_out[chan, at, :] = both.astype(jnp.bfloat16)
        return carry

    lax.fori_loop(0, TILES // 2, emit, 0)

    def pick(facet, carry):
        picked = []
        for slot in range(SLOTS):
            top = meta[facet, 0, 3 * slot + 1]
            col = meta[facet, 0, 3 * slot + 2]
            tile, shift = col // LANES, lax.rem(col, LANES)
            after = jnp.minimum(tile + 1, TILES - 1)
            at = pl.ds(top, SUB)
            parts = [
                jnp.where(lane >= shift, model[part, tile, at, :], model[part, after, at, :])
                for part in range(2)
            ]
            re = pltpu.roll(parts[0], lax.rem(LANES - shift, LANES), 1)
            im = pltpu.roll(parts[1], lax.rem(LANES + SUB - shift, LANES), 1)
            picked.append(jnp.where(lane < SUB, re, im).astype(jnp.bfloat16))
        out = left_pair(left_i[...], picked[0], picked[1])
        halves[pl.ds(pl.multiple_of(facet * 2 * SUB, 2 * SUB), SUB), :] = out[:, :LANES]
        halves[pl.ds(pl.multiple_of(facet * 2 * SUB + SUB, SUB), SUB), :] = out[:, LANES:]
        return carry

    lax.fori_loop(0, facets, pick, 0, unroll=2)

    def inverse_right(block, carry):
        at = pl.ds(pl.multiple_of(block * 256, 256), 256)
        out = jnp.dot(halves[at, :], right_i[...], preferred_element_type=jnp.float32)
        out = out.astype(jnp.bfloat16)
        for i in range(2):
            for slot in range(SLOTS):
                begin = (2 * i + slot) * SUB
                back_out[2 * block + i, slot] = out[begin : begin + SUB]
        return carry

    lax.fori_loop(0, facets * SLOTS * SUB // 256, inverse_right, 0, unroll=2)


PIECES = 4


def exchange_kernel(
    facets, side, chans,
    canvas, back,
    total, returned,
    pair_buf, send_buf, recv_buf,
    pair_send, pair_recv, ring_send, ring_recv, back_send, back_recv, own_sem,
):
    chips = chans // 2
    me_f, me_c = lax.axis_index("facet"), lax.axis_index("chan")
    z, core = me_c // 2, lax.rem(me_c, 2)
    partner = z * 2 + 1 - core
    right = lax.rem(z + 1, chips) * 2 + core
    left = lax.rem(z + chips - 1, chips) * 2 + core
    targets, _ = facet_peers(me_f, side)
    barrier = pltpu.get_barrier_semaphore()
    for peer in (partner, right, left):
        pl.semaphore_signal(barrier, inc=1, device_id={"chan": peer})
    for peer in targets:
        pl.semaphore_signal(barrier, inc=1, device_id={"facet": peer})
    pl.semaphore_wait(barrier, 3 + facets - 1)

    half = chips // 2
    offsets = [half]
    for d in range(half - 1, 0, -1):
        offsets += [d, chips - d]
    offsets += [0]
    waits = []
    pair_copy = {}
    for offset in offsets:
        there = lax.rem(z + offset, chips)
        copy = pltpu.make_async_remote_copy(
            src_ref=canvas.at[2 * there + 1 - core], dst_ref=pair_buf.at[offset],
            send_sem=pair_send.at[offset], recv_sem=pair_recv.at[offset], device_id={"chan": partner},
        )
        copy.start()
        pair_copy[offset] = copy
    for i, peer in enumerate(targets):
        copy = pltpu.make_async_remote_copy(
            src_ref=back.at[peer], dst_ref=returned.at[me_f],
            send_sem=back_send.at[i], recv_sem=back_recv.at[i], device_id={"facet": peer},
        )
        copy.start()
        waits.append(copy)
    own = pltpu.make_async_copy(back.at[me_f], returned.at[me_f], own_sem)
    own.start()

    depth = canvas.shape[1] // PIECES
    arrived = set()

    def mine(offset, piece):
        if offset not in arrived:
            arrived.add(offset)
            pair_copy[offset].wait_recv()
        at = pl.ds(piece * depth, depth)
        there = lax.rem(z + offset, chips)
        return canvas[2 * there + core, at, :].astype(jnp.float32) + pair_buf[offset, at, :].astype(
            jnp.float32
        )

    def length(piece, way):
        return half - (piece + way) % 2

    ring = {}
    for step in range(half + 1):
        for piece in range(PIECES):
            for way in range(2):
                count = length(piece, way)
                if step >= count:
                    continue
                distance = count - step
                offset = distance if way == 0 else chips - distance
                value = mine(offset % chips, piece)
                slot = (way * PIECES + piece) * half + step
                if step > 0:
                    ring[way, piece, step - 1].wait_recv()
                    value = value + recv_buf[slot - 1].astype(jnp.float32)
                send_buf[slot] = value.astype(jnp.bfloat16)
                copy = pltpu.make_async_remote_copy(
                    src_ref=send_buf.at[slot], dst_ref=recv_buf.at[slot],
                    send_sem=ring_send.at[slot], recv_sem=ring_recv.at[slot],
                    device_id={"chan": right if way == 0 else left},
                )
                copy.start()
                ring[way, piece, step] = copy
    for piece in range(PIECES):
        value = mine(0, piece)
        for way in range(2):
            step = length(piece, way) - 1
            ring[way, piece, step].wait_recv()
            value = value + recv_buf[(way * PIECES + piece) * half + step].astype(jnp.float32)
        total[pl.ds(piece * depth, depth), :] = value
    for copy in pair_copy.values():
        copy.wait_send()
    for copy in ring.values():
        copy.wait_send()
    for copy in waits:
        copy.wait()
    own.wait()


def residual_kernel(subgrids, facets, cnt, fid, vis, ku, kv, returned, out, seen):
    def clear(facet, carry):
        seen[facet] = 0
        return carry

    lax.fori_loop(0, facets, clear, 0)

    def one(s, carry):
        facet = fid[s]
        slot = seen[facet]
        seen[facet] = slot + 1
        image = returned[facet, slot]
        inner = lax.dot_general(
            image, ku[s], (((0,), (0,)), ((), ())), preferred_element_type=jnp.float32
        )
        weight = kv[s].astype(jnp.float32)
        live = live_row(cnt[s])
        for part in range(2):
            predicted = jnp.sum(inner[part * SUB : (part + 1) * SUB] * weight, 0, keepdims=True)
            out[s, pl.ds(part, 1), :] = (vis[s, pl.ds(part, 1), :] - predicted) * live
        return carry

    lax.fori_loop(0, subgrids, one, 0)


VMEM = pl.BlockSpec(memory_space=pltpu.VMEM)
SMEM = pl.BlockSpec(memory_space=pltpu.SMEM)


def per_device(
    visibility, uv_coords, vis_count, subgrid_facet, row_offset, col_offset, model_facet
):
    facets, chans = lax.axis_size("facet"), lax.axis_size("chan")
    side = math.isqrt(facets)
    chips = chans // 2
    subgrids = visibility.shape[0]
    rows = F_ROWS // chans
    shape = jax.ShapeDtypeStruct
    left_f, right_f, left_i, right_i = (jnp.asarray(table) for table in dft_tables())
    ids = subgrid_facet[:, 0]
    big = 60 << 20

    ku, kv, grid_in, meta = pl.pallas_call(
        functools.partial(grid_kernel, facets, side, subgrids),
        out_shape=(
            shape((subgrids, SUB, NV), jnp.bfloat16),
            shape((subgrids, SUB, NV), jnp.bfloat16),
            shape((facets, SLOTS, SUB, LANES), jnp.bfloat16),
            shape((facets, 1, LANES), jnp.int32),
        ),
        in_specs=[SMEM] * 4 + [VMEM] * 2,
        out_specs=(VMEM,) * 4,
        scratch_shapes=[
            pltpu.VMEM((subgrids, SUB, LANES), jnp.bfloat16),
            pltpu.VMEM((facets, SLOTS, SUB, LANES), jnp.bfloat16),
            pltpu.VMEM((facets, 1, LANES), jnp.int32),
            pltpu.SMEM((facets,), jnp.int32),
            pltpu.SMEM((facets,), jnp.int32),
            pltpu.SemaphoreType.DMA((facets - 1,)),
            pltpu.SemaphoreType.DMA((facets - 1,)),
            pltpu.SemaphoreType.DMA((facets - 1,)),
            pltpu.SemaphoreType.DMA((facets - 1,)),
            pltpu.SemaphoreType.DMA((2,)),
        ],
        compiler_params=pltpu.CompilerParams(collective_id=0, has_side_effects=True),
        name="grid_and_send",
    )(vis_count, ids, row_offset, col_offset, visibility, uv_coords)

    model = (
        model_facet[0]
        .reshape(F_ROWS, 2, TILES, LANES)
        .transpose(1, 2, 0, 3)
        .astype(jnp.float32)
    )
    canvas, back = pl.pallas_call(
        functools.partial(facet_kernel, facets, chans),
        out_shape=(
            shape((chans, 2 * TILES * rows, LANES), jnp.bfloat16),
            shape((facets, SLOTS, SUB, LANES), jnp.bfloat16),
        ),
        in_specs=[SMEM] + [VMEM] * 6,
        out_specs=(VMEM,) * 2,
        scratch_shapes=[
            pltpu.VMEM((2, TILES + 1, F_ROWS, LANES), jnp.float32),
            pltpu.VMEM((facets * SLOTS * SUB, LANES), jnp.bfloat16),
            pltpu.VMEM((facets * SLOTS * SUB, LANES), jnp.float32),
        ],
        compiler_params=pltpu.CompilerParams(vmem_limit_bytes=40 << 20),
        name="facet_work",
    )(meta, grid_in, model, left_f, right_f, left_i, right_i)

    depth = 2 * TILES * rows // PIECES
    links = 2 * PIECES * (chips // 2)
    total, returned = pl.pallas_call(
        functools.partial(exchange_kernel, facets, side, chans),
        out_shape=(
            shape((2 * TILES * rows, LANES), jnp.float32),
            shape((facets, SLOTS, SUB, LANES), jnp.bfloat16),
        ),
        in_specs=[VMEM] * 2,
        out_specs=(VMEM,) * 2,
        scratch_shapes=[
            pltpu.VMEM((chips, 2 * TILES * rows, LANES), jnp.bfloat16),
            pltpu.VMEM((links, depth, LANES), jnp.bfloat16),
            pltpu.VMEM((links, depth, LANES), jnp.bfloat16),
            pltpu.SemaphoreType.DMA((chips,)),
            pltpu.SemaphoreType.DMA((chips,)),
            pltpu.SemaphoreType.DMA((links,)),
            pltpu.SemaphoreType.DMA((links,)),
            pltpu.SemaphoreType.DMA((facets - 1,)),
            pltpu.SemaphoreType.DMA((facets - 1,)),
            pltpu.SemaphoreType.DMA,
        ],
        compiler_params=pltpu.CompilerParams(collective_id=1, has_side_effects=True),
        name="reduce_and_return",
    )(canvas, back)

    residual = pl.pallas_call(
        functools.partial(residual_kernel, subgrids, facets),
        out_shape=shape(visibility.shape, jnp.float32),
        in_specs=[SMEM] * 2 + [VMEM] * 4,
        out_specs=VMEM,
        scratch_shapes=[pltpu.SMEM((facets,), jnp.int32)],
        name="residual",
    )(vis_count, ids, visibility, ku, kv, returned)

    image = total.reshape(2, TILES, rows, LANES).transpose(2, 0, 1, 3).reshape(1, rows, 2, FACET)
    return image, residual


def solution(mesh):
    in_specs = (
        P(("facet", "chan"), None, None),
        P(("facet", "chan"), None, None),
        P(("facet", "chan")),
        P(("facet", "chan"), None),
        P(("facet", "chan")),
        P(("facet", "chan")),
        P("facet", None, None, None),
    )
    out_specs = (P("facet", "chan", None, None), P(("facet", "chan"), None, None))
    return jax.shard_map(
        per_device, mesh=mesh, in_specs=in_specs, out_specs=out_specs, check_vma=False
    )
```

```python
import functools
import math

import jax
import jax.numpy as jnp
import numpy as np
from jax import lax
from jax.experimental import pallas as pl
from jax.experimental.pallas import tpu as pltpu
from jax.sharding import PartitionSpec as P

SUB = 64
FACET = 4096
F_ROWS = 128
NV = 512
LANES = 128
TILES = FACET // LANES
SLOTS = 2


def dft_tables():
    line = np.arange(SUB)
    angle = 2.0 * math.pi * (line[:, None] * line[None, :] % SUB) / SUB
    cos_table = (np.cos(angle) / math.sqrt(SUB)).astype(jnp.bfloat16)
    sin_table = (-np.sin(angle) / math.sqrt(SUB)).astype(jnp.bfloat16)
    left_forward = np.concatenate([cos_table, sin_table], 1)
    left_inverse = np.concatenate([cos_table, -sin_table], 1)
    right_forward = np.concatenate(
        [np.concatenate([cos_table, sin_table], 1), np.concatenate([-sin_table, cos_table], 1)], 0
    )
    right_inverse = np.concatenate(
        [np.concatenate([cos_table, -sin_table], 1), np.concatenate([sin_table, cos_table], 1)], 0
    )
    return left_forward, right_forward, left_inverse, right_inverse


def kernel_of(coords):
    pixels = lax.broadcasted_iota(jnp.int32, (SUB, NV), 0).astype(jnp.float32)
    delta = pixels - coords
    return jnp.exp(-(delta * delta))


def live_row(count):
    lane = lax.broadcasted_iota(jnp.int32, (1, NV), 1)
    return (lane < count).astype(jnp.float32)


def facet_peers(me, side):
    x, y = me // side, lax.rem(me, side)
    order = {0: 0, 2: 2}
    steps = [(dx, dy) for dx in range(side) for dy in range(side) if dx or dy]
    steps.sort(key=lambda step: -sum(min(d, side - d) for d in step))
    return [lax.rem(x + dx, side) * side + lax.rem(y + dy, side) for dx, dy in steps], [
        lax.rem(x + side - dx, side) * side + lax.rem(y + side - dy, side) for dx, dy in steps
    ]


def grid_kernel(
    facets, side, subgrids,
    cnt, fid, row, col, vis, uv, model,
    ku_out, kv_out, grid_in, meta_in, planes,
    grids, grid_send, meta_send, first, last, raw,
    send_sem, recv_sem, meta_send_sem, meta_recv_sem, own_sem, raw_sem,
):
    me = lax.axis_index("facet")
    targets, sources = facet_peers(me, side)
    barrier = pltpu.get_barrier_semaphore()
    for peer in targets:
        pl.semaphore_signal(barrier, inc=1, device_id={"facet": peer})
    fetch = pltpu.make_async_copy(model.at[0], raw, raw_sem)
    fetch.start()

    ids = [fid[s] for s in range(subgrids)]

    def find(facet, carry):
        low = jnp.int32(subgrids)
        high = jnp.int32(-1)
        for s in range(subgrids):
            same = ids[s] == facet
            high = jnp.where(same, s, high)
            back = subgrids - 1 - s
            low = jnp.where(ids[back] == facet, back, low)
        first[facet] = low
        last[facet] = high
        return carry

    lax.fori_loop(0, facets, find, 0)

    def grid_one(s, carry):
        ku = kernel_of(uv[s, pl.ds(0, 1), :]).astype(jnp.bfloat16)
        kv = kernel_of(uv[s, pl.ds(1, 1), :])
        live = live_row(cnt[s])
        re = (vis[s, pl.ds(0, 1), :] * live) * kv
        im = (vis[s, pl.ds(1, 1), :] * live) * kv
        spread = jnp.concatenate([re.astype(jnp.bfloat16), im.astype(jnp.bfloat16)], 0)
        ku_out[s] = ku
        kv_out[s] = kv.astype(jnp.bfloat16)
        grids[s] = lax.dot_general(
            ku, spread, (((1,), (1,)), ((), ())), preferred_element_type=jnp.float32
        ).astype(jnp.bfloat16)
        return carry

    lax.fori_loop(0, subgrids, grid_one, 0, unroll=2)

    lane = lax.broadcasted_iota(jnp.int32, (1, LANES), 1)

    def pack(facet, carry):
        low, high = first[facet], last[facet]
        one = jnp.minimum(low, subgrids - 1)
        two = jnp.maximum(high, 0)
        grid_send[facet, 0] = grids[one]
        grid_send[facet, 1] = grids[two]
        values = (
            (high >= 0).astype(jnp.int32), row[one], col[one],
            (high > low).astype(jnp.int32), row[two], col[two],
        )
        line = jnp.zeros((1, LANES), jnp.int32)
        for place, value in enumerate(values):
            line = jnp.where(lane == place, value, line)
        meta_send[facet] = line
        return carry

    lax.fori_loop(0, facets, pack, 0)

    pl.semaphore_wait(barrier, facets - 1)
    started = []
    for i, peer in enumerate(targets):
        for src, dst, ssem, rsem in (
            (meta_send, meta_in, meta_send_sem, meta_recv_sem),
            (grid_send, grid_in, send_sem, recv_sem),
        ):
            copy = pltpu.make_async_remote_copy(
                src_ref=src.at[peer], dst_ref=dst.at[me], send_sem=ssem.at[i], recv_sem=rsem.at[i],
                device_id={"facet": peer},
            )
            copy.start()
            started.append(copy)
    own = pltpu.make_async_copy(grid_send.at[me], grid_in.at[me], own_sem.at[0])
    own_meta = pltpu.make_async_copy(meta_send.at[me], meta_in.at[me], own_sem.at[1])
    own.start()
    own_meta.start()
    fetch.wait()

    def split(tile, carry):
        at = pl.ds(pl.multiple_of(tile * LANES, LANES), LANES)
        for part in range(2):
            planes[part, tile] = raw[:, part, at].astype(jnp.float32)
        return carry

    lax.fori_loop(0, TILES, split, 0)
    for copy in started:
        copy.wait()
    own.wait()
    own_meta.wait()


def swapped(values):
    half = values.shape[-1] // 2
    return jnp.concatenate([-values[:, half:], values[:, :half]], 1)


def left_pair(table, one, two):
    upper = jnp.concatenate([one, two], 1)
    lower = jnp.concatenate([swapped(one), swapped(two)], 1)
    out = jnp.dot(table, jnp.concatenate([upper, lower], 0), preferred_element_type=jnp.float32)
    return out.astype(jnp.bfloat16)


def facet_kernel(
    facets, chans,
    meta, grid_in, left_f, right_f,
    canvas_out,
    canvas, halves, patches,
):
    rows = F_ROWS // chans
    lane = lax.broadcasted_iota(jnp.int32, (SUB, LANES), 1)
    zero = jnp.zeros((F_ROWS, LANES), jnp.float32)

    def clear(tile, carry):
        canvas[0, tile] = zero
        canvas[1, tile] = zero
        return carry

    lax.fori_loop(0, TILES + 1, clear, 0)

    def forward(facet, carry):
        out = left_pair(left_f[...], grid_in[facet, 0], grid_in[facet, 1])
        halves[pl.ds(pl.multiple_of(facet * 2 * SUB, 2 * SUB), SUB), :] = out[:, :LANES]
        halves[pl.ds(pl.multiple_of(facet * 2 * SUB + SUB, SUB), SUB), :] = out[:, LANES:]
        return carry

    lax.fori_loop(0, facets, forward, 0, unroll=4)

    def forward_right(block, carry):
        at = pl.ds(pl.multiple_of(block * 256, 256), 256)
        patches[at, :] = jnp.dot(halves[at, :], right_f[...], preferred_element_type=jnp.float32)
        return carry

    lax.fori_loop(0, facets * SLOTS * SUB // 256, forward_right, 0, unroll=2)

    def add(facet, carry):
        for slot in range(SLOTS):
            valid = meta[facet, 0, 3 * slot]

            @pl.when(valid > 0)
            def _():
                top = meta[facet, 0, 3 * slot + 1]
                col = meta[facet, 0, 3 * slot + 2]
                tile, shift = col // LANES, lax.rem(col, LANES)
                patch = patches[pl.ds(pl.multiple_of((facet * 2 + slot) * SUB, SUB), SUB), :]
                inside = (lane >= shift) & (lane < shift + SUB)
                at = pl.ds(top, SUB)
                turned = (
                    pltpu.roll(patch, shift, 1),
                    pltpu.roll(patch, lax.rem(shift + SUB, LANES), 1),
                )
                for part in range(2):
                    canvas[part, tile, at, :] += jnp.where(inside, turned[part], 0.0)

                @pl.when(shift > SUB)
                def _():
                    beyond = lane < shift - SUB
                    for part in range(2):
                        canvas[part, tile + 1, at, :] += jnp.where(beyond, turned[part], 0.0)

        return carry

    lax.fori_loop(0, facets, add, 0)

    def emit(pair, carry):
        for part in range(2):
            for chan in range(chans):
                both = jnp.concatenate(
                    [canvas[part, 2 * pair + i, pl.ds(chan * rows, rows), :] for i in range(2)], 0
                )
                at = pl.ds(pl.multiple_of(part * (TILES * rows) + pair * 2 * rows, 2 * rows), 2 * rows)
                canvas_out[chan, at, :] = both.astype(jnp.bfloat16)
        return carry

    lax.fori_loop(0, TILES // 2, emit, 0)


PIECES = 4


def exchange_kernel(
    facets, side, chans, subgrids,
    meta, cnt, fid, canvas, planes, vis, ku, kv, left_i, right_i,
    total, residual,
    pair_buf, send_buf, recv_buf, halves, back, returned, rank,
    pair_send, pair_recv, ring_send, ring_recv, back_send, back_recv, own_sem,
):
    chips = chans // 2
    me_f, me_c = lax.axis_index("facet"), lax.axis_index("chan")
    z, core = me_c // 2, lax.rem(me_c, 2)
    partner = z * 2 + 1 - core
    right = lax.rem(z + 1, chips) * 2 + core
    left = lax.rem(z + chips - 1, chips) * 2 + core
    targets, _ = facet_peers(me_f, side)
    barrier = pltpu.get_barrier_semaphore()
    for peer in (partner, right, left):
        pl.semaphore_signal(barrier, inc=1, device_id={"chan": peer})
    for peer in targets:
        pl.semaphore_signal(barrier, inc=1, device_id={"facet": peer})

    lane = lax.broadcasted_iota(jnp.int32, (SUB, LANES), 1)

    def pick(facet, carry):
        picked = []
        for slot in range(SLOTS):
            top = meta[facet, 0, 3 * slot + 1]
            col = meta[facet, 0, 3 * slot + 2]
            tile, shift = col // LANES, lax.rem(col, LANES)
            after = jnp.minimum(tile + 1, TILES - 1)
            at = pl.ds(top, SUB)
            parts = [
                jnp.where(lane >= shift, planes[part, tile, at, :], planes[part, after, at, :])
                for part in range(2)
            ]
            re = pltpu.roll(parts[0], lax.rem(LANES - shift, LANES), 1)
            im = pltpu.roll(parts[1], lax.rem(LANES + SUB - shift, LANES), 1)
            picked.append(jnp.where(lane < SUB, re, im).astype(jnp.bfloat16))
        out = left_pair(left_i[...], picked[0], picked[1])
        halves[pl.ds(pl.multiple_of(facet * 2 * SUB, 2 * SUB), SUB), :] = out[:, :LANES]
        halves[pl.ds(pl.multiple_of(facet * 2 * SUB + SUB, SUB), SUB), :] = out[:, LANES:]
        return carry

    def inverse_right(block, carry):
        at = pl.ds(pl.multiple_of(block * 256, 256), 256)
        out = jnp.dot(halves[at, :], right_i[...], preferred_element_type=jnp.float32)
        out = out.astype(jnp.bfloat16)
        for i in range(2):
            for slot in range(SLOTS):
                begin = (2 * i + slot) * SUB
                back[2 * block + i, slot] = out[begin : begin + SUB]
        return carry

    lax.fori_loop(0, facets // 2, pick, 0, unroll=2)
    pl.semaphore_wait(barrier, 3 + facets - 1)

    half = chips // 2
    offsets = [half]
    for d in range(half - 1, 0, -1):
        offsets += [d, chips - d]
    offsets += [0]
    pair_copy = {}
    for offset in offsets:
        there = lax.rem(z + offset, chips)
        copy = pltpu.make_async_remote_copy(
            src_ref=canvas.at[2 * there + 1 - core], dst_ref=pair_buf.at[offset],
            send_sem=pair_send.at[offset], recv_sem=pair_recv.at[offset], device_id={"chan": partner},
        )
        copy.start()
        pair_copy[offset] = copy

    lax.fori_loop(facets // 2, facets, pick, 0, unroll=2)
    lax.fori_loop(0, facets * SLOTS * SUB // 256, inverse_right, 0, unroll=2)
    back_copy = []
    for i, peer in enumerate(targets):
        copy = pltpu.make_async_remote_copy(
            src_ref=back.at[peer], dst_ref=returned.at[me_f],
            send_sem=back_send.at[i], recv_sem=back_recv.at[i], device_id={"facet": peer},
        )
        copy.start()
        back_copy.append(copy)
    own = pltpu.make_async_copy(back.at[me_f], returned.at[me_f], own_sem)
    own.start()

    depth = canvas.shape[1] // PIECES
    arrived = set()

    def mine(offset, piece):
        if offset not in arrived:
            arrived.add(offset)
            pair_copy[offset].wait_recv()
        at = pl.ds(piece * depth, depth)
        there = lax.rem(z + offset, chips)
        return canvas[2 * there + core, at, :].astype(jnp.float32) + pair_buf[offset, at, :].astype(
            jnp.float32
        )

    def length(piece, way):
        return half - (piece + way) % 2

    ring = {}

    def ring_step(step):
        for piece in range(PIECES):
            for way in range(2):
                count = length(piece, way)
                if step >= count:
                    continue
                distance = count - step
                offset = distance if way == 0 else chips - distance
                value = mine(offset % chips, piece)
                slot = (way * PIECES + piece) * half + step
                if step > 0:
                    ring[way, piece, step - 1].wait_recv()
                    value = value + recv_buf[slot - 1].astype(jnp.float32)
                send_buf[slot] = value.astype(jnp.bfloat16)
                copy = pltpu.make_async_remote_copy(
                    src_ref=send_buf.at[slot], dst_ref=recv_buf.at[slot],
                    send_sem=ring_send.at[slot], recv_sem=ring_recv.at[slot],
                    device_id={"chan": right if way == 0 else left},
                )
                copy.start()
                ring[way, piece, step] = copy

    def degrid(s, carry):
        image = returned[fid[s], rank[s]]
        inner = lax.dot_general(
            image, ku[s], (((0,), (0,)), ((), ())), preferred_element_type=jnp.float32
        )
        weight = kv[s].astype(jnp.float32)
        live = live_row(cnt[s])
        for part in range(2):
            predicted = jnp.sum(inner[part * SUB : (part + 1) * SUB] * weight, 0, keepdims=True)
            residual[s, pl.ds(part, 1), :] = (vis[s, pl.ds(part, 1), :] - predicted) * live
        return carry

    ring_step(0)
    ids = [fid[s] for s in range(subgrids)]
    for s in range(subgrids):
        before = jnp.int32(0)
        for other in range(s):
            before = jnp.where(ids[other] == ids[s], 1, before)
        rank[s] = before
    for step in range(1, half - 1):
        ring_step(step)
    for copy in back_copy:
        copy.wait()
    own.wait()
    lax.fori_loop(0, subgrids // 2, degrid, 0, unroll=2)
    ring_step(half - 1)
    lax.fori_loop(subgrids // 2, subgrids, degrid, 0, unroll=2)
    for piece in range(PIECES):
        value = mine(0, piece)
        for way in range(2):
            step = length(piece, way) - 1
            ring[way, piece, step].wait_recv()
            value = value + recv_buf[(way * PIECES + piece) * half + step].astype(jnp.float32)
        total[pl.ds(piece * depth, depth), :] = value
    for copy in pair_copy.values():
        copy.wait_send()
    for copy in ring.values():
        copy.wait_send()


VMEM = pl.BlockSpec(memory_space=pltpu.VMEM)
SMEM = pl.BlockSpec(memory_space=pltpu.SMEM)
HBM = pl.BlockSpec(memory_space=pltpu.HBM)


def per_device(
    visibility, uv_coords, vis_count, subgrid_facet, row_offset, col_offset, model_facet
):
    facets, chans = lax.axis_size("facet"), lax.axis_size("chan")
    side = math.isqrt(facets)
    chips = chans // 2
    subgrids = visibility.shape[0]
    rows = F_ROWS // chans
    shape = jax.ShapeDtypeStruct
    left_f, right_f, left_i, right_i = (jnp.asarray(table) for table in dft_tables())
    ids = subgrid_facet[:, 0]

    ku, kv, grid_in, meta, planes = pl.pallas_call(
        functools.partial(grid_kernel, facets, side, subgrids),
        out_shape=(
            shape((subgrids, SUB, NV), jnp.bfloat16),
            shape((subgrids, SUB, NV), jnp.bfloat16),
            shape((facets, SLOTS, SUB, LANES), jnp.bfloat16),
            shape((facets, 1, LANES), jnp.int32),
            shape((2, TILES, F_ROWS, LANES), jnp.float32),
        ),
        in_specs=[SMEM] * 4 + [VMEM] * 2 + [HBM],
        out_specs=(VMEM,) * 5,
        scratch_shapes=[
            pltpu.VMEM((subgrids, SUB, LANES), jnp.bfloat16),
            pltpu.VMEM((facets, SLOTS, SUB, LANES), jnp.bfloat16),
            pltpu.VMEM((facets, 1, LANES), jnp.int32),
            pltpu.SMEM((facets,), jnp.int32),
            pltpu.SMEM((facets,), jnp.int32),
            pltpu.VMEM(model_facet.shape[1:], jnp.bfloat16),
            pltpu.SemaphoreType.DMA((facets - 1,)),
            pltpu.SemaphoreType.DMA((facets - 1,)),
            pltpu.SemaphoreType.DMA((facets - 1,)),
            pltpu.SemaphoreType.DMA((facets - 1,)),
            pltpu.SemaphoreType.DMA((2,)),
            pltpu.SemaphoreType.DMA,
        ],
        compiler_params=pltpu.CompilerParams(
            collective_id=0, has_side_effects=True, vmem_limit_bytes=16 << 20
        ),
        name="grid_and_send",
    )(vis_count, ids, row_offset, col_offset, visibility, uv_coords, model_facet)

    canvas = pl.pallas_call(
        functools.partial(facet_kernel, facets, chans),
        out_shape=shape((chans, 2 * TILES * rows, LANES), jnp.bfloat16),
        in_specs=[SMEM] + [VMEM] * 3,
        out_specs=VMEM,
        scratch_shapes=[
            pltpu.VMEM((2, TILES + 1, F_ROWS, LANES), jnp.float32),
            pltpu.VMEM((facets * SLOTS * SUB, LANES), jnp.bfloat16),
            pltpu.VMEM((facets * SLOTS * SUB, LANES), jnp.float32),
        ],
        compiler_params=pltpu.CompilerParams(vmem_limit_bytes=16 << 20),
        name="facet_work",
    )(meta, grid_in, left_f, right_f)

    depth = 2 * TILES * rows // PIECES
    links = 2 * PIECES * (chips // 2)
    total, residual = pl.pallas_call(
        functools.partial(exchange_kernel, facets, side, chans, subgrids),
        out_shape=(
            shape((2 * TILES * rows, LANES), jnp.float32),
            shape(visibility.shape, jnp.float32),
        ),
        in_specs=[SMEM] * 3 + [VMEM] * 7,
        out_specs=(VMEM,) * 2,
        scratch_shapes=[
            pltpu.VMEM((chips, 2 * TILES * rows, LANES), jnp.bfloat16),
            pltpu.VMEM((links, depth, LANES), jnp.bfloat16),
            pltpu.VMEM((links, depth, LANES), jnp.bfloat16),
            pltpu.VMEM((facets * SLOTS * SUB, LANES), jnp.bfloat16),
            pltpu.VMEM((facets, SLOTS, SUB, LANES), jnp.bfloat16),
            pltpu.VMEM((facets, SLOTS, SUB, LANES), jnp.bfloat16),
            pltpu.SMEM((subgrids,), jnp.int32),
            pltpu.SemaphoreType.DMA((chips,)),
            pltpu.SemaphoreType.DMA((chips,)),
            pltpu.SemaphoreType.DMA((links,)),
            pltpu.SemaphoreType.DMA((links,)),
            pltpu.SemaphoreType.DMA((facets - 1,)),
            pltpu.SemaphoreType.DMA((facets - 1,)),
            pltpu.SemaphoreType.DMA,
        ],
        compiler_params=pltpu.CompilerParams(
            collective_id=1, has_side_effects=True, vmem_limit_bytes=20 << 20
        ),
        name="reduce_and_return",
    )(meta, vis_count, ids, canvas, planes, visibility, ku, kv, left_i, right_i)

    image = total.reshape(2, TILES, rows, LANES).transpose(2, 0, 1, 3).reshape(1, rows, 2, FACET)
    return image, residual


def solution(mesh):
    in_specs = (
        P(("facet", "chan"), None, None),
        P(("facet", "chan"), None, None),
        P(("facet", "chan")),
        P(("facet", "chan"), None),
        P(("facet", "chan")),
        P(("facet", "chan")),
        P("facet", None, None, None),
    )
    out_specs = (P("facet", "chan", None, None), P(("facet", "chan"), None, None))
    return jax.shard_map(
        per_device, mesh=mesh, in_specs=in_specs, out_specs=out_specs, check_vma=False
    )
```

```python
import functools
import math

import jax
import jax.numpy as jnp
import numpy as np
from jax import lax
from jax.experimental import pallas as pl
from jax.experimental.pallas import tpu as pltpu
from jax.sharding import PartitionSpec as P

SUB = 64
FACET = 4096
F_ROWS = 128
NV = 512
LANES = 128
TILES = FACET // LANES
SLOTS = 2


def dft_tables():
    line = np.arange(SUB)
    angle = 2.0 * math.pi * (line[:, None] * line[None, :] % SUB) / SUB
    cos_table = (np.cos(angle) / math.sqrt(SUB)).astype(jnp.bfloat16)
    sin_table = (-np.sin(angle) / math.sqrt(SUB)).astype(jnp.bfloat16)
    left_forward = np.concatenate([cos_table, sin_table], 1)
    left_inverse = np.concatenate([cos_table, -sin_table], 1)
    right_forward = np.concatenate(
        [np.concatenate([cos_table, sin_table], 1), np.concatenate([-sin_table, cos_table], 1)], 0
    )
    right_inverse = np.concatenate(
        [np.concatenate([cos_table, -sin_table], 1), np.concatenate([sin_table, cos_table], 1)], 0
    )
    return left_forward, right_forward, left_inverse, right_inverse


def kernel_of(coords):
    pixels = lax.broadcasted_iota(jnp.int32, (SUB, NV), 0).astype(jnp.float32)
    delta = pixels - coords
    return jnp.exp(-(delta * delta))


def live_row(count):
    lane = lax.broadcasted_iota(jnp.int32, (1, NV), 1)
    return (lane < count).astype(jnp.float32)


def facet_steps(me, side):
    x, y = me // side, lax.rem(me, side)
    targets, sources = [], []
    for step in range(1, side * side):
        dx, dy = step // side, step % side
        targets.append(lax.rem(x + dx, side) * side + lax.rem(y + dy, side))
        sources.append(lax.rem(x + side - dx, side) * side + lax.rem(y + side - dy, side))
    return targets, sources


def swapped(values):
    half = values.shape[-1] // 2
    return jnp.concatenate([-values[:, half:], values[:, :half]], 1)


def left_pair(table, one, two):
    upper = jnp.concatenate([one, two], 1)
    lower = jnp.concatenate([swapped(one), swapped(two)], 1)
    out = jnp.dot(table, jnp.concatenate([upper, lower], 0), preferred_element_type=jnp.float32)
    return out.astype(jnp.bfloat16)


def gridded(lines):
    ku = kernel_of(lines[2:3]).astype(jnp.bfloat16)
    kv = kernel_of(lines[3:4])
    spread = jnp.concatenate(
        [(lines[0:1] * kv).astype(jnp.bfloat16), (lines[1:2] * kv).astype(jnp.bfloat16)], 0
    )
    return lax.dot_general(
        ku, spread, (((1,), (1,)), ((), ())), preferred_element_type=jnp.float32
    ).astype(jnp.bfloat16)


GROUP = 2


def grid_kernel(
    facets, side, subgrids,
    cnt_hbm, fid_hbm, row_hbm, col_hbm, vis_hbm, uv_hbm, model, left_hbm, right_hbm,
    patches, meta_in, model_rows,
    cnt, fid, row, col, vis, uv, left_f, right_f, raw, lines_send, lines_in, meta_send, first, last,
    in_sem, raw_sem, send_sem, recv_sem, meta_send_sem, meta_recv_sem, own_sem,
):
    me = lax.axis_index("facet")
    targets, _ = facet_steps(me, side)
    barrier = pltpu.get_barrier_semaphore()
    for peer in targets:
        pl.semaphore_signal(barrier, inc=1, device_id={"facet": peer})
    fetches = []
    for i, (src, dst) in enumerate((
        (fid_hbm, fid), (cnt_hbm, cnt), (row_hbm, row), (col_hbm, col), (vis_hbm, vis), (uv_hbm, uv),
        (left_hbm, left_f), (right_hbm, right_f),
    )):
        fetch = pltpu.make_async_copy(src, dst, in_sem.at[i])
        fetch.start()
        fetches.append(fetch)

    def model_copy(tile):
        at = pl.ds(pl.multiple_of(tile * LANES, LANES), LANES)
        return pltpu.make_async_copy(model.at[0, :, :, at], raw.at[tile], raw_sem.at[tile])

    def fetch_model(tile, carry):
        model_copy(tile).start()
        return carry

    lax.fori_loop(0, TILES, fetch_model, 0)
    for fetch in fetches:
        fetch.wait()

    ids = [fid[s] for s in range(subgrids)]

    def find(facet, carry):
        low = jnp.int32(subgrids)
        high = jnp.int32(-1)
        for s in range(subgrids):
            high = jnp.where(ids[s] == facet, s, high)
            back = subgrids - 1 - s
            low = jnp.where(ids[back] == facet, back, low)
        first[facet] = low
        last[facet] = high
        return carry

    lax.fori_loop(0, facets, find, 0)

    lane = lax.broadcasted_iota(jnp.int32, (1, LANES), 1)

    def pack(facet, carry):
        low, high = first[facet], last[facet]
        one = jnp.minimum(low, subgrids - 1)
        two = jnp.maximum(high, 0)
        lines_send[facet] = jnp.concatenate(
            [vis[one] * live_row(cnt[one]), uv[one], vis[two] * live_row(cnt[two]), uv[two]], 0
        )
        values = (
            (high >= 0).astype(jnp.int32), row[one], col[one],
            (high > low).astype(jnp.int32), row[two], col[two],
        )
        line = jnp.zeros((1, LANES), jnp.int32)
        for place, value in enumerate(values):
            line = jnp.where(lane == place, value, line)
        meta_send[facet] = line
        return carry

    lax.fori_loop(0, facets, pack, 0)

    pl.semaphore_wait(barrier, facets - 1)
    copies = [None]
    metas = []
    for step, peer in enumerate(targets, 1):
        pair = []
        for src, dst, ssem, rsem in (
            (meta_send, meta_in, meta_send_sem, meta_recv_sem),
            (lines_send, lines_in, send_sem, recv_sem),
        ):
            copy = pltpu.make_async_remote_copy(
                src_ref=src.at[peer], dst_ref=dst.at[step], send_sem=ssem.at[step],
                recv_sem=rsem.at[step], device_id={"facet": peer},
            )
            copy.start()
            pair.append(copy)
        metas.append(pair[0])
        copies.append(pair[1])
    own = pltpu.make_async_copy(lines_send.at[me], lines_in.at[0], own_sem.at[0])
    own_meta = pltpu.make_async_copy(meta_send.at[me], meta_in.at[0], own_sem.at[1])
    own.start()
    own_meta.start()

    rows_view = raw.reshape(TILES, 2 * F_ROWS, LANES)

    def widen(tile, carry):
        model_copy(tile).wait()
        model_rows[tile] = rows_view[tile].astype(jnp.float32)
        return carry

    lax.fori_loop(0, TILES, widen, 0)

    own.wait()
    own_meta.wait()
    for begin in range(0, facets, GROUP):
        halves = []
        for step in range(begin, begin + GROUP):
            if step > 0:
                copies[step].wait_recv()
        for step in range(begin, begin + GROUP):
            lines = lines_in[step]
            out = left_pair(left_f[...], gridded(lines[:4]), gridded(lines[4:]))
            halves += [out[:, :LANES], out[:, LANES:]]
        out = jnp.dot(
            jnp.concatenate(halves, 0), right_f[...], preferred_element_type=jnp.float32
        )
        patches[pl.ds(begin * SLOTS * SUB, GROUP * SLOTS * SUB), :] = out
    for copy in copies[1:]:
        copy.wait_send()
    for copy in metas:
        copy.wait()


def add_kernel(facets, meta, patches, canvas):
    lane = lax.broadcasted_iota(jnp.int32, (SUB, LANES), 1)
    zero = jnp.zeros((F_ROWS, LANES), jnp.float32)

    def clear(tile, carry):
        canvas[0, tile] = zero
        canvas[1, tile] = zero
        return carry

    lax.fori_loop(0, TILES, clear, 0)

    def add(step, carry):
        for slot in range(SLOTS):
            valid = meta[step, 0, 3 * slot]

            @pl.when(valid > 0)
            def _():
                top = meta[step, 0, 3 * slot + 1]
                col = meta[step, 0, 3 * slot + 2]
                tile, shift = col // LANES, lax.rem(col, LANES)
                patch = patches[pl.ds(pl.multiple_of((step * 2 + slot) * SUB, SUB), SUB), :]
                inside = (lane >= shift) & (lane < shift + SUB)
                at = pl.ds(top, SUB)
                turned = (
                    pltpu.roll(patch, shift, 1),
                    pltpu.roll(patch, lax.rem(shift + SUB, LANES), 1),
                )
                for part in range(2):
                    canvas[part, tile, at, :] += jnp.where(inside, turned[part], 0.0)

                @pl.when(shift > SUB)
                def _():
                    beyond = lane < shift - SUB
                    for part in range(2):
                        canvas[part, tile + 1, at, :] += jnp.where(beyond, turned[part], 0.0)

        return carry

    lax.fori_loop(0, facets, add, 0)


PIECES = 4


def exchange_kernel(
    facets, side, chans, subgrids,
    meta, cnt, fid, canvas, model_rows, vis, uv, left_i, right_i,
    total, residual,
    half_buf, pair_buf, send_buf, recv_buf, halves, back, returned, place,
    pair_send, pair_recv, ring_send, ring_recv, back_send, back_recv, own_sem,
):
    chips = chans // 2
    me_f, me_c = lax.axis_index("facet"), lax.axis_index("chan")
    z, core = me_c // 2, lax.rem(me_c, 2)
    partner = z * 2 + 1 - core
    right = lax.rem(z + 1, chips) * 2 + core
    left = lax.rem(z + chips - 1, chips) * 2 + core
    targets, sources = facet_steps(me_f, side)
    rows = F_ROWS // chans
    barrier = pltpu.get_barrier_semaphore()
    for peer in (partner, right, left):
        pl.semaphore_signal(barrier, inc=1, device_id={"chan": peer})
    for peer in targets:
        pl.semaphore_signal(barrier, inc=1, device_id={"facet": peer})

    lane = lax.broadcasted_iota(jnp.int32, (SUB, LANES), 1)

    def pick(facet, carry):
        picked = []
        for slot in range(SLOTS):
            top = meta[facet, 0, 3 * slot + 1]
            col = meta[facet, 0, 3 * slot + 2]
            tile, shift = col // LANES, lax.rem(col, LANES)
            after = jnp.minimum(tile + 1, TILES - 1)
            parts = [
                jnp.where(
                    lane >= shift,
                    model_rows[tile, pl.ds(2 * top + part, SUB, stride=2), :],
                    model_rows[after, pl.ds(2 * top + part, SUB, stride=2), :],
                )
                for part in range(2)
            ]
            re = pltpu.roll(parts[0], lax.rem(LANES - shift, LANES), 1)
            im = pltpu.roll(parts[1], lax.rem(LANES + SUB - shift, LANES), 1)
            picked.append(jnp.where(lane < SUB, re, im).astype(jnp.bfloat16))
        out = left_pair(left_i[...], picked[0], picked[1])
        halves[pl.ds(pl.multiple_of(facet * 2 * SUB, 2 * SUB), SUB), :] = out[:, :LANES]
        halves[pl.ds(pl.multiple_of(facet * 2 * SUB + SUB, SUB), SUB), :] = out[:, LANES:]
        return carry

    def inverse_right(block, carry):
        at = pl.ds(pl.multiple_of(block * 256, 256), 256)
        out = jnp.dot(halves[at, :], right_i[...], preferred_element_type=jnp.float32)
        out = out.astype(jnp.bfloat16)
        for i in range(2):
            for slot in range(SLOTS):
                begin = (2 * i + slot) * SUB
                back[2 * block + i, slot] = out[begin : begin + SUB]
        return carry

    half = chips // 2
    offsets = [half]
    for d in range(half - 1, 0, -1):
        offsets += [d, chips - d]
    offsets += [0]

    def chan_rows(offset, which):
        there = lax.rem(z + offset, chips)
        return pl.ds(pl.multiple_of((2 * there + which) * rows, rows), rows)

    def narrow(pair, carry):
        for offset in range(chips):
            for part in range(2):
                both = canvas[part, pl.ds(2 * pair, 2), chan_rows(offset, 1 - core), :]
                at = pl.ds(pl.multiple_of((part * TILES + 2 * pair) * rows, 2 * rows), 2 * rows)
                half_buf[offset, at, :] = both.reshape(2 * rows, LANES).astype(jnp.bfloat16)
        return carry

    lax.fori_loop(0, TILES // 2, narrow, 0)
    pl.semaphore_wait(barrier, 3 + facets - 1)

    pair_copy = {}
    for offset in offsets:
        copy = pltpu.make_async_remote_copy(
            src_ref=half_buf.at[offset], dst_ref=pair_buf.at[offset],
            send_sem=pair_send.at[offset], recv_sem=pair_recv.at[offset], device_id={"chan": partner},
        )
        copy.start()
        pair_copy[offset] = copy

    lax.fori_loop(0, facets // 2, pick, 0, unroll=2)

    depth = half_buf.shape[1] // PIECES
    arrived = set()

    def mine(offset, piece):
        if offset not in arrived:
            arrived.add(offset)
            pair_copy[offset].wait_recv()
        at = pl.ds(piece * depth, depth)
        tiles = TILES * 2 // PIECES
        part, begin = divmod(piece * tiles, TILES)
        own = canvas[part, pl.ds(begin, tiles), chan_rows(offset, core), :]
        return own.reshape(depth, LANES) + pair_buf[offset, at, :].astype(jnp.float32)

    def length(piece, way):
        return half - (piece + way) % 2

    ring = {}

    def ring_step(step):
        for piece in range(PIECES):
            for way in range(2):
                count = length(piece, way)
                if step >= count:
                    continue
                distance = count - step
                offset = distance if way == 0 else chips - distance
                value = mine(offset % chips, piece)
                slot = (way * PIECES + piece) * half + step
                if step > 0:
                    ring[way, piece, step - 1].wait_recv()
                    value = value + recv_buf[slot - 1].astype(jnp.float32)
                send_buf[slot] = value.astype(jnp.bfloat16)
                copy = pltpu.make_async_remote_copy(
                    src_ref=send_buf.at[slot], dst_ref=recv_buf.at[slot],
                    send_sem=ring_send.at[slot], recv_sem=ring_recv.at[slot],
                    device_id={"chan": right if way == 0 else left},
                )
                copy.start()
                ring[way, piece, step] = copy

    def degrid(s, carry):
        image = returned[place[s], place[subgrids + s]]
        ku = kernel_of(uv[s, pl.ds(0, 1), :]).astype(jnp.bfloat16)
        weight = kernel_of(uv[s, pl.ds(1, 1), :])
        inner = lax.dot_general(
            image, ku, (((0,), (0,)), ((), ())), preferred_element_type=jnp.float32
        )
        live = live_row(cnt[s])
        for part in range(2):
            predicted = jnp.sum(inner[part * SUB : (part + 1) * SUB] * weight, 0, keepdims=True)
            residual[s, pl.ds(part, 1), :] = (vis[s, pl.ds(part, 1), :] - predicted) * live
        return carry

    ring_step(0)
    lax.fori_loop(facets // 2, facets, pick, 0, unroll=2)
    lax.fori_loop(0, facets * SLOTS * SUB // 256, inverse_right, 0, unroll=2)
    back_copy = []
    for step in range(1, facets):
        copy = pltpu.make_async_remote_copy(
            src_ref=back.at[step], dst_ref=returned.at[step],
            send_sem=back_send.at[step], recv_sem=back_recv.at[step],
            device_id={"facet": sources[step - 1]},
        )
        copy.start()
        back_copy.append(copy)
    own = pltpu.make_async_copy(back.at[0], returned.at[0], own_sem)
    own.start()
    ring_step(1)
    ids = [fid[s] for s in range(subgrids)]
    x, y = me_f // side, lax.rem(me_f, side)
    for s in range(subgrids):
        before = jnp.int32(0)
        for other in range(s):
            before = jnp.where(ids[other] == ids[s], 1, before)
        there_x, there_y = ids[s] // side, lax.rem(ids[s], side)
        place[s] = lax.rem(there_x + side - x, side) * side + lax.rem(there_y + side - y, side)
        place[subgrids + s] = before
    ring_step(2)
    for copy in back_copy:
        copy.wait()
    own.wait()
    lax.fori_loop(0, subgrids // 2, degrid, 0, unroll=2)
    ring_step(3)
    lax.fori_loop(subgrids // 2, subgrids, degrid, 0, unroll=2)
    for piece in range(PIECES):
        value = mine(0, piece)
        for way in range(2):
            step = length(piece, way) - 1
            ring[way, piece, step].wait_recv()
            value = value + recv_buf[(way * PIECES + piece) * half + step].astype(jnp.float32)
        total[pl.ds(piece * depth, depth), :] = value
    for copy in pair_copy.values():
        copy.wait_send()
    for copy in ring.values():
        copy.wait_send()


VMEM = pl.BlockSpec(memory_space=pltpu.VMEM)
SMEM = pl.BlockSpec(memory_space=pltpu.SMEM)
HBM = pl.BlockSpec(memory_space=pltpu.HBM)


def per_device(
    visibility, uv_coords, vis_count, subgrid_facet, row_offset, col_offset, model_facet
):
    facets, chans = lax.axis_size("facet"), lax.axis_size("chan")
    side = math.isqrt(facets)
    chips = chans // 2
    subgrids = visibility.shape[0]
    rows = F_ROWS // chans
    shape = jax.ShapeDtypeStruct
    left_f, right_f, left_i, right_i = (jnp.asarray(table) for table in dft_tables())
    ids = subgrid_facet[:, 0]

    lines = (facets, SLOTS * 4, NV)
    patches, meta, model_rows = pl.pallas_call(
        functools.partial(grid_kernel, facets, side, subgrids),
        out_shape=(
            shape((facets * SLOTS * SUB, LANES), jnp.float32),
            shape((facets, 1, LANES), jnp.int32),
            shape((TILES, 2 * F_ROWS, LANES), jnp.float32),
        ),
        in_specs=[HBM] * 9,
        out_specs=(VMEM,) * 3,
        scratch_shapes=[
            pltpu.SMEM((subgrids,), jnp.int32),
            pltpu.SMEM((subgrids,), jnp.int32),
            pltpu.SMEM((subgrids,), jnp.int32),
            pltpu.SMEM((subgrids,), jnp.int32),
            pltpu.VMEM(visibility.shape, jnp.float32),
            pltpu.VMEM(uv_coords.shape, jnp.float32),
            pltpu.VMEM(left_f.shape, jnp.bfloat16),
            pltpu.VMEM(right_f.shape, jnp.bfloat16),
            pltpu.VMEM((TILES, F_ROWS, 2, LANES), jnp.bfloat16),
            pltpu.VMEM(lines, jnp.float32),
            pltpu.VMEM(lines, jnp.float32),
            pltpu.VMEM((facets, 1, LANES), jnp.int32),
            pltpu.SMEM((facets,), jnp.int32),
            pltpu.SMEM((facets,), jnp.int32),
            pltpu.SemaphoreType.DMA((8,)),
            pltpu.SemaphoreType.DMA((TILES,)),
            pltpu.SemaphoreType.DMA((facets,)),
            pltpu.SemaphoreType.DMA((facets,)),
            pltpu.SemaphoreType.DMA((facets,)),
            pltpu.SemaphoreType.DMA((facets,)),
            pltpu.SemaphoreType.DMA((2,)),
        ],
        compiler_params=pltpu.CompilerParams(
            collective_id=0, has_side_effects=True, vmem_limit_bytes=16 << 20
        ),
        name="grid_and_send",
    )(
        *(
            pltpu.with_memory_space_constraint(array, pltpu.HBM)
            for array in (
                vis_count, ids, row_offset, col_offset, visibility, uv_coords, model_facet,
                left_f, right_f,
            )
        )
    )

    canvas = pl.pallas_call(
        functools.partial(add_kernel, facets),
        out_shape=shape((2, TILES, F_ROWS, LANES), jnp.float32),
        in_specs=[SMEM, VMEM],
        out_specs=VMEM,
        compiler_params=pltpu.CompilerParams(vmem_limit_bytes=16 << 20),
        name="add_windows",
    )(meta, patches)

    depth = 2 * TILES * rows // PIECES
    links = 2 * PIECES * (chips // 2)
    total, residual = pl.pallas_call(
        functools.partial(exchange_kernel, facets, side, chans, subgrids),
        out_shape=(
            shape((2 * TILES * rows, LANES), jnp.float32),
            shape(visibility.shape, jnp.float32),
        ),
        in_specs=[SMEM] * 3 + [VMEM] * 6,
        out_specs=(VMEM,) * 2,
        scratch_shapes=[
            pltpu.VMEM((chips, 2 * TILES * rows, LANES), jnp.bfloat16),
            pltpu.VMEM((chips, 2 * TILES * rows, LANES), jnp.bfloat16),
            pltpu.VMEM((links, depth, LANES), jnp.bfloat16),
            pltpu.VMEM((links, depth, LANES), jnp.bfloat16),
            pltpu.VMEM((facets * SLOTS * SUB, LANES), jnp.bfloat16),
            pltpu.VMEM((facets, SLOTS, SUB, LANES), jnp.bfloat16),
            pltpu.VMEM((facets, SLOTS, SUB, LANES), jnp.bfloat16),
            pltpu.SMEM((2 * subgrids,), jnp.int32),
            pltpu.SemaphoreType.DMA((chips,)),
            pltpu.SemaphoreType.DMA((chips,)),
            pltpu.SemaphoreType.DMA((links,)),
            pltpu.SemaphoreType.DMA((links,)),
            pltpu.SemaphoreType.DMA((facets,)),
            pltpu.SemaphoreType.DMA((facets,)),
            pltpu.SemaphoreType.DMA,
        ],
        compiler_params=pltpu.CompilerParams(
            collective_id=1, has_side_effects=True, vmem_limit_bytes=20 << 20
        ),
        name="reduce_and_return",
    )(meta, vis_count, ids, canvas, model_rows, visibility, uv_coords, left_i, right_i)

    image = total.reshape(2, TILES, rows, LANES).transpose(2, 0, 1, 3).reshape(1, rows, 2, FACET)
    return image, residual


def solution(mesh):
    in_specs = (
        P(("facet", "chan"), None, None),
        P(("facet", "chan"), None, None),
        P(("facet", "chan")),
        P(("facet", "chan"), None),
        P(("facet", "chan")),
        P(("facet", "chan")),
        P("facet", None, None, None),
    )
    out_specs = (P("facet", "chan", None, None), P(("facet", "chan"), None, None))
    return jax.shard_map(
        per_device, mesh=mesh, in_specs=in_specs, out_specs=out_specs, check_vma=False
    )
```

```python
import functools
import math

import jax
import jax.numpy as jnp
import numpy as np
from jax import lax
from jax.experimental import pallas as pl
from jax.experimental.pallas import tpu as pltpu
from jax.sharding import PartitionSpec as P

SUB = 64
FACET = 4096
F_ROWS = 128
NV = 512
LANES = 128
TILES = FACET // LANES
SLOTS = 2


def dft_tables():
    line = np.arange(SUB)
    angle = 2.0 * math.pi * (line[:, None] * line[None, :] % SUB) / SUB
    cos_table = (np.cos(angle) / math.sqrt(SUB)).astype(jnp.bfloat16)
    sin_table = (-np.sin(angle) / math.sqrt(SUB)).astype(jnp.bfloat16)
    left_forward = np.concatenate([cos_table, sin_table], 1)
    left_inverse = np.concatenate([cos_table, -sin_table], 1)
    right_forward = np.concatenate(
        [np.concatenate([cos_table, sin_table], 1), np.concatenate([-sin_table, cos_table], 1)], 0
    )
    right_inverse = np.concatenate(
        [np.concatenate([cos_table, -sin_table], 1), np.concatenate([sin_table, cos_table], 1)], 0
    )
    return left_forward, right_forward, left_inverse, right_inverse


ROOT = math.sqrt(math.log2(math.e))


def scaled_square(coords):
    pixels = lax.broadcasted_iota(jnp.int32, (SUB, NV), 0).astype(jnp.float32) * ROOT
    delta = pixels - coords * ROOT
    return delta * delta


def kernel_of(coords):
    return jnp.exp2(-scaled_square(coords))


def kernel_low(coords):
    return jnp.exp2(-(scaled_square(coords).astype(jnp.bfloat16)))


def live_row(count):
    lane = lax.broadcasted_iota(jnp.int32, (1, NV), 1)
    return (lane < count).astype(jnp.float32)


def facet_order(side):
    steps = [(dx, dy) for dx in range(side) for dy in range(side)]
    return sorted(steps, key=lambda d: (sum(min(n, side - n) for n in d), d))


def facet_steps(me, side):
    x, y = me // side, lax.rem(me, side)
    targets, sources = [], []
    for dx, dy in facet_order(side)[1:]:
        targets.append(lax.rem(x + dx, side) * side + lax.rem(y + dy, side))
        sources.append(lax.rem(x + side - dx, side) * side + lax.rem(y + side - dy, side))
    return targets, sources


def swapped(values):
    half = values.shape[-1] // 2
    return jnp.concatenate([-values[:, half:], values[:, :half]], 1)


def left_pair(table, one, two):
    upper = jnp.concatenate([one, two], 1)
    lower = jnp.concatenate([swapped(one), swapped(two)], 1)
    out = jnp.dot(table, jnp.concatenate([upper, lower], 0), preferred_element_type=jnp.float32)
    return out.astype(jnp.bfloat16)


def gridded(lines):
    ku = kernel_low(lines[2:3])
    kv = kernel_low(lines[3:4])
    weighted = lines[0:2].astype(jnp.bfloat16)
    spread = jnp.concatenate([weighted[0:1] * kv, weighted[1:2] * kv], 0)
    return lax.dot_general(
        ku, spread, (((1,), (1,)), ((), ())), preferred_element_type=jnp.float32
    ).astype(jnp.bfloat16)


GROUP = 4


def grid_kernel(
    facets, side, subgrids,
    cnt_hbm, fid_hbm, row_hbm, col_hbm, vis_hbm, uv_hbm, model, left_hbm, right_hbm,
    patches, meta_in, model_rows, canvas,
    cnt, fid, row, col, vis, uv, left_f, right_f, raw, lines_send, lines_in, meta_send, first, last,
    in_sem, raw_sem, send_sem, recv_sem, meta_send_sem, meta_recv_sem, own_sem,
):
    me = lax.axis_index("facet")
    targets, _ = facet_steps(me, side)
    barrier = pltpu.get_barrier_semaphore()
    for peer in targets:
        pl.semaphore_signal(barrier, inc=1, device_id={"facet": peer})
    fetches = []
    for i, (src, dst) in enumerate((
        (fid_hbm, fid), (cnt_hbm, cnt), (row_hbm, row), (col_hbm, col), (vis_hbm, vis), (uv_hbm, uv),
        (left_hbm, left_f), (right_hbm, right_f),
    )):
        fetch = pltpu.make_async_copy(src, dst, in_sem.at[i])
        fetch.start()
        fetches.append(fetch)

    def model_copy(tile):
        at = pl.ds(pl.multiple_of(tile * LANES, LANES), LANES)
        return pltpu.make_async_copy(model.at[0, :, :, at], raw.at[tile], raw_sem.at[tile])

    def fetch_model(tile, carry):
        model_copy(tile).start()
        return carry

    lax.fori_loop(0, TILES, fetch_model, 0)
    for fetch in fetches:
        fetch.wait()

    ids = [fid[s] for s in range(subgrids)]

    def find(facet, carry):
        low = jnp.int32(subgrids)
        high = jnp.int32(-1)
        for s in range(subgrids):
            high = jnp.where(ids[s] == facet, s, high)
            back = subgrids - 1 - s
            low = jnp.where(ids[back] == facet, back, low)
        first[facet] = low
        last[facet] = high
        return carry

    lax.fori_loop(0, facets, find, 0)

    lane = lax.broadcasted_iota(jnp.int32, (1, LANES), 1)

    def pack(facet, carry):
        low, high = first[facet], last[facet]
        one = jnp.minimum(low, subgrids - 1)
        two = jnp.maximum(high, 0)
        lines_send[facet] = jnp.concatenate(
            [vis[one] * live_row(cnt[one]), uv[one], vis[two] * live_row(cnt[two]), uv[two]], 0
        )
        values = (
            (high >= 0).astype(jnp.int32), row[one], col[one],
            (high > low).astype(jnp.int32), row[two], col[two],
        )
        line = jnp.zeros((1, LANES), jnp.int32)
        for place, value in enumerate(values):
            line = jnp.where(lane == place, value, line)
        meta_send[facet] = line
        return carry

    lax.fori_loop(0, facets, pack, 0)

    pl.semaphore_wait(barrier, facets - 1)
    copies = [None] * facets
    metas = [None] * facets
    for step in range(facets - 1, 0, -1):
        for src, dst, ssem, rsem, started in (
            (meta_send, meta_in, meta_send_sem, meta_recv_sem, metas),
            (lines_send, lines_in, send_sem, recv_sem, copies),
        ):
            started[step] = pltpu.make_async_remote_copy(
                src_ref=src.at[targets[step - 1]], dst_ref=dst.at[step], send_sem=ssem.at[step],
                recv_sem=rsem.at[step], device_id={"facet": targets[step - 1]},
            )
            started[step].start()
    own = pltpu.make_async_copy(lines_send.at[me], lines_in.at[0], own_sem.at[0])
    own_meta = pltpu.make_async_copy(meta_send.at[me], meta_in.at[0], own_sem.at[1])
    own.start()
    own_meta.start()

    rows_view = raw.reshape(TILES, 2 * F_ROWS, LANES)

    def widen(tile, carry):
        model_copy(tile).wait()
        model_rows[tile] = rows_view[tile].astype(jnp.float32)
        canvas[0, tile] = zero
        canvas[1, tile] = zero
        return carry

    zero = jnp.zeros((F_ROWS, LANES), jnp.float32)
    lax.fori_loop(0, TILES, widen, 0)
    canvas[0, TILES] = zero
    canvas[1, TILES] = zero

    own.wait()
    own_meta.wait()
    for begin in range(0, facets, GROUP):
        halves = []
        for step in range(begin, begin + GROUP):
            if step > 0:
                copies[step].wait_recv()
        for step in range(begin, begin + GROUP):
            lines = lines_in[step]
            out = left_pair(left_f[...], gridded(lines[:4]), gridded(lines[4:]))
            halves += [out[:, :LANES], out[:, LANES:]]
        out = jnp.dot(
            jnp.concatenate(halves, 0), right_f[...], preferred_element_type=jnp.float32
        )
        patches[pl.ds(begin * SLOTS * SUB, GROUP * SLOTS * SUB), :] = out
    for copy in copies[1:]:
        copy.wait_send()
    for copy in metas[1:]:
        copy.wait()


def add_kernel(facets, meta, patches, _, canvas):
    lane = lax.broadcasted_iota(jnp.int32, (SUB, LANES), 1)

    def add(step, carry):
        for slot in range(SLOTS):
            valid = meta[step, 0, 3 * slot] > 0
            top = meta[step, 0, 3 * slot + 1]
            col = meta[step, 0, 3 * slot + 2]
            tile, shift = col // LANES, lax.rem(col, LANES)
            low = jnp.where(valid, shift, LANES)
            high = jnp.where(valid, shift - SUB, 0)
            patch = patches[pl.ds(pl.multiple_of((step * 2 + slot) * SUB, SUB), SUB), :]
            inside = (lane >= low) & (lane < shift + SUB)
            beyond = lane < high
            at = pl.ds(top, SUB)
            spots = [(part, tile + next_tile) for part in range(2) for next_tile in range(2)]
            before = [canvas[part, spot, at, :] for part, spot in spots]
            turned = (
                pltpu.roll(patch, shift, 1),
                pltpu.roll(patch, lax.rem(shift + SUB, LANES), 1),
            )
            for i, (part, spot) in enumerate(spots):
                canvas[part, spot, at, :] = before[i] + jnp.where(
                    beyond if i % 2 else inside, turned[part], 0.0
                )
        return carry

    lax.fori_loop(0, facets, add, 0, unroll=2)


PIECES = 4
PICKS = 2
DEGRIDS = 2
EARLY = 3


def exchange_kernel(
    facets, side, chans, subgrids,
    meta, cnt, fid, canvas, model_rows, vis, uv, left_i, right_i,
    total, residual,
    half_buf, pair_buf, send_buf, recv_buf, back, returned, place,
    pair_send, pair_recv, ring_send, ring_recv, back_send, back_recv, own_sem,
):
    chips = chans // 2
    me_f, me_c = lax.axis_index("facet"), lax.axis_index("chan")
    z, core = me_c // 2, lax.rem(me_c, 2)
    partner = z * 2 + 1 - core
    right = lax.rem(z + 1, chips) * 2 + core
    left = lax.rem(z + chips - 1, chips) * 2 + core
    targets, sources = facet_steps(me_f, side)
    rows = F_ROWS // chans
    barrier = pltpu.get_barrier_semaphore()
    for peer in (partner, right, left):
        pl.semaphore_signal(barrier, inc=1, device_id={"chan": peer})
    for peer in targets:
        pl.semaphore_signal(barrier, inc=1, device_id={"facet": peer})

    lane = lax.broadcasted_iota(jnp.int32, (SUB, LANES), 1)

    def picked(step, slot):
        top = meta[step, 0, 3 * slot + 1]
        col = meta[step, 0, 3 * slot + 2]
        tile, shift = col // LANES, lax.rem(col, LANES)
        after = jnp.minimum(tile + 1, TILES - 1)
        parts = [
            jnp.where(
                lane >= shift,
                model_rows[tile, pl.ds(2 * top + part, SUB, stride=2), :],
                model_rows[after, pl.ds(2 * top + part, SUB, stride=2), :],
            )
            for part in range(2)
        ]
        re = pltpu.roll(parts[0], lax.rem(LANES - shift, LANES), 1)
        im = pltpu.roll(parts[1], lax.rem(LANES + SUB - shift, LANES), 1)
        return jnp.where(lane < SUB, re, im).astype(jnp.bfloat16)

    def pick(begin):
        halves = []
        for step in range(begin, begin + PICKS):
            out = left_pair(left_i[...], picked(step, 0), picked(step, 1))
            halves += [out[:, :LANES], out[:, LANES:]]
        out = jnp.dot(
            jnp.concatenate(halves, 0), right_i[...], preferred_element_type=jnp.float32
        ).astype(jnp.bfloat16)
        for i in range(PICKS):
            for slot in range(SLOTS):
                at = (2 * i + slot) * SUB
                back[begin + i, slot] = out[at : at + SUB]

    half = chips // 2
    offsets = [half]
    for d in range(half - 1, 0, -1):
        offsets += [d, chips - d]
    offsets += [0]

    work = [functools.partial(pick, begin) for begin in range(facets - PICKS, -1, -PICKS)]

    def chan_rows(offset, which):
        there = lax.rem(z + offset, chips)
        return pl.ds(pl.multiple_of((2 * there + which) * rows, rows), rows)

    def narrow(pair, carry):
        for offset in range(chips):
            for part in range(2):
                both = canvas[part, pl.ds(2 * pair, 2), chan_rows(offset, 1 - core), :]
                at = pl.ds(pl.multiple_of((part * TILES + 2 * pair) * rows, 2 * rows), 2 * rows)
                half_buf[offset, at, :] = both.reshape(2 * rows, LANES).astype(jnp.bfloat16)
        return carry

    lax.fori_loop(0, TILES // 2, narrow, 0)
    for _ in range(EARLY):
        work.pop(0)()
    pl.semaphore_wait(barrier, 3 + facets - 1)

    pair_copy = {}
    for offset in offsets:
        copy = pltpu.make_async_remote_copy(
            src_ref=half_buf.at[offset], dst_ref=pair_buf.at[offset],
            send_sem=pair_send.at[offset], recv_sem=pair_recv.at[offset], device_id={"chan": partner},
        )
        copy.start()
        pair_copy[offset] = copy

    depth = half_buf.shape[1] // PIECES
    arrived = set()

    def mine(offset, piece):
        if offset not in arrived:
            arrived.add(offset)
            pair_copy[offset].wait_recv()
        at = pl.ds(piece * depth, depth)
        tiles = TILES * 2 // PIECES
        part, begin = divmod(piece * tiles, TILES)
        own = canvas[part, pl.ds(begin, tiles), chan_rows(offset, core), :]
        return own.reshape(depth, LANES) + pair_buf[offset, at, :].astype(jnp.float32)

    def length(piece, way):
        return half - (piece + way) % 2

    ring = {}

    def ring_step(step, every):
        done = 0
        for piece in range(PIECES):
            for way in range(2):
                count = length(piece, way)
                if step >= count:
                    continue
                distance = count - step
                offset = distance if way == 0 else chips - distance
                value = mine(offset % chips, piece)
                slot = (way * PIECES + piece) * half + step
                if step > 0:
                    ring[way, piece, step - 1].wait_recv()
                    value = value + recv_buf[slot - 1].astype(jnp.float32)
                send_buf[slot] = value.astype(jnp.bfloat16)
                copy = pltpu.make_async_remote_copy(
                    src_ref=send_buf.at[slot], dst_ref=recv_buf.at[slot],
                    send_sem=ring_send.at[slot], recv_sem=ring_recv.at[slot],
                    device_id={"chan": right if way == 0 else left},
                )
                copy.start()
                ring[way, piece, step] = copy
                done += 1
                if done % every == 0 and work:
                    work.pop(0)()

    def degrid(begin):
        for s in range(begin, begin + DEGRIDS):
            image = returned[place[s], place[subgrids + s]]
            ku = kernel_low(uv[s, pl.ds(0, 1), :])
            weight = kernel_of(uv[s, pl.ds(1, 1), :])
            inner = lax.dot_general(
                image, ku, (((0,), (0,)), ((), ())), preferred_element_type=jnp.float32
            )
            live = live_row(cnt[s])
            for part in range(2):
                predicted = jnp.sum(inner[part * SUB : (part + 1) * SUB] * weight, 0, keepdims=True)
                residual[s, pl.ds(part, 1), :] = (vis[s, pl.ds(part, 1), :] - predicted) * live

    back_copy = []

    def send_back():
        for step in range(facets - 1, 0, -1):
            copy = pltpu.make_async_remote_copy(
                src_ref=back.at[step], dst_ref=returned.at[step],
                send_sem=back_send.at[step], recv_sem=back_recv.at[step],
                device_id={"facet": sources[step - 1]},
            )
            copy.start()
            back_copy.append(copy)
        own = pltpu.make_async_copy(back.at[0], returned.at[0], own_sem)
        own.start()
        back_copy.append(own)

    def locate():
        ids = [fid[s] for s in range(subgrids)]
        x, y = me_f // side, lax.rem(me_f, side)
        codes = []
        for s in range(subgrids):
            before = jnp.int32(0)
            for other in range(s):
                before = jnp.where(ids[other] == ids[s], 1, before)
            there_x, there_y = ids[s] // side, lax.rem(ids[s], side)
            code = lax.rem(there_x + side - x, side) * side + lax.rem(there_y + side - y, side)
            where = jnp.int32(0)
            for step, known in enumerate(facet_order(side)):
                where = jnp.where(code == known[0] * side + known[1], step, where)
            place[s] = where
            place[subgrids + s] = before

    work += [send_back, locate]
    ring_step(0, 1)
    while work:
        work.pop(0)()
    ring_step(1, 1)
    ring_step(2, 1)
    for copy in back_copy:
        copy.wait()
    work += [functools.partial(degrid, s) for s in range(0, subgrids, DEGRIDS)]
    ring_step(half - 1, 1)
    for piece in range(PIECES):
        if work:
            work.pop(0)()
        value = mine(0, piece)
        for way in range(2):
            step = length(piece, way) - 1
            ring[way, piece, step].wait_recv()
            value = value + recv_buf[(way * PIECES + piece) * half + step].astype(jnp.float32)
        total[pl.ds(piece * depth, depth), :] = value
    while work:
        work.pop(0)()
    for copy in pair_copy.values():
        copy.wait_send()
    for copy in ring.values():
        copy.wait_send()


VMEM = pl.BlockSpec(memory_space=pltpu.VMEM)
SMEM = pl.BlockSpec(memory_space=pltpu.SMEM)
HBM = pl.BlockSpec(memory_space=pltpu.HBM)


def per_device(
    visibility, uv_coords, vis_count, subgrid_facet, row_offset, col_offset, model_facet
):
    facets, chans = lax.axis_size("facet"), lax.axis_size("chan")
    side = math.isqrt(facets)
    chips = chans // 2
    subgrids = visibility.shape[0]
    rows = F_ROWS // chans
    shape = jax.ShapeDtypeStruct
    left_f, right_f, left_i, right_i = (jnp.asarray(table) for table in dft_tables())
    ids = subgrid_facet[:, 0]

    lines = (facets, SLOTS * 4, NV)
    patches, meta, model_rows, zeros = pl.pallas_call(
        functools.partial(grid_kernel, facets, side, subgrids),
        out_shape=(
            shape((facets * SLOTS * SUB, LANES), jnp.float32),
            shape((facets, 1, LANES), jnp.int32),
            shape((TILES, 2 * F_ROWS, LANES), jnp.float32),
            shape((2, TILES + 1, F_ROWS, LANES), jnp.float32),
        ),
        in_specs=[HBM] * 9,
        out_specs=(VMEM,) * 4,
        scratch_shapes=[
            pltpu.SMEM((subgrids,), jnp.int32),
            pltpu.SMEM((subgrids,), jnp.int32),
            pltpu.SMEM((subgrids,), jnp.int32),
            pltpu.SMEM((subgrids,), jnp.int32),
            pltpu.VMEM(visibility.shape, jnp.float32),
            pltpu.VMEM(uv_coords.shape, jnp.float32),
            pltpu.VMEM(left_f.shape, jnp.bfloat16),
            pltpu.VMEM(right_f.shape, jnp.bfloat16),
            pltpu.VMEM((TILES, F_ROWS, 2, LANES), jnp.bfloat16),
            pltpu.VMEM(lines, jnp.float32),
            pltpu.VMEM(lines, jnp.float32),
            pltpu.VMEM((facets, 1, LANES), jnp.int32),
            pltpu.SMEM((facets,), jnp.int32),
            pltpu.SMEM((facets,), jnp.int32),
            pltpu.SemaphoreType.DMA((8,)),
            pltpu.SemaphoreType.DMA((TILES,)),
            pltpu.SemaphoreType.DMA((facets,)),
            pltpu.SemaphoreType.DMA((facets,)),
            pltpu.SemaphoreType.DMA((facets,)),
            pltpu.SemaphoreType.DMA((facets,)),
            pltpu.SemaphoreType.DMA((2,)),
        ],
        compiler_params=pltpu.CompilerParams(
            collective_id=0, has_side_effects=True, vmem_limit_bytes=16 << 20
        ),
        name="grid_and_send",
    )(
        *(
            pltpu.with_memory_space_constraint(array, pltpu.HBM)
            for array in (
                vis_count, ids, row_offset, col_offset, visibility, uv_coords, model_facet,
                left_f, right_f,
            )
        )
    )

    canvas = pl.pallas_call(
        functools.partial(add_kernel, facets),
        out_shape=shape((2, TILES + 1, F_ROWS, LANES), jnp.float32),
        in_specs=[SMEM, VMEM, VMEM],
        out_specs=VMEM,
        input_output_aliases={2: 0},
        compiler_params=pltpu.CompilerParams(vmem_limit_bytes=16 << 20),
        name="add_windows",
    )(meta, patches, zeros)

    depth = 2 * TILES * rows // PIECES
    links = 2 * PIECES * (chips // 2)
    total, residual = pl.pallas_call(
        functools.partial(exchange_kernel, facets, side, chans, subgrids),
        out_shape=(
            shape((2 * TILES * rows, LANES), jnp.float32),
            shape(visibility.shape, jnp.float32),
        ),
        in_specs=[SMEM] * 3 + [VMEM] * 6,
        out_specs=(VMEM,) * 2,
        scratch_shapes=[
            pltpu.VMEM((chips, 2 * TILES * rows, LANES), jnp.bfloat16),
            pltpu.VMEM((chips, 2 * TILES * rows, LANES), jnp.bfloat16),
            pltpu.VMEM((links, depth, LANES), jnp.bfloat16),
            pltpu.VMEM((links, depth, LANES), jnp.bfloat16),
            pltpu.VMEM((facets, SLOTS, SUB, LANES), jnp.bfloat16),
            pltpu.VMEM((facets, SLOTS, SUB, LANES), jnp.bfloat16),
            pltpu.SMEM((2 * subgrids,), jnp.int32),
            pltpu.SemaphoreType.DMA((chips,)),
            pltpu.SemaphoreType.DMA((chips,)),
            pltpu.SemaphoreType.DMA((links,)),
            pltpu.SemaphoreType.DMA((links,)),
            pltpu.SemaphoreType.DMA((facets,)),
            pltpu.SemaphoreType.DMA((facets,)),
            pltpu.SemaphoreType.DMA,
        ],
        compiler_params=pltpu.CompilerParams(
            collective_id=1, has_side_effects=True, vmem_limit_bytes=20 << 20
        ),
        name="reduce_and_return",
    )(meta, vis_count, ids, canvas, model_rows, visibility, uv_coords, left_i, right_i)

    image = total.reshape(2, TILES, rows, LANES).transpose(2, 0, 1, 3).reshape(1, rows, 2, FACET)
    return image, residual


def solution(mesh):
    in_specs = (
        P(("facet", "chan"), None, None),
        P(("facet", "chan"), None, None),
        P(("facet", "chan")),
        P(("facet", "chan"), None),
        P(("facet", "chan")),
        P(("facet", "chan")),
        P("facet", None, None, None),
    )
    out_specs = (P("facet", "chan", None, None), P(("facet", "chan"), None, None))
    return jax.shard_map(
        per_device, mesh=mesh, in_specs=in_specs, out_specs=out_specs, check_vma=False
    )
```

```python
import functools
import itertools
import math

import jax
import jax.numpy as jnp
import numpy as np
from jax import lax
from jax.experimental import pallas as pl
from jax.experimental.pallas import tpu as pltpu
from jax.sharding import PartitionSpec as P

SUB = 64
FACET = 4096
F_ROWS = 128
NV = 512
LANES = 128
TILES = FACET // LANES
SLOTS = 2


def dft_tables():
    line = np.arange(SUB)
    angle = 2.0 * math.pi * (line[:, None] * line[None, :] % SUB) / SUB
    cos_table = (np.cos(angle) / math.sqrt(SUB)).astype(jnp.bfloat16)
    sin_table = (-np.sin(angle) / math.sqrt(SUB)).astype(jnp.bfloat16)
    left_forward = np.concatenate([cos_table, sin_table], 1)
    left_inverse = np.concatenate([cos_table, -sin_table], 1)
    right_forward = np.concatenate(
        [np.concatenate([cos_table, sin_table], 1), np.concatenate([-sin_table, cos_table], 1)], 0
    )
    right_inverse = np.concatenate(
        [np.concatenate([cos_table, -sin_table], 1), np.concatenate([sin_table, cos_table], 1)], 0
    )
    return left_forward, right_forward, left_inverse, right_inverse


ROOT = math.sqrt(math.log2(math.e))


def scaled_square(coords):
    pixels = lax.broadcasted_iota(jnp.int32, (SUB, NV), 0).astype(jnp.float32) * ROOT
    delta = pixels - coords * ROOT
    return delta * delta


def kernel_of(coords):
    return jnp.exp2(-scaled_square(coords))


def kernel_low(coords):
    return kernel_of(coords).astype(jnp.bfloat16)


def live_row(count):
    lane = lax.broadcasted_iota(jnp.int32, (1, NV), 1)
    return (lane < count).astype(jnp.float32)


def facet_order(side):
    steps = [(dx, dy) for dx in range(side) for dy in range(side)]
    return sorted(steps, key=lambda d: (sum(min(n, side - n) for n in d), d))


def facet_steps(me, side):
    x, y = me // side, lax.rem(me, side)
    targets, sources = [], []
    for dx, dy in facet_order(side)[1:]:
        targets.append(lax.rem(x + dx, side) * side + lax.rem(y + dy, side))
        sources.append(lax.rem(x + side - dx, side) * side + lax.rem(y + side - dy, side))
    return targets, sources


def swapped(values):
    half = values.shape[-1] // 2
    return jnp.concatenate([-values[:, half:], values[:, :half]], 1)


def left_pair(table, one, two):
    upper = jnp.concatenate([one, two], 1)
    lower = jnp.concatenate([swapped(one), swapped(two)], 1)
    out = jnp.dot(table, jnp.concatenate([upper, lower], 0), preferred_element_type=jnp.float32)
    return out.astype(jnp.bfloat16)


def gridded(coords, weighted):
    ku = kernel_low(coords[0:1])
    kv = kernel_low(coords[1:2])
    spread = jnp.concatenate([weighted[0:1] * kv, weighted[1:2] * kv], 0)
    return lax.dot_general(
        ku, spread, (((1,), (1,)), ((), ())), preferred_element_type=jnp.float32
    ).astype(jnp.bfloat16)


SIZES = (6, 6, 4)


def grid_kernel(
    facets, side, subgrids,
    cnt_hbm, fid_hbm, row_hbm, col_hbm, vis_hbm, uv_hbm, model, left_hbm, right_hbm,
    patches, meta_in, model_rows, canvas,
    cnt, fid, row, col, vis, uv, left_f, right_f, raw, vis_send, vis_in, uv_send, uv_in, meta_send,
    grids, halves, first, last,
    in_sem, raw_sem, send_sem, recv_sem, own_sem,
):
    me = lax.axis_index("facet")
    targets, _ = facet_steps(me, side)
    barrier = pltpu.get_barrier_semaphore()
    for peer in targets:
        pl.semaphore_signal(barrier, inc=1, device_id={"facet": peer})
    fetches = []
    for i, (src, dst) in enumerate((
        (fid_hbm, fid), (cnt_hbm, cnt), (row_hbm, row), (col_hbm, col), (vis_hbm, vis), (uv_hbm, uv),
        (left_hbm, left_f), (right_hbm, right_f),
    )):
        fetch = pltpu.make_async_copy(src, dst, in_sem.at[i])
        fetch.start()
        fetches.append(fetch)

    def model_copy(tile):
        at = pl.ds(pl.multiple_of(tile * LANES, LANES), LANES)
        return pltpu.make_async_copy(model.at[0, :, :, at], raw.at[tile], raw_sem.at[tile])

    def fetch_model(tile, carry):
        model_copy(tile).start()
        return carry

    lax.fori_loop(0, TILES, fetch_model, 0)
    for fetch in fetches:
        fetch.wait()

    ids = [fid[s] for s in range(subgrids)]

    def find(facet, carry):
        low = jnp.int32(subgrids)
        high = jnp.int32(-1)
        for s in range(subgrids):
            high = jnp.where(ids[s] == facet, s, high)
            back = subgrids - 1 - s
            low = jnp.where(ids[back] == facet, back, low)
        first[facet] = low
        last[facet] = high
        return carry

    lax.fori_loop(0, facets, find, 0)

    lane = lax.broadcasted_iota(jnp.int32, (1, LANES), 1)

    def pack(facet, carry):
        low, high = first[facet], last[facet]
        one = jnp.minimum(low, subgrids - 1)
        two = jnp.maximum(high, 0)
        weighted = [vis[s] * live_row(cnt[s]) for s in (one, two)]
        vis_send[facet] = jnp.concatenate(weighted, 0).astype(jnp.bfloat16)
        uv_send[facet] = jnp.concatenate([uv[one], uv[two]], 0)
        values = (
            (high >= 0).astype(jnp.int32), row[one], col[one],
            (high > low).astype(jnp.int32), row[two], col[two],
        )
        line = jnp.zeros((1, LANES), jnp.int32)
        for place, value in enumerate(values):
            line = jnp.where(lane == place, value, line)
        meta_send[facet] = line
        return carry

    lax.fori_loop(0, facets, pack, 0)

    pl.semaphore_wait(barrier, facets - 1)
    moved = ((meta_send, meta_in), (vis_send, vis_in), (uv_send, uv_in))
    copies = [[] for _ in range(facets)]
    for step in range(facets - 1, -1, -1):
        for i, (src, dst) in enumerate(moved):
            if step > 0:
                copy = pltpu.make_async_remote_copy(
                    src_ref=src.at[targets[step - 1]], dst_ref=dst.at[step],
                    send_sem=send_sem.at[i, step], recv_sem=recv_sem.at[i, step],
                    device_id={"facet": targets[step - 1]},
                )
            else:
                copy = pltpu.make_async_copy(src.at[me], dst.at[0], own_sem.at[i])
            copy.start()
            copies[step].append(copy)

    rows_view = raw.reshape(TILES, 2 * F_ROWS, LANES)

    def widen(tile, carry):
        model_copy(tile).wait()
        model_rows[tile] = rows_view[tile].astype(jnp.float32)
        canvas[0, tile] = zero
        canvas[1, tile] = zero
        return carry

    zero = jnp.zeros((F_ROWS, LANES), jnp.float32)
    lax.fori_loop(0, TILES, widen, 0)
    canvas[0, TILES] = zero
    canvas[1, TILES] = zero

    def grid_one(step):
        for slot in range(SLOTS):
            at = pl.ds(2 * slot, 2)
            grids[SLOTS * step + slot] = gridded(uv_in[step, at, :], vis_in[step, at, :])

    def left_one(step):
        out = left_pair(left_f[...], grids[SLOTS * step], grids[SLOTS * step + 1])
        halves[SLOTS * step] = out[:, :LANES]
        halves[SLOTS * step + 1] = out[:, LANES:]

    def right_one(step):
        both = halves[pl.ds(SLOTS * step, SLOTS)].reshape(SLOTS * SUB, LANES)
        patches[pl.ds(SLOTS * SUB * step, SLOTS * SUB), :] = jnp.dot(
            both, right_f[...], preferred_element_type=jnp.float32
        )

    begins = [0]
    for size in SIZES:
        begins.append(begins[-1] + size)
    groups = [range(a, b) for a, b in zip(begins, begins[1:])]
    stages = (grid_one, left_one, right_one)
    for turn in range(len(groups) + len(stages) - 1):
        if turn < len(groups):
            for step in groups[turn]:
                for copy in copies[step]:
                    copy.wait_recv() if step > 0 else copy.wait()
        now = []
        for lag, stage in enumerate(stages):
            if 0 <= turn - lag < len(groups):
                now.append([functools.partial(stage, step) for step in groups[turn - lag]])
        for parts in itertools.zip_longest(*now):
            for part in reversed(parts):
                if part is not None:
                    part()
    for step in range(1, facets):
        for copy in copies[step]:
            copy.wait_send()


def add_kernel(facets, meta, patches, _, canvas):
    lane = lax.broadcasted_iota(jnp.int32, (SUB, LANES), 1)

    def add(step, carry):
        for slot in range(SLOTS):
            valid = meta[step, 0, 3 * slot] > 0
            top = meta[step, 0, 3 * slot + 1]
            col = meta[step, 0, 3 * slot + 2]
            tile, shift = col // LANES, lax.rem(col, LANES)
            low = jnp.where(valid, shift, LANES)
            high = jnp.where(valid, shift - SUB, 0)
            patch = patches[pl.ds(pl.multiple_of((step * 2 + slot) * SUB, SUB), SUB), :]
            inside = (lane >= low) & (lane < shift + SUB)
            beyond = lane < high
            at = pl.ds(top, SUB)
            spots = [(part, tile + next_tile) for part in range(2) for next_tile in range(2)]
            before = [canvas[part, spot, at, :] for part, spot in spots]
            turned = (
                pltpu.roll(patch, shift, 1),
                pltpu.roll(patch, lax.rem(shift + SUB, LANES), 1),
            )
            for i, (part, spot) in enumerate(spots):
                canvas[part, spot, at, :] = before[i] + jnp.where(
                    beyond if i % 2 else inside, turned[part], 0.0
                )
        return carry

    lax.fori_loop(0, facets, add, 0, unroll=2)


PIECES = 4
PICKS = 2
DEGRIDS = 4
EARLY = 8


def exchange_kernel(
    facets, side, chans, subgrids,
    meta, cnt, fid, canvas, model_rows, vis, uv, left_i, right_i,
    total, residual,
    half_buf, pair_buf, send_buf, recv_buf, back, returned, place,
    pair_send, pair_recv, ring_send, ring_recv, back_send, back_recv, own_sem,
):
    chips = chans // 2
    me_f, me_c = lax.axis_index("facet"), lax.axis_index("chan")
    z, core = me_c // 2, lax.rem(me_c, 2)
    partner = z * 2 + 1 - core
    right = lax.rem(z + 1, chips) * 2 + core
    left = lax.rem(z + chips - 1, chips) * 2 + core
    targets, sources = facet_steps(me_f, side)
    rows = F_ROWS // chans
    barrier = pltpu.get_barrier_semaphore()
    for peer in (partner, right, left):
        pl.semaphore_signal(barrier, inc=1, device_id={"chan": peer})
    for peer in targets:
        pl.semaphore_signal(barrier, inc=1, device_id={"facet": peer})

    lane = lax.broadcasted_iota(jnp.int32, (SUB, LANES), 1)

    def picked(step, slot):
        top = meta[step, 0, 3 * slot + 1]
        col = meta[step, 0, 3 * slot + 2]
        tile, shift = col // LANES, lax.rem(col, LANES)
        after = jnp.minimum(tile + 1, TILES - 1)
        parts = [
            jnp.where(
                lane >= shift,
                model_rows[tile, pl.ds(2 * top + part, SUB, stride=2), :],
                model_rows[after, pl.ds(2 * top + part, SUB, stride=2), :],
            )
            for part in range(2)
        ]
        re = pltpu.roll(parts[0], lax.rem(LANES - shift, LANES), 1)
        im = pltpu.roll(parts[1], lax.rem(LANES + SUB - shift, LANES), 1)
        return jnp.where(lane < SUB, re, im).astype(jnp.bfloat16)

    def pick(begin):
        halves = []
        for step in range(begin, begin + PICKS):
            out = left_pair(left_i[...], picked(step, 0), picked(step, 1))
            halves += [out[:, :LANES], out[:, LANES:]]
        out = jnp.dot(
            jnp.concatenate(halves, 0), right_i[...], preferred_element_type=jnp.float32
        ).astype(jnp.bfloat16)
        for i in range(PICKS):
            for slot in range(SLOTS):
                at = (2 * i + slot) * SUB
                back[begin + i, slot] = out[at : at + SUB]

    half = chips // 2
    offsets = [half]
    for d in range(half - 1, 0, -1):
        offsets += [d, chips - d]
    offsets += [0]

    work = [functools.partial(pick, begin) for begin in range(facets - PICKS, -1, -PICKS)]

    def chan_rows(offset, which):
        there = lax.rem(z + offset, chips)
        return pl.ds(pl.multiple_of((2 * there + which) * rows, rows), rows)

    def narrow(pair, carry):
        for offset in range(chips):
            for part in range(2):
                both = canvas[part, pl.ds(2 * pair, 2), chan_rows(offset, 1 - core), :]
                at = pl.ds(pl.multiple_of((part * TILES + 2 * pair) * rows, 2 * rows), 2 * rows)
                half_buf[offset, at, :] = both.reshape(2 * rows, LANES).astype(jnp.bfloat16)
        return carry

    lax.fori_loop(0, TILES // 2, narrow, 0)
    for _ in range(EARLY):
        work.pop(0)()
    pl.semaphore_wait(barrier, 3 + facets - 1)

    pair_copy = {}
    for offset in offsets:
        copy = pltpu.make_async_remote_copy(
            src_ref=half_buf.at[offset], dst_ref=pair_buf.at[offset],
            send_sem=pair_send.at[offset], recv_sem=pair_recv.at[offset], device_id={"chan": partner},
        )
        copy.start()
        pair_copy[offset] = copy

    depth = half_buf.shape[1] // PIECES
    arrived = set()

    def mine(offset, piece):
        if offset not in arrived:
            arrived.add(offset)
            pair_copy[offset].wait_recv()
        at = pl.ds(piece * depth, depth)
        tiles = TILES * 2 // PIECES
        part, begin = divmod(piece * tiles, TILES)
        own = canvas[part, pl.ds(begin, tiles), chan_rows(offset, core), :]
        return own.reshape(depth, LANES) + pair_buf[offset, at, :].astype(jnp.float32)

    def length(piece, way):
        return half - (piece + way) % 2

    ring = {}

    def ring_step(step, every):
        done = 0
        for piece in range(PIECES):
            for way in range(2):
                count = length(piece, way)
                if step >= count:
                    continue
                distance = count - step
                offset = distance if way == 0 else chips - distance
                value = mine(offset % chips, piece)
                slot = (way * PIECES + piece) * half + step
                if step > 0:
                    ring[way, piece, step - 1].wait_recv()
                    value = value + recv_buf[slot - 1].astype(jnp.float32)
                send_buf[slot] = value.astype(jnp.bfloat16)
                copy = pltpu.make_async_remote_copy(
                    src_ref=send_buf.at[slot], dst_ref=recv_buf.at[slot],
                    send_sem=ring_send.at[slot], recv_sem=ring_recv.at[slot],
                    device_id={"chan": right if way == 0 else left},
                )
                copy.start()
                ring[way, piece, step] = copy
                done += 1
                if done % every == 0 and work:
                    work.pop(0)()

    def degrid(begin):
        for s in range(begin, begin + DEGRIDS):
            image = returned[place[s], place[subgrids + s]]
            ku = kernel_low(uv[s, pl.ds(0, 1), :])
            weight = kernel_of(uv[s, pl.ds(1, 1), :])
            inner = lax.dot_general(
                image, ku, (((0,), (0,)), ((), ())), preferred_element_type=jnp.float32
            )
            live = live_row(cnt[s])
            for part in range(2):
                predicted = jnp.sum(inner[part * SUB : (part + 1) * SUB] * weight, 0, keepdims=True)
                residual[s, pl.ds(part, 1), :] = (vis[s, pl.ds(part, 1), :] - predicted) * live

    back_copy = []

    def send_back():
        for step in range(facets - 1, 0, -1):
            copy = pltpu.make_async_remote_copy(
                src_ref=back.at[step], dst_ref=returned.at[step],
                send_sem=back_send.at[step], recv_sem=back_recv.at[step],
                device_id={"facet": sources[step - 1]},
            )
            copy.start()
            back_copy.append(copy)
        own = pltpu.make_async_copy(back.at[0], returned.at[0], own_sem)
        own.start()
        back_copy.append(own)

    def locate():
        ids = [fid[s] for s in range(subgrids)]
        x, y = me_f // side, lax.rem(me_f, side)
        codes = []
        for s in range(subgrids):
            before = jnp.int32(0)
            for other in range(s):
                before = jnp.where(ids[other] == ids[s], 1, before)
            there_x, there_y = ids[s] // side, lax.rem(ids[s], side)
            code = lax.rem(there_x + side - x, side) * side + lax.rem(there_y + side - y, side)
            where = jnp.int32(0)
            for step, known in enumerate(facet_order(side)):
                where = jnp.where(code == known[0] * side + known[1], step, where)
            place[s] = where
            place[subgrids + s] = before

    work += [send_back, locate]
    ring_step(0, 1)
    while work:
        work.pop(0)()
    ring_step(1, 1)
    ring_step(2, 1)
    for copy in back_copy:
        copy.wait()
    work += [functools.partial(degrid, s) for s in range(0, subgrids, DEGRIDS)]
    ring_step(half - 1, 1)
    for piece in range(PIECES):
        if work:
            work.pop(0)()
        value = mine(0, piece)
        for way in range(2):
            step = length(piece, way) - 1
            ring[way, piece, step].wait_recv()
            value = value + recv_buf[(way * PIECES + piece) * half + step].astype(jnp.float32)
        total[pl.ds(piece * depth, depth), :] = value
    while work:
        work.pop(0)()
    for copy in pair_copy.values():
        copy.wait_send()
    for copy in ring.values():
        copy.wait_send()


def output_kernel(rows, total, values, image, residual):
    def place(tile, carry):
        at = pl.ds(pl.multiple_of(tile * LANES, LANES), LANES)
        for part in range(2):
            begin = pl.multiple_of((part * TILES + tile) * rows, rows)
            image[0, :, part, at] = total[pl.ds(begin, rows), :]
        return carry

    lax.fori_loop(0, TILES, place, 0, unroll=4)
    residual[...] = values[...]


VMEM = pl.BlockSpec(memory_space=pltpu.VMEM)
SMEM = pl.BlockSpec(memory_space=pltpu.SMEM)
HBM = pl.BlockSpec(memory_space=pltpu.HBM)


def per_device(
    visibility, uv_coords, vis_count, subgrid_facet, row_offset, col_offset, model_facet
):
    facets, chans = lax.axis_size("facet"), lax.axis_size("chan")
    side = math.isqrt(facets)
    chips = chans // 2
    subgrids = visibility.shape[0]
    rows = F_ROWS // chans
    shape = jax.ShapeDtypeStruct
    left_f, right_f, left_i, right_i = (jnp.asarray(table) for table in dft_tables())
    ids = subgrid_facet[:, 0]

    patches, meta, model_rows, zeros = pl.pallas_call(
        functools.partial(grid_kernel, facets, side, subgrids),
        out_shape=(
            shape((facets * SLOTS * SUB, LANES), jnp.float32),
            shape((facets, 1, LANES), jnp.int32),
            shape((TILES, 2 * F_ROWS, LANES), jnp.float32),
            shape((2, TILES + 1, F_ROWS, LANES), jnp.float32),
        ),
        in_specs=[HBM] * 9,
        out_specs=(VMEM,) * 4,
        scratch_shapes=[
            pltpu.SMEM((subgrids,), jnp.int32),
            pltpu.SMEM((subgrids,), jnp.int32),
            pltpu.SMEM((subgrids,), jnp.int32),
            pltpu.SMEM((subgrids,), jnp.int32),
            pltpu.VMEM(visibility.shape, jnp.float32),
            pltpu.VMEM(uv_coords.shape, jnp.float32),
            pltpu.VMEM(left_f.shape, jnp.bfloat16),
            pltpu.VMEM(right_f.shape, jnp.bfloat16),
            pltpu.VMEM((TILES, F_ROWS, 2, LANES), jnp.bfloat16),
            pltpu.VMEM((facets, 2 * SLOTS, NV), jnp.bfloat16),
            pltpu.VMEM((facets, 2 * SLOTS, NV), jnp.bfloat16),
            pltpu.VMEM((facets, 2 * SLOTS, NV), jnp.float32),
            pltpu.VMEM((facets, 2 * SLOTS, NV), jnp.float32),
            pltpu.VMEM((facets, 1, LANES), jnp.int32),
            pltpu.VMEM((facets * SLOTS, SUB, LANES), jnp.bfloat16),
            pltpu.VMEM((facets * SLOTS, SUB, LANES), jnp.bfloat16),
            pltpu.SMEM((facets,), jnp.int32),
            pltpu.SMEM((facets,), jnp.int32),
            pltpu.SemaphoreType.DMA((8,)),
            pltpu.SemaphoreType.DMA((TILES,)),
            pltpu.SemaphoreType.DMA((3, facets)),
            pltpu.SemaphoreType.DMA((3, facets)),
            pltpu.SemaphoreType.DMA((3,)),
        ],
        compiler_params=pltpu.CompilerParams(
            collective_id=0, has_side_effects=True, vmem_limit_bytes=16 << 20
        ),
        name="grid_and_send",
    )(
        *(
            pltpu.with_memory_space_constraint(array, pltpu.HBM)
            for array in (
                vis_count, ids, row_offset, col_offset, visibility, uv_coords, model_facet,
                left_f, right_f,
            )
        )
    )

    canvas = pl.pallas_call(
        functools.partial(add_kernel, facets),
        out_shape=shape((2, TILES + 1, F_ROWS, LANES), jnp.float32),
        in_specs=[SMEM, VMEM, VMEM],
        out_specs=VMEM,
        input_output_aliases={2: 0},
        compiler_params=pltpu.CompilerParams(vmem_limit_bytes=16 << 20),
        name="add_windows",
    )(meta, patches, zeros)

    depth = 2 * TILES * rows // PIECES
    links = 2 * PIECES * (chips // 2)
    total, residual = pl.pallas_call(
        functools.partial(exchange_kernel, facets, side, chans, subgrids),
        out_shape=(
            shape((2 * TILES * rows, LANES), jnp.float32),
            shape(visibility.shape, jnp.float32),
        ),
        in_specs=[SMEM] * 3 + [VMEM] * 6,
        out_specs=(VMEM,) * 2,
        scratch_shapes=[
            pltpu.VMEM((chips, 2 * TILES * rows, LANES), jnp.bfloat16),
            pltpu.VMEM((chips, 2 * TILES * rows, LANES), jnp.bfloat16),
            pltpu.VMEM((links, depth, LANES), jnp.bfloat16),
            pltpu.VMEM((links, depth, LANES), jnp.bfloat16),
            pltpu.VMEM((facets, SLOTS, SUB, LANES), jnp.bfloat16),
            pltpu.VMEM((facets, SLOTS, SUB, LANES), jnp.bfloat16),
            pltpu.SMEM((2 * subgrids,), jnp.int32),
            pltpu.SemaphoreType.DMA((chips,)),
            pltpu.SemaphoreType.DMA((chips,)),
            pltpu.SemaphoreType.DMA((links,)),
            pltpu.SemaphoreType.DMA((links,)),
            pltpu.SemaphoreType.DMA((facets,)),
            pltpu.SemaphoreType.DMA((facets,)),
            pltpu.SemaphoreType.DMA,
        ],
        compiler_params=pltpu.CompilerParams(
            collective_id=1, has_side_effects=True, vmem_limit_bytes=20 << 20
        ),
        name="reduce_and_return",
    )(meta, vis_count, ids, canvas, model_rows, visibility, uv_coords, left_i, right_i)

    image, residual = pl.pallas_call(
        functools.partial(output_kernel, rows),
        out_shape=(
            shape((1, rows, 2, FACET), jnp.float32),
            shape(visibility.shape, jnp.float32),
        ),
        in_specs=[VMEM] * 2,
        out_specs=(VMEM,) * 2,
        compiler_params=pltpu.CompilerParams(vmem_limit_bytes=8 << 20),
        name="outputs",
    )(total, residual)
    return image, residual


def solution(mesh):
    in_specs = (
        P(("facet", "chan"), None, None),
        P(("facet", "chan"), None, None),
        P(("facet", "chan")),
        P(("facet", "chan"), None),
        P(("facet", "chan")),
        P(("facet", "chan")),
        P("facet", None, None, None),
    )
    out_specs = (P("facet", "chan", None, None), P(("facet", "chan"), None, None))
    return jax.shard_map(
        per_device, mesh=mesh, in_specs=in_specs, out_specs=out_specs, check_vma=False
    )
```

```python
import functools
import itertools
import math

import jax
import jax.numpy as jnp
import numpy as np
from jax import lax
from jax.experimental import pallas as pl
from jax.experimental.pallas import tpu as pltpu
from jax.sharding import PartitionSpec as P

SUB = 64
FACET = 4096
F_ROWS = 128
NV = 512
LANES = 128
TILES = FACET // LANES
SLOTS = 2


def dft_tables():
    line = np.arange(SUB)
    angle = 2.0 * math.pi * (line[:, None] * line[None, :] % SUB) / SUB
    cos_table = (np.cos(angle) / math.sqrt(SUB)).astype(jnp.bfloat16)
    sin_table = (-np.sin(angle) / math.sqrt(SUB)).astype(jnp.bfloat16)
    left_forward = np.concatenate([cos_table, sin_table], 1)
    left_inverse = np.concatenate([cos_table, -sin_table], 1)
    right_forward = np.concatenate(
        [np.concatenate([cos_table, sin_table], 1), np.concatenate([-sin_table, cos_table], 1)], 0
    )
    right_inverse = np.concatenate(
        [np.concatenate([cos_table, -sin_table], 1), np.concatenate([sin_table, cos_table], 1)], 0
    )
    return left_forward, right_forward, left_inverse, right_inverse


ROOT = math.sqrt(math.log2(math.e))


def scaled_square(coords):
    pixels = lax.broadcasted_iota(jnp.int32, (SUB, NV), 0).astype(jnp.float32) * ROOT
    delta = pixels - coords * ROOT
    return delta * delta


def kernel_of(coords):
    return jnp.exp2(-scaled_square(coords))


def kernel_low(coords):
    return kernel_of(coords).astype(jnp.bfloat16)


def live_row(count):
    lane = lax.broadcasted_iota(jnp.int32, (1, NV), 1)
    return (lane < count).astype(jnp.float32)


def facet_order(side):
    steps = [(dx, dy) for dx in range(side) for dy in range(side)]
    return sorted(steps, key=lambda d: (sum(min(n, side - n) for n in d), d))


def facet_steps(me, side):
    x, y = me // side, lax.rem(me, side)
    targets, sources = [], []
    for dx, dy in facet_order(side)[1:]:
        targets.append(lax.rem(x + dx, side) * side + lax.rem(y + dy, side))
        sources.append(lax.rem(x + side - dx, side) * side + lax.rem(y + side - dy, side))
    return targets, sources


def swapped(values):
    half = values.shape[-1] // 2
    return jnp.concatenate([-values[:, half:], values[:, :half]], 1)


def left_pair(table, one, two):
    upper = jnp.concatenate([one, two], 1)
    lower = jnp.concatenate([swapped(one), swapped(two)], 1)
    out = jnp.dot(table, jnp.concatenate([upper, lower], 0), preferred_element_type=jnp.float32)
    return out.astype(jnp.bfloat16)


def gridded(coords, weighted):
    ku = kernel_low(coords[0:1])
    kv = kernel_low(coords[1:2])
    spread = jnp.concatenate([weighted[0:1] * kv, weighted[1:2] * kv], 0)
    return lax.dot_general(
        ku, spread, (((1,), (1,)), ((), ())), preferred_element_type=jnp.float32
    ).astype(jnp.bfloat16)


SIZES = (6, 6, 4)


def grid_kernel(
    facets, side, subgrids,
    cnt_hbm, fid_hbm, row_hbm, col_hbm, vis_hbm, uv_hbm, model, left_hbm, right_hbm,
    patches, meta_in, model_rows, canvas,
    cnt, fid, row, col, vis, uv, left_f, right_f, raw, vis_send, vis_in, uv_send, uv_in, meta_send,
    grids, halves, first, last,
    in_sem, raw_sem, send_sem, recv_sem, own_sem,
):
    me = lax.axis_index("facet")
    targets, _ = facet_steps(me, side)
    barrier = pltpu.get_barrier_semaphore()
    for peer in targets:
        pl.semaphore_signal(barrier, inc=1, device_id={"facet": peer})
    fetches = []
    for i, (src, dst) in enumerate((
        (fid_hbm, fid), (cnt_hbm, cnt), (row_hbm, row), (col_hbm, col), (vis_hbm, vis), (uv_hbm, uv),
        (left_hbm, left_f), (right_hbm, right_f),
    )):
        fetch = pltpu.make_async_copy(src, dst, in_sem.at[i])
        fetch.start()
        fetches.append(fetch)

    def model_copy(tile):
        at = pl.ds(pl.multiple_of(tile * LANES, LANES), LANES)
        return pltpu.make_async_copy(model.at[0, :, :, at], raw.at[tile], raw_sem.at[tile])

    def fetch_model(tile, carry):
        model_copy(tile).start()
        return carry

    lax.fori_loop(0, TILES, fetch_model, 0)
    for fetch in fetches:
        fetch.wait()

    ids = [fid[s] for s in range(subgrids)]

    def find(facet, carry):
        low = jnp.int32(subgrids)
        high = jnp.int32(-1)
        for s in range(subgrids):
            high = jnp.where(ids[s] == facet, s, high)
            back = subgrids - 1 - s
            low = jnp.where(ids[back] == facet, back, low)
        first[facet] = low
        last[facet] = high
        return carry

    lax.fori_loop(0, facets, find, 0)

    lane = lax.broadcasted_iota(jnp.int32, (1, LANES), 1)

    def pack(facet, carry):
        low, high = first[facet], last[facet]
        one = jnp.minimum(low, subgrids - 1)
        two = jnp.maximum(high, 0)
        weighted = [vis[s] * live_row(cnt[s]) for s in (one, two)]
        vis_send[facet] = jnp.concatenate(weighted, 0).astype(jnp.bfloat16)
        uv_send[facet] = jnp.concatenate([uv[one], uv[two]], 0)
        values = (
            (high >= 0).astype(jnp.int32), row[one], col[one],
            (high > low).astype(jnp.int32), row[two], col[two],
        )
        line = jnp.zeros((1, LANES), jnp.int32)
        for place, value in enumerate(values):
            line = jnp.where(lane == place, value, line)
        meta_send[facet] = line
        return carry

    lax.fori_loop(0, facets, pack, 0)

    pl.semaphore_wait(barrier, facets - 1)
    moved = ((meta_send, meta_in), (vis_send, vis_in), (uv_send, uv_in))
    copies = [[] for _ in range(facets)]
    for step in range(facets - 1, -1, -1):
        for i, (src, dst) in enumerate(moved):
            if step > 0:
                copy = pltpu.make_async_remote_copy(
                    src_ref=src.at[targets[step - 1]], dst_ref=dst.at[step],
                    send_sem=send_sem.at[i, step], recv_sem=recv_sem.at[i, step],
                    device_id={"facet": targets[step - 1]},
                )
            else:
                copy = pltpu.make_async_copy(src.at[me], dst.at[0], own_sem.at[i])
            copy.start()
            copies[step].append(copy)

    rows_view = raw.reshape(TILES, 2 * F_ROWS, LANES)

    def widen(tile, carry):
        model_copy(tile).wait()
        model_rows[tile] = rows_view[tile].astype(jnp.float32)
        canvas[0, tile] = zero
        canvas[1, tile] = zero
        return carry

    zero = jnp.zeros((F_ROWS, LANES), jnp.float32)
    lax.fori_loop(0, TILES, widen, 0)
    canvas[0, TILES] = zero
    canvas[1, TILES] = zero

    def grid_one(step):
        for slot in range(SLOTS):
            at = pl.ds(2 * slot, 2)
            grids[SLOTS * step + slot] = gridded(uv_in[step, at, :], vis_in[step, at, :])

    def left_one(step):
        out = left_pair(left_f[...], grids[SLOTS * step], grids[SLOTS * step + 1])
        halves[SLOTS * step] = out[:, :LANES]
        halves[SLOTS * step + 1] = out[:, LANES:]

    def right_one(step):
        both = halves[pl.ds(SLOTS * step, SLOTS)].reshape(SLOTS * SUB, LANES)
        patches[pl.ds(SLOTS * SUB * step, SLOTS * SUB), :] = jnp.dot(
            both, right_f[...], preferred_element_type=jnp.float32
        )

    begins = [0]
    for size in SIZES:
        begins.append(begins[-1] + size)
    groups = [range(a, b) for a, b in zip(begins, begins[1:])]
    stages = (grid_one, left_one, right_one)
    for turn in range(len(groups) + len(stages) - 1):
        if turn < len(groups):
            for step in groups[turn]:
                for copy in copies[step]:
                    copy.wait_recv() if step > 0 else copy.wait()
        now = []
        for lag, stage in enumerate(stages):
            if 0 <= turn - lag < len(groups):
                now.append([functools.partial(stage, step) for step in groups[turn - lag]])
        for parts in itertools.zip_longest(*now):
            for part in reversed(parts):
                if part is not None:
                    part()
    for step in range(1, facets):
        for copy in copies[step]:
            copy.wait_send()


def add_kernel(facets, meta, patches, _, canvas):
    lane = lax.broadcasted_iota(jnp.int32, (SUB, LANES), 1)

    def add(step, carry):
        for slot in range(SLOTS):
            valid = meta[step, 0, 3 * slot] > 0
            top = meta[step, 0, 3 * slot + 1]
            col = meta[step, 0, 3 * slot + 2]
            tile, shift = col // LANES, lax.rem(col, LANES)
            low = jnp.where(valid, shift, LANES)
            high = jnp.where(valid, shift - SUB, 0)
            patch = patches[pl.ds(pl.multiple_of((step * 2 + slot) * SUB, SUB), SUB), :]
            inside = (lane >= low) & (lane < shift + SUB)
            beyond = lane < high
            at = pl.ds(top, SUB)
            spots = [(part, tile + next_tile) for part in range(2) for next_tile in range(2)]
            before = [canvas[part, spot, at, :] for part, spot in spots]
            turned = (
                pltpu.roll(patch, shift, 1),
                pltpu.roll(patch, lax.rem(shift + SUB, LANES), 1),
            )
            for i, (part, spot) in enumerate(spots):
                canvas[part, spot, at, :] = before[i] + jnp.where(
                    beyond if i % 2 else inside, turned[part], 0.0
                )
        return carry

    lax.fori_loop(0, facets, add, 0, unroll=2)


PIECES = 4
PICKS = 2
DEGRIDS = 4


def exchange_kernel(
    facets, side, chans, subgrids,
    meta, cnt, fid, canvas, model_rows, vis, uv, left_i, right_i,
    total, residual,
    half_buf, pair_buf, send_buf, recv_buf, back, returned, place,
    pair_send, pair_recv, ring_send, ring_recv, back_send, back_recv, own_sem, near_sem, far_sem,
):
    chips = chans // 2
    me_f, me_c = lax.axis_index("facet"), lax.axis_index("chan")
    z, core = me_c // 2, lax.rem(me_c, 2)
    partner = z * 2 + 1 - core
    right = lax.rem(z + 1, chips) * 2 + core
    left = lax.rem(z + chips - 1, chips) * 2 + core
    targets, sources = facet_steps(me_f, side)
    hops = [sum(min(n, side - n) for n in d) for d in facet_order(side)][1:]
    near = [peer for peer, hop in zip(targets, hops) if hop == 1]
    middle = [peer for peer, hop in zip(targets, hops) if hop == 2]
    rows = F_ROWS // chans
    barrier = pltpu.get_barrier_semaphore()
    for peer in (partner, right, left):
        pl.semaphore_signal(barrier, inc=1, device_id={"chan": peer})
    for peer in near:
        pl.semaphore_signal(barrier, inc=1, device_id={"facet": peer})

    lane = lax.broadcasted_iota(jnp.int32, (SUB, LANES), 1)

    def picked(step, slot):
        top = meta[step, 0, 3 * slot + 1]
        col = meta[step, 0, 3 * slot + 2]
        tile, shift = col // LANES, lax.rem(col, LANES)
        after = jnp.minimum(tile + 1, TILES - 1)
        parts = [
            jnp.where(
                lane >= shift,
                model_rows[tile, pl.ds(2 * top + part, SUB, stride=2), :],
                model_rows[after, pl.ds(2 * top + part, SUB, stride=2), :],
            )
            for part in range(2)
        ]
        re = pltpu.roll(parts[0], lax.rem(LANES - shift, LANES), 1)
        im = pltpu.roll(parts[1], lax.rem(LANES + SUB - shift, LANES), 1)
        return jnp.where(lane < SUB, re, im).astype(jnp.bfloat16)

    def pick(begin):
        halves = []
        for step in range(begin, begin + PICKS):
            out = left_pair(left_i[...], picked(step, 0), picked(step, 1))
            halves += [out[:, :LANES], out[:, LANES:]]
        out = jnp.dot(
            jnp.concatenate(halves, 0), right_i[...], preferred_element_type=jnp.float32
        ).astype(jnp.bfloat16)
        for i in range(PICKS):
            for slot in range(SLOTS):
                at = (2 * i + slot) * SUB
                back[begin + i, slot] = out[at : at + SUB]

    half = chips // 2
    depth = half_buf.shape[1] // PIECES

    def length(piece, way):
        return half - (piece + way) % 2

    needed = []
    for step in range(half):
        for piece in range(PIECES):
            for way in range(2):
                distance = length(piece, way) - step
                need = (distance % chips if way == 0 else (chips - distance) % chips, piece)
                if distance > 0 and need not in needed:
                    needed.append(need)
    needed += [(0, piece) for piece in range(PIECES)]

    work = [functools.partial(pick, begin) for begin in range(facets - PICKS, -1, -PICKS)]

    def chan_rows(offset, which):
        there = lax.rem(z + offset, chips)
        return pl.ds(pl.multiple_of((2 * there + which) * rows, rows), rows)

    def narrow(pair, carry):
        for offset in range(chips):
            for part in range(2):
                both = canvas[part, pl.ds(2 * pair, 2), chan_rows(offset, 1 - core), :]
                at = pl.ds(pl.multiple_of((part * TILES + 2 * pair) * rows, 2 * rows), 2 * rows)
                half_buf[offset, at, :] = both.reshape(2 * rows, LANES).astype(jnp.bfloat16)
        return carry

    lax.fori_loop(0, TILES // 2, narrow, 0)
    pl.semaphore_wait(barrier, 3 + len(near))
    for peer in near:
        pl.semaphore_signal(near_sem, inc=1, device_id={"facet": peer})

    pair_copy = {}
    for i, (offset, piece) in enumerate(needed):
        at = pl.ds(piece * depth, depth)
        copy = pltpu.make_async_remote_copy(
            src_ref=half_buf.at[offset, at, :], dst_ref=pair_buf.at[offset, at, :],
            send_sem=pair_send.at[i], recv_sem=pair_recv.at[i], device_id={"chan": partner},
        )
        copy.start()
        pair_copy[offset, piece] = copy

    arrived = set()

    def mine(offset, piece):
        if (offset, piece) not in arrived:
            arrived.add((offset, piece))
            pair_copy[offset, piece].wait_recv()
        at = pl.ds(piece * depth, depth)
        tiles = TILES * 2 // PIECES
        part, begin = divmod(piece * tiles, TILES)
        own = canvas[part, pl.ds(begin, tiles), chan_rows(offset, core), :]
        return own.reshape(depth, LANES) + pair_buf[offset, at, :].astype(jnp.float32)

    ring = {}

    def ring_step(step):
        for piece in range(PIECES):
            for way in range(2):
                count = length(piece, way)
                if step >= count:
                    continue
                distance = count - step
                offset = distance if way == 0 else chips - distance
                value = mine(offset % chips, piece)
                slot = (way * PIECES + piece) * half + step
                if step > 0:
                    ring[way, piece, step - 1].wait_recv()
                    value = value + recv_buf[slot - 1].astype(jnp.float32)
                send_buf[slot] = value.astype(jnp.bfloat16)
                copy = pltpu.make_async_remote_copy(
                    src_ref=send_buf.at[slot], dst_ref=recv_buf.at[slot],
                    send_sem=ring_send.at[slot], recv_sem=ring_recv.at[slot],
                    device_id={"chan": right if way == 0 else left},
                )
                copy.start()
                ring[way, piece, step] = copy

    def degrid(begin):
        for s in range(begin, begin + DEGRIDS):
            image = returned[place[s], place[subgrids + s]]
            ku = kernel_low(uv[s, pl.ds(0, 1), :])
            weight = kernel_of(uv[s, pl.ds(1, 1), :])
            inner = lax.dot_general(
                image, ku, (((0,), (0,)), ((), ())), preferred_element_type=jnp.float32
            )
            live = live_row(cnt[s])
            for part in range(2):
                predicted = jnp.sum(inner[part * SUB : (part + 1) * SUB] * weight, 0, keepdims=True)
                residual[s, pl.ds(part, 1), :] = (vis[s, pl.ds(part, 1), :] - predicted) * live

    back_copy = []

    def send_back():
        for step in range(facets - 1, 0, -1):
            copy = pltpu.make_async_remote_copy(
                src_ref=back.at[step], dst_ref=returned.at[step],
                send_sem=back_send.at[step], recv_sem=back_recv.at[step],
                device_id={"facet": sources[step - 1]},
            )
            copy.start()
            back_copy.append(copy)
        own = pltpu.make_async_copy(back.at[0], returned.at[0], own_sem)
        own.start()
        back_copy.append(own)

    def locate():
        ids = [fid[s] for s in range(subgrids)]
        x, y = me_f // side, lax.rem(me_f, side)
        codes = []
        for s in range(subgrids):
            before = jnp.int32(0)
            for other in range(s):
                before = jnp.where(ids[other] == ids[s], 1, before)
            there_x, there_y = ids[s] // side, lax.rem(ids[s], side)
            code = lax.rem(there_x + side - x, side) * side + lax.rem(there_y + side - y, side)
            where = jnp.int32(0)
            for step, known in enumerate(facet_order(side)):
                where = jnp.where(code == known[0] * side + known[1], step, where)
            place[s] = where
            place[subgrids + s] = before

    ring_step(0)
    pl.semaphore_wait(near_sem, len(near))
    for peer in middle:
        pl.semaphore_signal(far_sem, inc=1, device_id={"facet": peer})
    while work:
        work.pop(0)()
    pl.semaphore_wait(far_sem, len(middle))
    send_back()
    locate()
    for step in range(1, half):
        ring_step(step)
    for copy in back_copy:
        copy.wait()
    for begin in range(0, subgrids, DEGRIDS):
        degrid(begin)
    for piece in range(PIECES):
        value = mine(0, piece)
        for way in range(2):
            step = length(piece, way) - 1
            ring[way, piece, step].wait_recv()
            value = value + recv_buf[(way * PIECES + piece) * half + step].astype(jnp.float32)
        total[pl.ds(piece * depth, depth), :] = value
    for copy in pair_copy.values():
        copy.wait_send()
    for copy in ring.values():
        copy.wait_send()


def output_kernel(rows, total, values, image, residual):
    def place(tile, carry):
        at = pl.ds(pl.multiple_of(tile * LANES, LANES), LANES)
        for part in range(2):
            begin = pl.multiple_of((part * TILES + tile) * rows, rows)
            image[0, :, part, at] = total[pl.ds(begin, rows), :]
        return carry

    lax.fori_loop(0, TILES, place, 0, unroll=4)
    residual[...] = values[...]


VMEM = pl.BlockSpec(memory_space=pltpu.VMEM)
SMEM = pl.BlockSpec(memory_space=pltpu.SMEM)
HBM = pl.BlockSpec(memory_space=pltpu.HBM)


def per_device(
    visibility, uv_coords, vis_count, subgrid_facet, row_offset, col_offset, model_facet
):
    facets, chans = lax.axis_size("facet"), lax.axis_size("chan")
    side = math.isqrt(facets)
    chips = chans // 2
    subgrids = visibility.shape[0]
    rows = F_ROWS // chans
    shape = jax.ShapeDtypeStruct
    left_f, right_f, left_i, right_i = (jnp.asarray(table) for table in dft_tables())
    ids = subgrid_facet[:, 0]

    patches, meta, model_rows, zeros = pl.pallas_call(
        functools.partial(grid_kernel, facets, side, subgrids),
        out_shape=(
            shape((facets * SLOTS * SUB, LANES), jnp.float32),
            shape((facets, 1, LANES), jnp.int32),
            shape((TILES, 2 * F_ROWS, LANES), jnp.float32),
            shape((2, TILES + 1, F_ROWS, LANES), jnp.float32),
        ),
        in_specs=[HBM] * 9,
        out_specs=(VMEM,) * 4,
        scratch_shapes=[
            pltpu.SMEM((subgrids,), jnp.int32),
            pltpu.SMEM((subgrids,), jnp.int32),
            pltpu.SMEM((subgrids,), jnp.int32),
            pltpu.SMEM((subgrids,), jnp.int32),
            pltpu.VMEM(visibility.shape, jnp.float32),
            pltpu.VMEM(uv_coords.shape, jnp.float32),
            pltpu.VMEM(left_f.shape, jnp.bfloat16),
            pltpu.VMEM(right_f.shape, jnp.bfloat16),
            pltpu.VMEM((TILES, F_ROWS, 2, LANES), jnp.bfloat16),
            pltpu.VMEM((facets, 2 * SLOTS, NV), jnp.bfloat16),
            pltpu.VMEM((facets, 2 * SLOTS, NV), jnp.bfloat16),
            pltpu.VMEM((facets, 2 * SLOTS, NV), jnp.float32),
            pltpu.VMEM((facets, 2 * SLOTS, NV), jnp.float32),
            pltpu.VMEM((facets, 1, LANES), jnp.int32),
            pltpu.VMEM((facets * SLOTS, SUB, LANES), jnp.bfloat16),
            pltpu.VMEM((facets * SLOTS, SUB, LANES), jnp.bfloat16),
            pltpu.SMEM((facets,), jnp.int32),
            pltpu.SMEM((facets,), jnp.int32),
            pltpu.SemaphoreType.DMA((8,)),
            pltpu.SemaphoreType.DMA((TILES,)),
            pltpu.SemaphoreType.DMA((3, facets)),
            pltpu.SemaphoreType.DMA((3, facets)),
            pltpu.SemaphoreType.DMA((3,)),
        ],
        compiler_params=pltpu.CompilerParams(
            collective_id=0, has_side_effects=True, vmem_limit_bytes=16 << 20
        ),
        name="grid_and_send",
    )(
        *(
            pltpu.with_memory_space_constraint(array, pltpu.HBM)
            for array in (
                vis_count, ids, row_offset, col_offset, visibility, uv_coords, model_facet,
                left_f, right_f,
            )
        )
    )

    canvas = pl.pallas_call(
        functools.partial(add_kernel, facets),
        out_shape=shape((2, TILES + 1, F_ROWS, LANES), jnp.float32),
        in_specs=[SMEM, VMEM, VMEM],
        out_specs=VMEM,
        input_output_aliases={2: 0},
        compiler_params=pltpu.CompilerParams(vmem_limit_bytes=16 << 20),
        name="add_windows",
    )(meta, patches, zeros)

    depth = 2 * TILES * rows // PIECES
    links = 2 * PIECES * (chips // 2)
    total, residual = pl.pallas_call(
        functools.partial(exchange_kernel, facets, side, chans, subgrids),
        out_shape=(
            shape((2 * TILES * rows, LANES), jnp.float32),
            shape(visibility.shape, jnp.float32),
        ),
        in_specs=[SMEM] * 3 + [VMEM] * 6,
        out_specs=(VMEM,) * 2,
        scratch_shapes=[
            pltpu.VMEM((chips, 2 * TILES * rows, LANES), jnp.bfloat16),
            pltpu.VMEM((chips, 2 * TILES * rows, LANES), jnp.bfloat16),
            pltpu.VMEM((links, depth, LANES), jnp.bfloat16),
            pltpu.VMEM((links, depth, LANES), jnp.bfloat16),
            pltpu.VMEM((facets, SLOTS, SUB, LANES), jnp.bfloat16),
            pltpu.VMEM((facets, SLOTS, SUB, LANES), jnp.bfloat16),
            pltpu.SMEM((2 * subgrids,), jnp.int32),
            pltpu.SemaphoreType.DMA((chips * PIECES,)),
            pltpu.SemaphoreType.DMA((chips * PIECES,)),
            pltpu.SemaphoreType.DMA((links,)),
            pltpu.SemaphoreType.DMA((links,)),
            pltpu.SemaphoreType.DMA((facets,)),
            pltpu.SemaphoreType.DMA((facets,)),
            pltpu.SemaphoreType.DMA,
            pltpu.SemaphoreType.REGULAR,
            pltpu.SemaphoreType.REGULAR,
        ],
        compiler_params=pltpu.CompilerParams(
            collective_id=1, has_side_effects=True, vmem_limit_bytes=20 << 20
        ),
        name="reduce_and_return",
    )(meta, vis_count, ids, canvas, model_rows, visibility, uv_coords, left_i, right_i)

    image, residual = pl.pallas_call(
        functools.partial(output_kernel, rows),
        out_shape=(
            shape((1, rows, 2, FACET), jnp.float32),
            shape(visibility.shape, jnp.float32),
        ),
        in_specs=[VMEM] * 2,
        out_specs=(VMEM,) * 2,
        compiler_params=pltpu.CompilerParams(vmem_limit_bytes=8 << 20),
        name="outputs",
    )(total, residual)
    return image, residual


def solution(mesh):
    in_specs = (
        P(("facet", "chan"), None, None),
        P(("facet", "chan"), None, None),
        P(("facet", "chan")),
        P(("facet", "chan"), None),
        P(("facet", "chan")),
        P(("facet", "chan")),
        P("facet", None, None, None),
    )
    out_specs = (P("facet", "chan", None, None), P(("facet", "chan"), None, None))
    return jax.shard_map(
        per_device, mesh=mesh, in_specs=in_specs, out_specs=out_specs, check_vma=False
    )
```

```python
import functools
import itertools
import math

import jax
import jax.numpy as jnp
import numpy as np
from jax import lax
from jax.experimental import pallas as pl
from jax.experimental.pallas import tpu as pltpu
from jax.sharding import PartitionSpec as P

SUB = 64
FACET = 4096
F_ROWS = 128
NV = 512
LANES = 128
TILES = FACET // LANES
SLOTS = 2


def dft_tables():
    line = np.arange(SUB)
    angle = 2.0 * math.pi * (line[:, None] * line[None, :] % SUB) / SUB
    cos_table = (np.cos(angle) / math.sqrt(SUB)).astype(jnp.bfloat16)
    sin_table = (-np.sin(angle) / math.sqrt(SUB)).astype(jnp.bfloat16)
    left_forward = np.concatenate([cos_table, sin_table], 1)
    left_inverse = np.concatenate([cos_table, -sin_table], 1)
    right_forward = np.concatenate(
        [np.concatenate([cos_table, sin_table], 1), np.concatenate([-sin_table, cos_table], 1)], 0
    )
    right_inverse = np.concatenate(
        [np.concatenate([cos_table, -sin_table], 1), np.concatenate([sin_table, cos_table], 1)], 0
    )
    return left_forward, right_forward, left_inverse, right_inverse


ROOT = math.sqrt(math.log2(math.e))


def scaled_square(coords):
    pixels = lax.broadcasted_iota(jnp.int32, (SUB, NV), 0).astype(jnp.float32) * ROOT
    delta = pixels - coords * ROOT
    return delta * delta


def kernel_of(coords):
    return jnp.exp2(-scaled_square(coords))


def kernel_low(coords):
    return kernel_of(coords).astype(jnp.bfloat16)


def live_row(count):
    lane = lax.broadcasted_iota(jnp.int32, (1, NV), 1)
    return (lane < count).astype(jnp.float32)


def facet_order(side):
    steps = [(dx, dy) for dx in range(side) for dy in range(side)]
    return sorted(steps, key=lambda d: (sum(min(n, side - n) for n in d), d))


def facet_steps(me, side):
    x, y = me // side, lax.rem(me, side)
    targets, sources = [], []
    for dx, dy in facet_order(side)[1:]:
        targets.append(lax.rem(x + dx, side) * side + lax.rem(y + dy, side))
        sources.append(lax.rem(x + side - dx, side) * side + lax.rem(y + side - dy, side))
    return targets, sources


def swapped(values):
    half = values.shape[-1] // 2
    return jnp.concatenate([-values[:, half:], values[:, :half]], 1)


def left_pair(table, one, two):
    upper = jnp.concatenate([one, two], 1)
    lower = jnp.concatenate([swapped(one), swapped(two)], 1)
    out = jnp.dot(table, jnp.concatenate([upper, lower], 0), preferred_element_type=jnp.float32)
    return out.astype(jnp.bfloat16)


def gridded(coords, weighted):
    ku = kernel_low(coords[0:1])
    kv = kernel_low(coords[1:2])
    spread = jnp.concatenate([weighted[0:1] * kv, weighted[1:2] * kv], 0)
    return lax.dot_general(
        ku, spread, (((1,), (1,)), ((), ())), preferred_element_type=jnp.float32
    ).astype(jnp.bfloat16)


SIZES = (6, 6, 4)


def grid_kernel(
    facets, side, subgrids,
    cnt_hbm, fid_hbm, row_hbm, col_hbm, vis_hbm, uv_hbm, model, left_hbm, right_hbm,
    patches, meta_in, model_rows, canvas,
    cnt, fid, row, col, vis, uv, left_f, right_f, raw, vis_send, vis_in, uv_send, uv_in, meta_send,
    grids, halves, first, last,
    in_sem, raw_sem, send_sem, recv_sem, own_sem,
):
    me = lax.axis_index("facet")
    targets, _ = facet_steps(me, side)
    barrier = pltpu.get_barrier_semaphore()
    for peer in targets:
        pl.semaphore_signal(barrier, inc=1, device_id={"facet": peer})
    fetches = []
    for i, (src, dst) in enumerate((
        (fid_hbm, fid), (cnt_hbm, cnt), (row_hbm, row), (col_hbm, col), (vis_hbm, vis), (uv_hbm, uv),
        (left_hbm, left_f), (right_hbm, right_f),
    )):
        fetch = pltpu.make_async_copy(src, dst, in_sem.at[i])
        fetch.start()
        fetches.append(fetch)

    def model_copy(tile):
        at = pl.ds(pl.multiple_of(tile * LANES, LANES), LANES)
        return pltpu.make_async_copy(model.at[0, :, :, at], raw.at[tile], raw_sem.at[tile])

    def fetch_model(tile, carry):
        model_copy(tile).start()
        return carry

    lax.fori_loop(0, TILES, fetch_model, 0)
    for fetch in fetches:
        fetch.wait()

    ids = [fid[s] for s in range(subgrids)]

    def find(facet, carry):
        low = jnp.int32(subgrids)
        high = jnp.int32(-1)
        for s in range(subgrids):
            high = jnp.where(ids[s] == facet, s, high)
            back = subgrids - 1 - s
            low = jnp.where(ids[back] == facet, back, low)
        first[facet] = low
        last[facet] = high
        return carry

    lax.fori_loop(0, facets, find, 0)

    lane = lax.broadcasted_iota(jnp.int32, (1, LANES), 1)

    def pack(facet, carry):
        low, high = first[facet], last[facet]
        one = jnp.minimum(low, subgrids - 1)
        two = jnp.maximum(high, 0)
        weighted = [vis[s] * live_row(cnt[s]) for s in (one, two)]
        vis_send[facet] = jnp.concatenate(weighted, 0).astype(jnp.bfloat16)
        uv_send[facet] = jnp.concatenate([uv[one], uv[two]], 0)
        values = (
            (high >= 0).astype(jnp.int32), row[one], col[one],
            (high > low).astype(jnp.int32), row[two], col[two],
        )
        line = jnp.zeros((1, LANES), jnp.int32)
        for place, value in enumerate(values):
            line = jnp.where(lane == place, value, line)
        meta_send[facet] = line
        return carry

    lax.fori_loop(0, facets, pack, 0)

    pl.semaphore_wait(barrier, facets - 1)
    moved = ((meta_send, meta_in), (vis_send, vis_in), (uv_send, uv_in))
    copies = [[] for _ in range(facets)]
    for step in range(facets - 1, -1, -1):
        for i, (src, dst) in enumerate(moved):
            if step > 0:
                copy = pltpu.make_async_remote_copy(
                    src_ref=src.at[targets[step - 1]], dst_ref=dst.at[step],
                    send_sem=send_sem.at[i, step], recv_sem=recv_sem.at[i, step],
                    device_id={"facet": targets[step - 1]},
                )
            else:
                copy = pltpu.make_async_copy(src.at[me], dst.at[0], own_sem.at[i])
            copy.start()
            copies[step].append(copy)

    rows_view = raw.reshape(TILES, 2 * F_ROWS, LANES)

    def widen(tile, carry):
        model_copy(tile).wait()
        model_rows[tile] = rows_view[tile].astype(jnp.float32)
        canvas[0, tile] = zero
        canvas[1, tile] = zero
        return carry

    zero = jnp.zeros((F_ROWS, LANES), jnp.float32)
    lax.fori_loop(0, TILES, widen, 0)
    canvas[0, TILES] = zero
    canvas[1, TILES] = zero

    def grid_one(step):
        for slot in range(SLOTS):
            at = pl.ds(2 * slot, 2)
            grids[SLOTS * step + slot] = gridded(uv_in[step, at, :], vis_in[step, at, :])

    def left_one(step):
        out = left_pair(left_f[...], grids[SLOTS * step], grids[SLOTS * step + 1])
        halves[SLOTS * step] = out[:, :LANES]
        halves[SLOTS * step + 1] = out[:, LANES:]

    def right_one(step):
        both = halves[pl.ds(SLOTS * step, SLOTS)].reshape(SLOTS * SUB, LANES)
        patches[pl.ds(SLOTS * SUB * step, SLOTS * SUB), :] = jnp.dot(
            both, right_f[...], preferred_element_type=jnp.float32
        )

    begins = [0]
    for size in SIZES:
        begins.append(begins[-1] + size)
    groups = [range(a, b) for a, b in zip(begins, begins[1:])]
    stages = (grid_one, left_one, right_one)
    for turn in range(len(groups) + len(stages) - 1):
        if turn < len(groups):
            for step in groups[turn]:
                for copy in copies[step]:
                    copy.wait_recv() if step > 0 else copy.wait()
        now = []
        for lag, stage in enumerate(stages):
            if 0 <= turn - lag < len(groups):
                now.append([functools.partial(stage, step) for step in groups[turn - lag]])
        for parts in itertools.zip_longest(*now):
            for part in reversed(parts):
                if part is not None:
                    part()
    for step in range(1, facets):
        for copy in copies[step]:
            copy.wait_send()


def add_kernel(facets, meta, patches, _, canvas):
    lane = lax.broadcasted_iota(jnp.int32, (SUB, LANES), 1)

    def add(step, carry):
        for slot in range(SLOTS):
            valid = meta[step, 0, 3 * slot] > 0
            top = meta[step, 0, 3 * slot + 1]
            col = meta[step, 0, 3 * slot + 2]
            tile, shift = col // LANES, lax.rem(col, LANES)
            low = jnp.where(valid, shift, LANES)
            high = jnp.where(valid, shift - SUB, 0)
            patch = patches[pl.ds(pl.multiple_of((step * 2 + slot) * SUB, SUB), SUB), :]
            inside = (lane >= low) & (lane < shift + SUB)
            beyond = lane < high
            at = pl.ds(top, SUB)
            spots = [(part, tile + next_tile) for part in range(2) for next_tile in range(2)]
            before = [canvas[part, spot, at, :] for part, spot in spots]
            turned = (
                pltpu.roll(patch, shift, 1),
                pltpu.roll(patch, lax.rem(shift + SUB, LANES), 1),
            )
            for i, (part, spot) in enumerate(spots):
                canvas[part, spot, at, :] = before[i] + jnp.where(
                    beyond if i % 2 else inside, turned[part], 0.0
                )
        return carry

    lax.fori_loop(0, facets, add, 0, unroll=2)


PIECES = 4
PICKS = 2
DEGRIDS = 4


def exchange_kernel(
    facets, side, chans, subgrids,
    meta, cnt, fid, canvas, model_rows, vis, uv, left_i, right_i,
    total, residual,
    own_ku, own_kv, half_buf, pair_buf, send_buf, recv_buf, back, returned, place,
    pair_send, pair_recv, ring_send, ring_recv, back_send, back_recv, own_sem, near_sem, far_sem,
):
    chips = chans // 2
    me_f, me_c = lax.axis_index("facet"), lax.axis_index("chan")
    z, core = me_c // 2, lax.rem(me_c, 2)
    partner = z * 2 + 1 - core
    right = lax.rem(z + 1, chips) * 2 + core
    left = lax.rem(z + chips - 1, chips) * 2 + core
    targets, sources = facet_steps(me_f, side)
    hops = [sum(min(n, side - n) for n in d) for d in facet_order(side)][1:]
    near = [peer for peer, hop in zip(targets, hops) if hop == 1]
    middle = [peer for peer, hop in zip(targets, hops) if hop == 2]
    rows = F_ROWS // chans
    barrier = pltpu.get_barrier_semaphore()
    for peer in (partner, right, left):
        pl.semaphore_signal(barrier, inc=1, device_id={"chan": peer})
    for peer in near:
        pl.semaphore_signal(barrier, inc=1, device_id={"facet": peer})

    lane = lax.broadcasted_iota(jnp.int32, (SUB, LANES), 1)

    def picked(step, slot):
        top = meta[step, 0, 3 * slot + 1]
        col = meta[step, 0, 3 * slot + 2]
        tile, shift = col // LANES, lax.rem(col, LANES)
        after = jnp.minimum(tile + 1, TILES - 1)
        parts = [
            jnp.where(
                lane >= shift,
                model_rows[tile, pl.ds(2 * top + part, SUB, stride=2), :],
                model_rows[after, pl.ds(2 * top + part, SUB, stride=2), :],
            )
            for part in range(2)
        ]
        re = pltpu.roll(parts[0], lax.rem(LANES - shift, LANES), 1)
        im = pltpu.roll(parts[1], lax.rem(LANES + SUB - shift, LANES), 1)
        return jnp.where(lane < SUB, re, im).astype(jnp.bfloat16)

    def pick(begin):
        halves = []
        for step in range(begin, begin + PICKS):
            out = left_pair(left_i[...], picked(step, 0), picked(step, 1))
            halves += [out[:, :LANES], out[:, LANES:]]
        out = jnp.dot(
            jnp.concatenate(halves, 0), right_i[...], preferred_element_type=jnp.float32
        ).astype(jnp.bfloat16)
        for i in range(PICKS):
            for slot in range(SLOTS):
                at = (2 * i + slot) * SUB
                back[begin + i, slot] = out[at : at + SUB]

    half = chips // 2
    depth = half_buf.shape[1] // PIECES

    def length(piece, way):
        return half - (piece + way) % 2

    needed = []
    for step in range(half):
        for piece in range(PIECES):
            for way in range(2):
                distance = length(piece, way) - step
                need = (distance % chips if way == 0 else (chips - distance) % chips, piece)
                if distance > 0 and need not in needed:
                    needed.append(need)
    needed += [(0, piece) for piece in range(PIECES)]

    work = [functools.partial(pick, begin) for begin in range(facets - PICKS, -1, -PICKS)]

    def chan_rows(offset, which):
        there = lax.rem(z + offset, chips)
        return pl.ds(pl.multiple_of((2 * there + which) * rows, rows), rows)

    def narrow(pair, carry):
        for offset in range(chips):
            for part in range(2):
                both = canvas[part, pl.ds(2 * pair, 2), chan_rows(offset, 1 - core), :]
                at = pl.ds(pl.multiple_of((part * TILES + 2 * pair) * rows, 2 * rows), 2 * rows)
                half_buf[offset, at, :] = both.reshape(2 * rows, LANES).astype(jnp.bfloat16)
        return carry

    lax.fori_loop(0, TILES // 2, narrow, 0)
    pl.semaphore_wait(barrier, 3 + len(near))
    for peer in near:
        pl.semaphore_signal(near_sem, inc=1, device_id={"facet": peer})

    pair_copy = {}
    for i, (offset, piece) in enumerate(needed):
        at = pl.ds(piece * depth, depth)
        copy = pltpu.make_async_remote_copy(
            src_ref=half_buf.at[offset, at, :], dst_ref=pair_buf.at[offset, at, :],
            send_sem=pair_send.at[i], recv_sem=pair_recv.at[i], device_id={"chan": partner},
        )
        copy.start()
        pair_copy[offset, piece] = copy

    arrived = set()

    def mine(offset, piece):
        if (offset, piece) not in arrived:
            arrived.add((offset, piece))
            pair_copy[offset, piece].wait_recv()
        at = pl.ds(piece * depth, depth)
        tiles = TILES * 2 // PIECES
        part, begin = divmod(piece * tiles, TILES)
        own = canvas[part, pl.ds(begin, tiles), chan_rows(offset, core), :]
        return own.reshape(depth, LANES) + pair_buf[offset, at, :].astype(jnp.float32)

    ring = {}

    def ring_step(step):
        for piece in range(PIECES):
            for way in range(2):
                count = length(piece, way)
                if step >= count:
                    continue
                distance = count - step
                offset = distance if way == 0 else chips - distance
                value = mine(offset % chips, piece)
                slot = (way * PIECES + piece) * half + step
                if step > 0:
                    ring[way, piece, step - 1].wait_recv()
                    value = value + recv_buf[slot - 1].astype(jnp.float32)
                send_buf[slot] = value.astype(jnp.bfloat16)
                copy = pltpu.make_async_remote_copy(
                    src_ref=send_buf.at[slot], dst_ref=recv_buf.at[slot],
                    send_sem=ring_send.at[slot], recv_sem=ring_recv.at[slot],
                    device_id={"chan": right if way == 0 else left},
                )
                copy.start()
                ring[way, piece, step] = copy

    def own_kernels(begin, end):
        def one(s, carry):
            own_ku[s] = kernel_low(uv[s, pl.ds(0, 1), :])
            own_kv[s] = kernel_of(uv[s, pl.ds(1, 1), :])
            return carry

        lax.fori_loop(begin, end, one, 0, unroll=2)

    def degrid(begin):
        for s in range(begin, begin + DEGRIDS):
            image = returned[place[s], place[subgrids + s]]
            ku, weight = own_ku[s], own_kv[s]
            inner = lax.dot_general(
                image, ku, (((0,), (0,)), ((), ())), preferred_element_type=jnp.float32
            )
            live = live_row(cnt[s])
            for part in range(2):
                predicted = jnp.sum(inner[part * SUB : (part + 1) * SUB] * weight, 0, keepdims=True)
                residual[s, pl.ds(part, 1), :] = (vis[s, pl.ds(part, 1), :] - predicted) * live

    back_copy = []

    def send_back():
        for step in range(facets - 1, 0, -1):
            copy = pltpu.make_async_remote_copy(
                src_ref=back.at[step], dst_ref=returned.at[step],
                send_sem=back_send.at[step], recv_sem=back_recv.at[step],
                device_id={"facet": sources[step - 1]},
            )
            copy.start()
            back_copy.append(copy)
        own = pltpu.make_async_copy(back.at[0], returned.at[0], own_sem)
        own.start()
        back_copy.append(own)

    def locate():
        ids = [fid[s] for s in range(subgrids)]
        x, y = me_f // side, lax.rem(me_f, side)
        codes = []
        for s in range(subgrids):
            before = jnp.int32(0)
            for other in range(s):
                before = jnp.where(ids[other] == ids[s], 1, before)
            there_x, there_y = ids[s] // side, lax.rem(ids[s], side)
            code = lax.rem(there_x + side - x, side) * side + lax.rem(there_y + side - y, side)
            where = jnp.int32(0)
            for step, known in enumerate(facet_order(side)):
                where = jnp.where(code == known[0] * side + known[1], step, where)
            place[s] = where
            place[subgrids + s] = before

    ring_step(0)
    pl.semaphore_wait(near_sem, len(near))
    for peer in middle:
        pl.semaphore_signal(far_sem, inc=1, device_id={"facet": peer})
    while work:
        work.pop(0)()
    pl.semaphore_wait(far_sem, len(middle))
    send_back()
    locate()
    for step in range(1, half):
        ring_step(step)
        if step < half - 1:
            own_kernels((step - 1) * subgrids // 2, step * subgrids // 2)
    for copy in back_copy:
        copy.wait()
    for begin in range(0, subgrids, DEGRIDS):
        degrid(begin)
    for piece in range(PIECES):
        value = mine(0, piece)
        for way in range(2):
            step = length(piece, way) - 1
            ring[way, piece, step].wait_recv()
            value = value + recv_buf[(way * PIECES + piece) * half + step].astype(jnp.float32)
        total[pl.ds(piece * depth, depth), :] = value
    for copy in pair_copy.values():
        copy.wait_send()
    for copy in ring.values():
        copy.wait_send()


def output_kernel(rows, total, values, image, residual):
    def place(tile, carry):
        at = pl.ds(pl.multiple_of(tile * LANES, LANES), LANES)
        for part in range(2):
            begin = pl.multiple_of((part * TILES + tile) * rows, rows)
            image[0, :, part, at] = total[pl.ds(begin, rows), :]
        return carry

    lax.fori_loop(0, TILES, place, 0, unroll=4)
    residual[...] = values[...]


VMEM = pl.BlockSpec(memory_space=pltpu.VMEM)
SMEM = pl.BlockSpec(memory_space=pltpu.SMEM)
HBM = pl.BlockSpec(memory_space=pltpu.HBM)


def per_device(
    visibility, uv_coords, vis_count, subgrid_facet, row_offset, col_offset, model_facet
):
    facets, chans = lax.axis_size("facet"), lax.axis_size("chan")
    side = math.isqrt(facets)
    chips = chans // 2
    subgrids = visibility.shape[0]
    rows = F_ROWS // chans
    shape = jax.ShapeDtypeStruct
    left_f, right_f, left_i, right_i = (jnp.asarray(table) for table in dft_tables())
    ids = subgrid_facet[:, 0]

    patches, meta, model_rows, zeros = pl.pallas_call(
        functools.partial(grid_kernel, facets, side, subgrids),
        out_shape=(
            shape((facets * SLOTS * SUB, LANES), jnp.float32),
            shape((facets, 1, LANES), jnp.int32),
            shape((TILES, 2 * F_ROWS, LANES), jnp.float32),
            shape((2, TILES + 1, F_ROWS, LANES), jnp.float32),
        ),
        in_specs=[HBM] * 9,
        out_specs=(VMEM,) * 4,
        scratch_shapes=[
            pltpu.SMEM((subgrids,), jnp.int32),
            pltpu.SMEM((subgrids,), jnp.int32),
            pltpu.SMEM((subgrids,), jnp.int32),
            pltpu.SMEM((subgrids,), jnp.int32),
            pltpu.VMEM(visibility.shape, jnp.float32),
            pltpu.VMEM(uv_coords.shape, jnp.float32),
            pltpu.VMEM(left_f.shape, jnp.bfloat16),
            pltpu.VMEM(right_f.shape, jnp.bfloat16),
            pltpu.VMEM((TILES, F_ROWS, 2, LANES), jnp.bfloat16),
            pltpu.VMEM((facets, 2 * SLOTS, NV), jnp.bfloat16),
            pltpu.VMEM((facets, 2 * SLOTS, NV), jnp.bfloat16),
            pltpu.VMEM((facets, 2 * SLOTS, NV), jnp.float32),
            pltpu.VMEM((facets, 2 * SLOTS, NV), jnp.float32),
            pltpu.VMEM((facets, 1, LANES), jnp.int32),
            pltpu.VMEM((facets * SLOTS, SUB, LANES), jnp.bfloat16),
            pltpu.VMEM((facets * SLOTS, SUB, LANES), jnp.bfloat16),
            pltpu.SMEM((facets,), jnp.int32),
            pltpu.SMEM((facets,), jnp.int32),
            pltpu.SemaphoreType.DMA((8,)),
            pltpu.SemaphoreType.DMA((TILES,)),
            pltpu.SemaphoreType.DMA((3, facets)),
            pltpu.SemaphoreType.DMA((3, facets)),
            pltpu.SemaphoreType.DMA((3,)),
        ],
        compiler_params=pltpu.CompilerParams(
            collective_id=0, has_side_effects=True, vmem_limit_bytes=16 << 20
        ),
        name="grid_and_send",
    )(
        *(
            pltpu.with_memory_space_constraint(array, pltpu.HBM)
            for array in (
                vis_count, ids, row_offset, col_offset, visibility, uv_coords, model_facet,
                left_f, right_f,
            )
        )
    )

    canvas = pl.pallas_call(
        functools.partial(add_kernel, facets),
        out_shape=shape((2, TILES + 1, F_ROWS, LANES), jnp.float32),
        in_specs=[SMEM, VMEM, VMEM],
        out_specs=VMEM,
        input_output_aliases={2: 0},
        compiler_params=pltpu.CompilerParams(vmem_limit_bytes=16 << 20),
        name="add_windows",
    )(meta, patches, zeros)

    depth = 2 * TILES * rows // PIECES
    links = 2 * PIECES * (chips // 2)
    total, residual = pl.pallas_call(
        functools.partial(exchange_kernel, facets, side, chans, subgrids),
        out_shape=(
            shape((2 * TILES * rows, LANES), jnp.float32),
            shape(visibility.shape, jnp.float32),
        ),
        in_specs=[SMEM] * 3 + [VMEM] * 6,
        out_specs=(VMEM,) * 2,
        scratch_shapes=[
            pltpu.VMEM((subgrids, SUB, NV), jnp.bfloat16),
            pltpu.VMEM((subgrids, SUB, NV), jnp.float32),
            pltpu.VMEM((chips, 2 * TILES * rows, LANES), jnp.bfloat16),
            pltpu.VMEM((chips, 2 * TILES * rows, LANES), jnp.bfloat16),
            pltpu.VMEM((links, depth, LANES), jnp.bfloat16),
            pltpu.VMEM((links, depth, LANES), jnp.bfloat16),
            pltpu.VMEM((facets, SLOTS, SUB, LANES), jnp.bfloat16),
            pltpu.VMEM((facets, SLOTS, SUB, LANES), jnp.bfloat16),
            pltpu.SMEM((2 * subgrids,), jnp.int32),
            pltpu.SemaphoreType.DMA((chips * PIECES,)),
            pltpu.SemaphoreType.DMA((chips * PIECES,)),
            pltpu.SemaphoreType.DMA((links,)),
            pltpu.SemaphoreType.DMA((links,)),
            pltpu.SemaphoreType.DMA((facets,)),
            pltpu.SemaphoreType.DMA((facets,)),
            pltpu.SemaphoreType.DMA,
            pltpu.SemaphoreType.REGULAR,
            pltpu.SemaphoreType.REGULAR,
        ],
        compiler_params=pltpu.CompilerParams(
            collective_id=1, has_side_effects=True, vmem_limit_bytes=20 << 20
        ),
        name="reduce_and_return",
    )(meta, vis_count, ids, canvas, model_rows, visibility, uv_coords, left_i, right_i)

    image, residual = pl.pallas_call(
        functools.partial(output_kernel, rows),
        out_shape=(
            shape((1, rows, 2, FACET), jnp.float32),
            shape(visibility.shape, jnp.float32),
        ),
        in_specs=[VMEM] * 2,
        out_specs=(VMEM,) * 2,
        compiler_params=pltpu.CompilerParams(vmem_limit_bytes=8 << 20),
        name="outputs",
    )(total, residual)
    return image, residual


def solution(mesh):
    in_specs = (
        P(("facet", "chan"), None, None),
        P(("facet", "chan"), None, None),
        P(("facet", "chan")),
        P(("facet", "chan"), None),
        P(("facet", "chan")),
        P(("facet", "chan")),
        P("facet", None, None, None),
    )
    out_specs = (P("facet", "chan", None, None), P(("facet", "chan"), None, None))
    return jax.shard_map(
        per_device, mesh=mesh, in_specs=in_specs, out_specs=out_specs, check_vma=False
    )
```

```python
import functools
import itertools
import math

import jax
import jax.numpy as jnp
import numpy as np
from jax import lax
from jax.experimental import pallas as pl
from jax.experimental.pallas import tpu as pltpu
from jax.sharding import PartitionSpec as P

SUB = 64
FACET = 4096
F_ROWS = 128
NV = 512
LANES = 128
TILES = FACET // LANES
SLOTS = 2


def dft_tables():
    line = np.arange(SUB)
    angle = 2.0 * math.pi * (line[:, None] * line[None, :] % SUB) / SUB
    cos_table = (np.cos(angle) / math.sqrt(SUB)).astype(jnp.bfloat16)
    sin_table = (-np.sin(angle) / math.sqrt(SUB)).astype(jnp.bfloat16)
    left_forward = np.concatenate([cos_table, sin_table], 1)
    left_inverse = np.concatenate([cos_table, -sin_table], 1)
    right_forward = np.concatenate(
        [np.concatenate([cos_table, sin_table], 1), np.concatenate([-sin_table, cos_table], 1)], 0
    )
    right_inverse = np.concatenate(
        [np.concatenate([cos_table, -sin_table], 1), np.concatenate([sin_table, cos_table], 1)], 0
    )
    return left_forward, right_forward, left_inverse, right_inverse


ROOT = math.sqrt(math.log2(math.e))


def scaled_square(coords):
    pixels = lax.broadcasted_iota(jnp.int32, (SUB, NV), 0).astype(jnp.float32) * ROOT
    delta = pixels - coords * ROOT
    return delta * delta


def kernel_of(coords):
    return jnp.exp2(-scaled_square(coords))


def kernel_low(coords):
    return kernel_of(coords).astype(jnp.bfloat16)


def live_row(count):
    lane = lax.broadcasted_iota(jnp.int32, (1, NV), 1)
    return (lane < count).astype(jnp.float32)


def facet_order(side):
    steps = [(dx, dy) for dx in range(side) for dy in range(side)]
    return sorted(steps, key=lambda d: (sum(min(n, side - n) for n in d), d))


def facet_steps(me, side):
    x, y = me // side, lax.rem(me, side)
    targets, sources = [], []
    for dx, dy in facet_order(side)[1:]:
        targets.append(lax.rem(x + dx, side) * side + lax.rem(y + dy, side))
        sources.append(lax.rem(x + side - dx, side) * side + lax.rem(y + side - dy, side))
    return targets, sources


def swapped(values):
    half = values.shape[-1] // 2
    return jnp.concatenate([-values[:, half:], values[:, :half]], 1)


def left_pair(table, one, two):
    upper = jnp.concatenate([one, two], 1)
    lower = jnp.concatenate([swapped(one), swapped(two)], 1)
    out = jnp.dot(table, jnp.concatenate([upper, lower], 0), preferred_element_type=jnp.float32)
    return out.astype(jnp.bfloat16)


def gridded(coords, weighted):
    ku = kernel_low(coords[0:1])
    kv = kernel_low(coords[1:2])
    spread = jnp.concatenate([weighted[0:1] * kv, weighted[1:2] * kv], 0)
    return lax.dot_general(
        ku, spread, (((1,), (1,)), ((), ())), preferred_element_type=jnp.float32
    ).astype(jnp.bfloat16)


SIZES = (6, 6, 4)


def grid_kernel(
    facets, side, subgrids,
    cnt_hbm, fid_hbm, row_hbm, col_hbm, vis_hbm, uv_hbm, model, left_hbm, right_hbm,
    patches, meta_in, model_rows, canvas,
    cnt, fid, row, col, vis, uv, left_f, right_f, raw, vis_send, vis_in, uv_send, uv_in, meta_send,
    grids, halves, first, last,
    in_sem, raw_sem, send_sem, recv_sem, own_sem,
):
    me = lax.axis_index("facet")
    targets, _ = facet_steps(me, side)
    barrier = pltpu.get_barrier_semaphore()
    for peer in targets:
        pl.semaphore_signal(barrier, inc=1, device_id={"facet": peer})
    fetches = []
    for i, (src, dst) in enumerate((
        (fid_hbm, fid), (cnt_hbm, cnt), (row_hbm, row), (col_hbm, col), (vis_hbm, vis), (uv_hbm, uv),
        (left_hbm, left_f), (right_hbm, right_f),
    )):
        fetch = pltpu.make_async_copy(src, dst, in_sem.at[i])
        fetch.start()
        fetches.append(fetch)

    def model_copy(tile):
        at = pl.ds(pl.multiple_of(tile * LANES, LANES), LANES)
        return pltpu.make_async_copy(model.at[0, :, :, at], raw.at[tile], raw_sem.at[tile])

    def fetch_model(tile, carry):
        model_copy(tile).start()
        return carry

    lax.fori_loop(0, TILES, fetch_model, 0)
    for fetch in fetches:
        fetch.wait()

    ids = [fid[s] for s in range(subgrids)]

    def find(facet, carry):
        low = jnp.int32(subgrids)
        high = jnp.int32(-1)
        for s in range(subgrids):
            high = jnp.where(ids[s] == facet, s, high)
            back = subgrids - 1 - s
            low = jnp.where(ids[back] == facet, back, low)
        first[facet] = low
        last[facet] = high
        return carry

    lax.fori_loop(0, facets, find, 0)

    lane = lax.broadcasted_iota(jnp.int32, (1, LANES), 1)

    def pack(facet, carry):
        low, high = first[facet], last[facet]
        one = jnp.minimum(low, subgrids - 1)
        two = jnp.maximum(high, 0)
        weighted = [vis[s] * live_row(cnt[s]) for s in (one, two)]
        vis_send[facet] = jnp.concatenate(weighted, 0).astype(jnp.bfloat16)
        uv_send[facet] = jnp.concatenate([uv[one], uv[two]], 0)
        values = (
            (high >= 0).astype(jnp.int32), row[one], col[one],
            (high > low).astype(jnp.int32), row[two], col[two],
        )
        line = jnp.zeros((1, LANES), jnp.int32)
        for place, value in enumerate(values):
            line = jnp.where(lane == place, value, line)
        meta_send[facet] = line
        return carry

    lax.fori_loop(0, facets, pack, 0)

    pl.semaphore_wait(barrier, facets - 1)
    moved = ((meta_send, meta_in), (vis_send, vis_in), (uv_send, uv_in))
    copies = [[] for _ in range(facets)]
    for step in range(facets - 1, -1, -1):
        for i, (src, dst) in enumerate(moved):
            if step > 0:
                copy = pltpu.make_async_remote_copy(
                    src_ref=src.at[targets[step - 1]], dst_ref=dst.at[step],
                    send_sem=send_sem.at[i, step], recv_sem=recv_sem.at[i, step],
                    device_id={"facet": targets[step - 1]},
                )
            else:
                copy = pltpu.make_async_copy(src.at[me], dst.at[0], own_sem.at[i])
            copy.start()
            copies[step].append(copy)

    rows_view = raw.reshape(TILES, 2 * F_ROWS, LANES)

    def widen(tile, carry):
        model_copy(tile).wait()
        model_rows[tile] = rows_view[tile].astype(jnp.float32)
        canvas[0, tile] = zero
        canvas[1, tile] = zero
        return carry

    zero = jnp.zeros((F_ROWS, LANES), jnp.float32)
    lax.fori_loop(0, TILES, widen, 0)
    canvas[0, TILES] = zero
    canvas[1, TILES] = zero

    def grid_one(step):
        for slot in range(SLOTS):
            at = pl.ds(2 * slot, 2)
            grids[SLOTS * step + slot] = gridded(uv_in[step, at, :], vis_in[step, at, :])

    def left_one(step):
        out = left_pair(left_f[...], grids[SLOTS * step], grids[SLOTS * step + 1])
        halves[SLOTS * step] = out[:, :LANES]
        halves[SLOTS * step + 1] = out[:, LANES:]

    def right_one(step):
        both = halves[pl.ds(SLOTS * step, SLOTS)].reshape(SLOTS * SUB, LANES)
        patches[pl.ds(SLOTS * SUB * step, SLOTS * SUB), :] = jnp.dot(
            both, right_f[...], preferred_element_type=jnp.float32
        )

    begins = [0]
    for size in SIZES:
        begins.append(begins[-1] + size)
    groups = [range(a, b) for a, b in zip(begins, begins[1:])]
    stages = (grid_one, left_one, right_one)
    for turn in range(len(groups) + len(stages) - 1):
        if turn < len(groups):
            for step in groups[turn]:
                for copy in copies[step]:
                    copy.wait_recv() if step > 0 else copy.wait()
        now = []
        for lag, stage in enumerate(stages):
            if 0 <= turn - lag < len(groups):
                now.append([functools.partial(stage, step) for step in groups[turn - lag]])
        for parts in itertools.zip_longest(*now):
            for part in reversed(parts):
                if part is not None:
                    part()
    for step in range(1, facets):
        for copy in copies[step]:
            copy.wait_send()


def add_kernel(facets, meta, patches, _, canvas):
    lane = lax.broadcasted_iota(jnp.int32, (SUB, LANES), 1)

    def add(step, carry):
        for slot in range(SLOTS):
            valid = meta[step, 0, 3 * slot] > 0
            top = meta[step, 0, 3 * slot + 1]
            col = meta[step, 0, 3 * slot + 2]
            tile, shift = col // LANES, lax.rem(col, LANES)
            low = jnp.where(valid, shift, LANES)
            high = jnp.where(valid, shift - SUB, 0)
            patch = patches[pl.ds(pl.multiple_of((step * 2 + slot) * SUB, SUB), SUB), :]
            inside = (lane >= low) & (lane < shift + SUB)
            beyond = lane < high
            at = pl.ds(top, SUB)
            spots = [(part, tile + next_tile) for part in range(2) for next_tile in range(2)]
            before = [canvas[part, spot, at, :] for part, spot in spots]
            turned = (
                pltpu.roll(patch, shift, 1),
                pltpu.roll(patch, lax.rem(shift + SUB, LANES), 1),
            )
            for i, (part, spot) in enumerate(spots):
                canvas[part, spot, at, :] = before[i] + jnp.where(
                    beyond if i % 2 else inside, turned[part], 0.0
                )
        return carry

    lax.fori_loop(0, facets, add, 0, unroll=4)


PIECES = 4
PICKS = 2
DEGRIDS = 4


def exchange_kernel(
    facets, side, chans, subgrids,
    meta, cnt, fid, canvas, model_rows, vis, uv, left_i, right_i,
    total, residual,
    own_ku, own_kv, half_buf, pair_buf, send_buf, recv_buf, back, returned, place,
    pair_send, pair_recv, ring_send, ring_recv, back_send, back_recv, own_sem, near_sem, far_sem,
):
    chips = chans // 2
    me_f, me_c = lax.axis_index("facet"), lax.axis_index("chan")
    z, core = me_c // 2, lax.rem(me_c, 2)
    partner = z * 2 + 1 - core
    right = lax.rem(z + 1, chips) * 2 + core
    left = lax.rem(z + chips - 1, chips) * 2 + core
    targets, sources = facet_steps(me_f, side)
    hops = [sum(min(n, side - n) for n in d) for d in facet_order(side)][1:]
    near = [peer for peer, hop in zip(targets, hops) if hop == 1]
    middle = [peer for peer, hop in zip(targets, hops) if hop == 2]
    rows = F_ROWS // chans
    barrier = pltpu.get_barrier_semaphore()
    for peer in (partner, right, left):
        pl.semaphore_signal(barrier, inc=1, device_id={"chan": peer})
    for peer in near:
        pl.semaphore_signal(barrier, inc=1, device_id={"facet": peer})

    lane = lax.broadcasted_iota(jnp.int32, (SUB, LANES), 1)

    def picked(step, slot):
        top = meta[step, 0, 3 * slot + 1]
        col = meta[step, 0, 3 * slot + 2]
        tile, shift = col // LANES, lax.rem(col, LANES)
        after = jnp.minimum(tile + 1, TILES - 1)
        parts = [
            jnp.where(
                lane >= shift,
                model_rows[tile, pl.ds(2 * top + part, SUB, stride=2), :],
                model_rows[after, pl.ds(2 * top + part, SUB, stride=2), :],
            )
            for part in range(2)
        ]
        re = pltpu.roll(parts[0], lax.rem(LANES - shift, LANES), 1)
        im = pltpu.roll(parts[1], lax.rem(LANES + SUB - shift, LANES), 1)
        return jnp.where(lane < SUB, re, im).astype(jnp.bfloat16)

    def pick(begin):
        halves = []
        for step in range(begin, begin + PICKS):
            out = left_pair(left_i[...], picked(step, 0), picked(step, 1))
            halves += [out[:, :LANES], out[:, LANES:]]
        out = jnp.dot(
            jnp.concatenate(halves, 0), right_i[...], preferred_element_type=jnp.float32
        ).astype(jnp.bfloat16)
        for i in range(PICKS):
            for slot in range(SLOTS):
                at = (2 * i + slot) * SUB
                back[begin + i, slot] = out[at : at + SUB]

    half = chips // 2
    depth = half_buf.shape[1] // PIECES

    def length(piece, way):
        return half - (piece + way) % 2

    needed = []
    for step in range(half):
        for piece in range(PIECES):
            for way in range(2):
                distance = length(piece, way) - step
                need = (distance % chips if way == 0 else (chips - distance) % chips, piece)
                if distance > 0 and need not in needed:
                    needed.append(need)
    needed += [(0, piece) for piece in range(PIECES)]

    work = [functools.partial(pick, begin) for begin in range(facets - PICKS, -1, -PICKS)]

    def chan_rows(offset, which):
        there = lax.rem(z + offset, chips)
        return pl.ds(pl.multiple_of((2 * there + which) * rows, rows), rows)

    def narrow(pair, carry):
        for offset in range(chips):
            for part in range(2):
                both = canvas[part, pl.ds(2 * pair, 2), chan_rows(offset, 1 - core), :]
                at = pl.ds(pl.multiple_of((part * TILES + 2 * pair) * rows, 2 * rows), 2 * rows)
                half_buf[offset, at, :] = both.reshape(2 * rows, LANES).astype(jnp.bfloat16)
        return carry

    lax.fori_loop(0, TILES // 2, narrow, 0)
    pl.semaphore_wait(barrier, 3 + len(near))
    for peer in near:
        pl.semaphore_signal(near_sem, inc=1, device_id={"facet": peer})

    pair_copy = {}
    for i, (offset, piece) in enumerate(needed):
        at = pl.ds(piece * depth, depth)
        copy = pltpu.make_async_remote_copy(
            src_ref=half_buf.at[offset, at, :], dst_ref=pair_buf.at[offset, at, :],
            send_sem=pair_send.at[i], recv_sem=pair_recv.at[i], device_id={"chan": partner},
        )
        copy.start()
        pair_copy[offset, piece] = copy

    arrived = set()

    def mine(offset, piece):
        if (offset, piece) not in arrived:
            arrived.add((offset, piece))
            pair_copy[offset, piece].wait_recv()
        at = pl.ds(piece * depth, depth)
        tiles = TILES * 2 // PIECES
        part, begin = divmod(piece * tiles, TILES)
        own = canvas[part, pl.ds(begin, tiles), chan_rows(offset, core), :]
        return own.reshape(depth, LANES) + pair_buf[offset, at, :].astype(jnp.float32)

    ring = {}

    def ring_step(step):
        for piece in range(PIECES):
            for way in range(2):
                count = length(piece, way)
                if step >= count:
                    continue
                distance = count - step
                offset = distance if way == 0 else chips - distance
                value = mine(offset % chips, piece)
                slot = (way * PIECES + piece) * half + step
                if step > 0:
                    ring[way, piece, step - 1].wait_recv()
                    value = value + recv_buf[slot - 1].astype(jnp.float32)
                send_buf[slot] = value.astype(jnp.bfloat16)
                copy = pltpu.make_async_remote_copy(
                    src_ref=send_buf.at[slot], dst_ref=recv_buf.at[slot],
                    send_sem=ring_send.at[slot], recv_sem=ring_recv.at[slot],
                    device_id={"chan": right if way == 0 else left},
                )
                copy.start()
                ring[way, piece, step] = copy

    def own_kernels(begin, end):
        def one(s, carry):
            own_ku[s] = kernel_low(uv[s, pl.ds(0, 1), :])
            own_kv[s] = kernel_of(uv[s, pl.ds(1, 1), :])
            return carry

        lax.fori_loop(begin, end, one, 0, unroll=2)

    def degrid(begin):
        for s in range(begin, begin + DEGRIDS):
            image = returned[place[s], place[subgrids + s]]
            ku, weight = own_ku[s], own_kv[s]
            inner = lax.dot_general(
                image, ku, (((0,), (0,)), ((), ())), preferred_element_type=jnp.float32
            )
            live = live_row(cnt[s])
            for part in range(2):
                predicted = jnp.sum(inner[part * SUB : (part + 1) * SUB] * weight, 0, keepdims=True)
                residual[s, pl.ds(part, 1), :] = (vis[s, pl.ds(part, 1), :] - predicted) * live

    back_copy = []

    def send_back():
        for step in range(facets - 1, 0, -1):
            copy = pltpu.make_async_remote_copy(
                src_ref=back.at[step], dst_ref=returned.at[step],
                send_sem=back_send.at[step], recv_sem=back_recv.at[step],
                device_id={"facet": sources[step - 1]},
            )
            copy.start()
            back_copy.append(copy)
        own = pltpu.make_async_copy(back.at[0], returned.at[0], own_sem)
        own.start()
        back_copy.append(own)

    def locate():
        ids = [fid[s] for s in range(subgrids)]
        x, y = me_f // side, lax.rem(me_f, side)
        codes = []
        for s in range(subgrids):
            before = jnp.int32(0)
            for other in range(s):
                before = jnp.where(ids[other] == ids[s], 1, before)
            there_x, there_y = ids[s] // side, lax.rem(ids[s], side)
            code = lax.rem(there_x + side - x, side) * side + lax.rem(there_y + side - y, side)
            where = jnp.int32(0)
            for step, known in enumerate(facet_order(side)):
                where = jnp.where(code == known[0] * side + known[1], step, where)
            place[s] = where
            place[subgrids + s] = before

    ring_step(0)
    pl.semaphore_wait(near_sem, len(near))
    for peer in middle:
        pl.semaphore_signal(far_sem, inc=1, device_id={"facet": peer})
    while work:
        work.pop(0)()
    pl.semaphore_wait(far_sem, len(middle))
    send_back()
    locate()
    for step in range(1, half):
        ring_step(step)
        if step < half - 1:
            own_kernels((step - 1) * subgrids // 2, step * subgrids // 2)
    for copy in back_copy:
        copy.wait()
    for begin in range(0, subgrids, DEGRIDS):
        degrid(begin)
    for piece in range(PIECES):
        value = mine(0, piece)
        for way in range(2):
            step = length(piece, way) - 1
            ring[way, piece, step].wait_recv()
            value = value + recv_buf[(way * PIECES + piece) * half + step].astype(jnp.float32)
        total[pl.ds(piece * depth, depth), :] = value
    for copy in pair_copy.values():
        copy.wait_send()
    for copy in ring.values():
        copy.wait_send()


def output_kernel(rows, total, values, image, residual, held, sem):
    copies = [pltpu.make_async_copy(values, residual, sem.at[0])]
    copies[0].start()
    span = TILES // 4

    def place(tile, carry):
        at = pl.ds(pl.multiple_of(tile * LANES, LANES), LANES)
        for part in range(2):
            begin = pl.multiple_of((part * TILES + tile) * rows, rows)
            held[0, :, part, at] = total[pl.ds(begin, rows), :]
        return carry

    for chunk in range(4):
        lax.fori_loop(chunk * span, (chunk + 1) * span, place, 0, unroll=4)
        at = pl.ds(chunk * span * LANES, span * LANES)
        copy = pltpu.make_async_copy(held.at[:, :, :, at], image.at[:, :, :, at], sem.at[chunk + 1])
        copy.start()
        copies.append(copy)
    for copy in copies:
        copy.wait()


VMEM = pl.BlockSpec(memory_space=pltpu.VMEM)
SMEM = pl.BlockSpec(memory_space=pltpu.SMEM)
HBM = pl.BlockSpec(memory_space=pltpu.HBM)


def per_device(
    visibility, uv_coords, vis_count, subgrid_facet, row_offset, col_offset, model_facet
):
    facets, chans = lax.axis_size("facet"), lax.axis_size("chan")
    side = math.isqrt(facets)
    chips = chans // 2
    subgrids = visibility.shape[0]
    rows = F_ROWS // chans
    shape = jax.ShapeDtypeStruct
    left_f, right_f, left_i, right_i = (jnp.asarray(table) for table in dft_tables())
    ids = subgrid_facet[:, 0]

    patches, meta, model_rows, zeros = pl.pallas_call(
        functools.partial(grid_kernel, facets, side, subgrids),
        out_shape=(
            shape((facets * SLOTS * SUB, LANES), jnp.float32),
            shape((facets, 1, LANES), jnp.int32),
            shape((TILES, 2 * F_ROWS, LANES), jnp.float32),
            shape((2, TILES + 1, F_ROWS, LANES), jnp.float32),
        ),
        in_specs=[HBM] * 9,
        out_specs=(VMEM,) * 4,
        scratch_shapes=[
            pltpu.SMEM((subgrids,), jnp.int32),
            pltpu.SMEM((subgrids,), jnp.int32),
            pltpu.SMEM((subgrids,), jnp.int32),
            pltpu.SMEM((subgrids,), jnp.int32),
            pltpu.VMEM(visibility.shape, jnp.float32),
            pltpu.VMEM(uv_coords.shape, jnp.float32),
            pltpu.VMEM(left_f.shape, jnp.bfloat16),
            pltpu.VMEM(right_f.shape, jnp.bfloat16),
            pltpu.VMEM((TILES, F_ROWS, 2, LANES), jnp.bfloat16),
            pltpu.VMEM((facets, 2 * SLOTS, NV), jnp.bfloat16),
            pltpu.VMEM((facets, 2 * SLOTS, NV), jnp.bfloat16),
            pltpu.VMEM((facets, 2 * SLOTS, NV), jnp.float32),
            pltpu.VMEM((facets, 2 * SLOTS, NV), jnp.float32),
            pltpu.VMEM((facets, 1, LANES), jnp.int32),
            pltpu.VMEM((facets * SLOTS, SUB, LANES), jnp.bfloat16),
            pltpu.VMEM((facets * SLOTS, SUB, LANES), jnp.bfloat16),
            pltpu.SMEM((facets,), jnp.int32),
            pltpu.SMEM((facets,), jnp.int32),
            pltpu.SemaphoreType.DMA((8,)),
            pltpu.SemaphoreType.DMA((TILES,)),
            pltpu.SemaphoreType.DMA((3, facets)),
            pltpu.SemaphoreType.DMA((3, facets)),
            pltpu.SemaphoreType.DMA((3,)),
        ],
        compiler_params=pltpu.CompilerParams(
            collective_id=0, has_side_effects=True, vmem_limit_bytes=16 << 20
        ),
        name="grid_and_send",
    )(
        *(
            pltpu.with_memory_space_constraint(array, pltpu.HBM)
            for array in (
                vis_count, ids, row_offset, col_offset, visibility, uv_coords, model_facet,
                left_f, right_f,
            )
        )
    )

    canvas = pl.pallas_call(
        functools.partial(add_kernel, facets),
        out_shape=shape((2, TILES + 1, F_ROWS, LANES), jnp.float32),
        in_specs=[SMEM, VMEM, VMEM],
        out_specs=VMEM,
        input_output_aliases={2: 0},
        compiler_params=pltpu.CompilerParams(vmem_limit_bytes=16 << 20),
        name="add_windows",
    )(meta, patches, zeros)

    depth = 2 * TILES * rows // PIECES
    links = 2 * PIECES * (chips // 2)
    total, residual = pl.pallas_call(
        functools.partial(exchange_kernel, facets, side, chans, subgrids),
        out_shape=(
            shape((2 * TILES * rows, LANES), jnp.float32),
            shape(visibility.shape, jnp.float32),
        ),
        in_specs=[SMEM] * 3 + [VMEM] * 6,
        out_specs=(VMEM,) * 2,
        scratch_shapes=[
            pltpu.VMEM((subgrids, SUB, NV), jnp.bfloat16),
            pltpu.VMEM((subgrids, SUB, NV), jnp.float32),
            pltpu.VMEM((chips, 2 * TILES * rows, LANES), jnp.bfloat16),
            pltpu.VMEM((chips, 2 * TILES * rows, LANES), jnp.bfloat16),
            pltpu.VMEM((links, depth, LANES), jnp.bfloat16),
            pltpu.VMEM((links, depth, LANES), jnp.bfloat16),
            pltpu.VMEM((facets, SLOTS, SUB, LANES), jnp.bfloat16),
            pltpu.VMEM((facets, SLOTS, SUB, LANES), jnp.bfloat16),
            pltpu.SMEM((2 * subgrids,), jnp.int32),
            pltpu.SemaphoreType.DMA((chips * PIECES,)),
            pltpu.SemaphoreType.DMA((chips * PIECES,)),
            pltpu.SemaphoreType.DMA((links,)),
            pltpu.SemaphoreType.DMA((links,)),
            pltpu.SemaphoreType.DMA((facets,)),
            pltpu.SemaphoreType.DMA((facets,)),
            pltpu.SemaphoreType.DMA,
            pltpu.SemaphoreType.REGULAR,
            pltpu.SemaphoreType.REGULAR,
        ],
        compiler_params=pltpu.CompilerParams(
            collective_id=1, has_side_effects=True, vmem_limit_bytes=20 << 20
        ),
        name="reduce_and_return",
    )(meta, vis_count, ids, canvas, model_rows, visibility, uv_coords, left_i, right_i)

    image, residual = pl.pallas_call(
        functools.partial(output_kernel, rows),
        out_shape=(
            shape((1, rows, 2, FACET), jnp.float32),
            shape(visibility.shape, jnp.float32),
        ),
        in_specs=[VMEM] * 2,
        out_specs=(HBM,) * 2,
        scratch_shapes=[
            pltpu.VMEM((1, rows, 2, FACET), jnp.float32),
            pltpu.SemaphoreType.DMA((5,)),
        ],
        compiler_params=pltpu.CompilerParams(vmem_limit_bytes=8 << 20),
        name="outputs",
    )(total, residual)
    return image, residual


def solution(mesh):
    in_specs = (
        P(("facet", "chan"), None, None),
        P(("facet", "chan"), None, None),
        P(("facet", "chan")),
        P(("facet", "chan"), None),
        P(("facet", "chan")),
        P(("facet", "chan")),
        P("facet", None, None, None),
    )
    out_specs = (P("facet", "chan", None, None), P(("facet", "chan"), None, None))
    return jax.shard_map(
        per_device, mesh=mesh, in_specs=in_specs, out_specs=out_specs, check_vma=False
    )
```
